256 devices in a mesh: frame: 32 (over z_lo, x, core), tile: 8 (over y, z_hi).
Axes of the slice: x: 4, y: 4, z: 8 (z_hi: 2, z_lo: 4; z = z_hi * 4 + z_lo), core: 2. Of those that a mesh axis runs over, the one named last changes fastest.
Arguments:
- queries: bfloat16 [32, 8, 64, 5120], P('frame', 'tile'), may hold values from -6 to 6
- keys: bfloat16 [32, 8, 64, 5120], P('frame', 'tile'), may hold values from -6 to 6
- values: bfloat16 [32, 8, 64, 5120], P('frame', 'tile'), may hold values from -6 to 6
- step_index: int32 [32], P('frame'), may hold values from 0 to 3
- frame_index: int32 [32], P('frame'), may hold values from 0 to 9
- window_mask: int32 [40, 9], replicated, may hold values 0 or 1
- history_mask: int32 [32, 5], P('frame'), may hold values 0 or 1
- step_gain: float32 [4, 40], replicated, may hold values from 0.5 to 2
Outputs:
- output: bfloat16 [32, 8, 64, 5120], P('frame', 'tile')
The draws below stay inside these ranges and needn't reach their ends.
All inputs are finite; a program needn't handle non-finite values. No bound on the sum of `history_mask` on one device may be relied on, other than what follows from the above.
Results may differ from the reference program's by a relative error of at most 0.0095.
Values may be sent and summed in bfloat16 or wider, within the bound.
A program may use at most 128 MiB of HBM per device.

```python
import math
import jax
import jax.numpy as jnp
from jax import lax

HEADS = 40
HD = 128
TH = 8
TW = 8
BLK = 4
WIN = 5
STEPS = 4
FRAMES = 32
TILES = 8
FRAME_TOK = 512
C = 5120


def shared_draw(key):
    shape = (FRAMES, TILES, TH * TW, C)
    query_base = jax.random.truncated_normal(jax.random.fold_in(key, 11), -6.0, 6.0, shape, jnp.float32)
    key_base = jax.random.truncated_normal(jax.random.fold_in(key, 12), -6.0, 6.0, shape, jnp.float32)
    return (query_base, key_base)


def draw_queries(key, part):
    return shared_draw(key)[0].astype(jnp.bfloat16)


def draw_keys(key, part):
    return shared_draw(key)[1].astype(jnp.bfloat16)


def plant(drawn, stream_key, low, top_value):
    place = [jax.random.randint(jax.random.fold_in(stream_key, axis), (), 0, length) for axis, length in enumerate(drawn.shape)]
    main_axis = drawn.shape.index(max(drawn.shape))
    next_to = place[:main_axis] + [(place[main_axis] + 1) % drawn.shape[main_axis]] + place[main_axis + 1:]
    return drawn.at[tuple(place)].set(low).at[tuple(next_to)].set(top_value)


def shard_levels(stream_key, shape, shards, smallest, top_value):
    gain = 1.0
    for dim, blocks in shards:
        steps = jax.random.uniform(jax.random.fold_in(jax.random.fold_in(stream_key, 6), dim), (blocks,), jnp.float32, smallest / len(shards), top_value / len(shards))
        gain = gain * jnp.repeat(jnp.exp(steps), shape[dim] // blocks).reshape((-1,) + (1,) * (len(shape) - 1 - dim))
    return gain


def scatter_about(key, extent, width, most, split=(), kind=jnp.bfloat16):
    values = jax.random.normal(key, extent, jnp.float32) * width
    if len(split) > 0:
        values = shard_levels(key, extent, split, -0.22, 0.18) * values
    return jnp.clip(values, min=-most, max=most).astype(kind)


def setup_inputs(seed: int = 0) -> dict:
    arg_keys = jax.random.split(jax.random.key(seed), 9)
    queries = draw_queries(jax.random.fold_in(arg_keys[8], 71), 0)
    keys = draw_keys(jax.random.fold_in(arg_keys[8], 71), 0)
    values = scatter_about(arg_keys[2], (FRAMES, TILES, TH * TW, C), 1.0, 6.0, ((0, 32), (1, 8)))
    step_index = plant(jax.random.randint(arg_keys[3], (FRAMES,), 0, STEPS), jax.random.fold_in(arg_keys[3], 1), 0, STEPS - 1).astype(jnp.int32)
    frame_index = plant(jax.random.randint(arg_keys[4], (FRAMES,), 0, 2 * WIN), jax.random.fold_in(arg_keys[4], 1), 0, (2 * WIN) - 1).astype(jnp.int32)
    window_mask = plant((jax.random.randint(arg_keys[5], (HEADS, 9), 0, 2) < 1).astype(jnp.int32), jax.random.fold_in(arg_keys[5], 1), 0, 1)
    history_mask = plant((jax.random.randint(arg_keys[6], (FRAMES, WIN), 0, 4) < 3).astype(jnp.int32), jax.random.fold_in(arg_keys[6], 1), 0, 1)
    step_gain = jnp.clip(jnp.exp(jax.random.uniform(arg_keys[7], (STEPS, HEADS), jnp.float32, math.log(0.5), math.log(2.0))), 0.5, 2.0)
    return {"queries": queries, "keys": keys, "values": values, "step_index": step_index, "frame_index": frame_index, "window_mask": window_mask, "history_mask": history_mask, "step_gain": step_gain}


def token_place(positions, tile_cols):
    tile_of = positions // (TH * TW)
    within = positions % (TH * TW)
    grid_row = tile_of // tile_cols * TH + within // TW
    grid_col = tile_of % tile_cols * TW + within % TW
    return (grid_row, grid_col)

def offset_code(query_row, query_col, key_row, key_col):
    row_step = key_row // BLK - query_row // BLK
    across = key_col // BLK - query_col // BLK
    nearby = (jnp.abs(row_step) <= 1) & (jnp.abs(across) <= 1)
    return jnp.where(nearby, (row_step + 1) * 3 + across + 1, -1).astype(jnp.int32)

def window_allow(offset_ids, mask_rows):
    allowed = (offset_ids == 4)[None]
    for offset in range(9):
        allowed = allowed | (offset_ids == offset)[None] & (mask_rows[:, offset] == 1)[:, None, None]
    return allowed

def reference(queries, keys, values, step_index, frame_index, window_mask, history_mask, step_gain):
    tile_cols = min(TILES, 4)
    scale_factor = 1.0 / math.sqrt(HD)
    positions = jnp.arange(FRAME_TOK, dtype=jnp.int32)
    grid_row, grid_col = token_place(positions, tile_cols)
    offset_ids = offset_code(grid_row[:, None], grid_col[:, None], grid_row[None, :], grid_col[None, :])
    flat_q = queries.reshape(FRAMES, FRAME_TOK, HEADS, HD)
    flat_k = keys.reshape(FRAMES, FRAME_TOK, HEADS, HD)
    flat_v = values.reshape(FRAMES, FRAME_TOK, HEADS, HD)
    distance = jnp.arange(1, WIN + 1, dtype=jnp.int32)

    def one_group(group_id):
        source = group_id - distance
        usable = (history_mask[group_id] == 1) & (distance <= frame_index[group_id]) & (source >= 0)
        source = jnp.maximum(source, 0).astype(jnp.int32)
        past_k = flat_k[source]
        past_v = flat_v[source]
        head_gains = step_gain[step_index[group_id]]

        def one_head(head_id):
            query_h = flat_q[group_id, :, head_id].astype(jnp.float32)
            own_k = flat_k[group_id, :, head_id].astype(jnp.float32)
            allowed = window_allow(offset_ids, window_mask[head_id][None, :])[0]
            own_s = jnp.dot(query_h, own_k.T, precision=lax.Precision.HIGHEST) * scale_factor
            own_s = jnp.where(allowed, own_s, -jnp.inf)
            past_s = jnp.einsum('qd,wkd->qwk', query_h, past_k[:, :, head_id].astype(jnp.float32), precision=lax.Precision.HIGHEST) * scale_factor
            past_s = jnp.where(usable[None, :, None], past_s, -jnp.inf).reshape(FRAME_TOK, WIN * FRAME_TOK)
            scores = jnp.concatenate([own_s, past_s], axis=1)
            row_max = lax.optimization_barrier(jnp.max(scores, axis=1, keepdims=True))
            weights = jnp.exp(scores - row_max)
            denominator = lax.optimization_barrier(jnp.sum(weights, axis=1, keepdims=True))
            all_values = jnp.concatenate([flat_v[group_id, :, head_id][None], past_v[:, :, head_id]], axis=0)
            all_values = all_values.reshape((WIN + 1) * FRAME_TOK, HD)
            blended = jnp.dot(weights.astype(jnp.bfloat16), all_values, preferred_element_type=jnp.float32)
            return blended / denominator * head_gains[head_id]
        per_head = lax.map(one_head, jnp.arange(HEADS, dtype=jnp.int32))
        return jnp.transpose(per_head, (1, 0, 2)).reshape(FRAME_TOK, C).astype(jnp.bfloat16)
    result = lax.map(one_group, jnp.arange(FRAMES, dtype=jnp.int32))
    return result.reshape(FRAMES, TILES, TH * TW, C)
```

```python
import math

import jax
import jax.numpy as jnp
from jax import lax
from jax.sharding import PartitionSpec as P

HEADS = 40
HD = 128
TH = 8
TW = 8
BLK = 4
WIN = 5
STEPS = 4


NEG_BIG = -1e30


def next_frame(block):
    count = lax.axis_size("frame")
    return lax.ppermute(block, "frame", [(i, i + 1) for i in range(count - 1)])


def window_allowed(tile_count, tile_tok, head_masks):
    tile_cols = min(tile_count, 4)
    positions = jnp.arange(tile_count * tile_tok, dtype=jnp.int32)
    tile_of = positions // tile_tok
    within = positions % tile_tok
    row = tile_of // tile_cols * TH + within // TW
    col = tile_of % tile_cols * TW + within % TW
    row_step = row[None, :] // BLK - row[:, None] // BLK
    across = col[None, :] // BLK - col[:, None] // BLK
    nearby = (jnp.abs(row_step) <= 1) & (jnp.abs(across) <= 1)
    code = jnp.where(nearby, (row_step + 1) * 3 + across + 1, -1)
    allowed = (code == 4)[None]
    for offset in range(9):
        allowed = allowed | ((code == offset)[None] & (head_masks[:, offset] == 1)[:, None, None])
    return allowed


def blend(carry_state, query_blk, key_blk, value_blk, allowed):
    running_max, normaliser, summed = carry_state
    scale_factor = 1.0 / math.sqrt(HD)
    scores = (
        jnp.einsum("qhd,khd->hqk", query_blk, key_blk, preferred_element_type=jnp.float32)
        * scale_factor
    )
    scores = jnp.where(allowed, scores, NEG_BIG)
    new_max = jnp.maximum(running_max, jnp.max(scores, axis=2))
    weights = jnp.where(allowed, jnp.exp(scores - new_max[:, :, None]), 0.0)
    factor = jnp.exp(running_max - new_max)
    normaliser = normaliser * factor + jnp.sum(weights, axis=2)
    summed = summed * factor[:, :, None] + jnp.einsum(
        "hqk,khd->hqd", weights.astype(jnp.bfloat16), value_blk, preferred_element_type=jnp.float32
    )
    return (new_max, normaliser, summed)


def shards(queries, keys, values, step_index, frame_index, window_mask, history_mask, step_gain):
    tile_count = lax.axis_size("tile")
    tile_id = lax.axis_index("tile")
    group_id = lax.axis_index("frame")
    channels = queries.shape[-1]
    head_share = HEADS // tile_count
    tile_tok = queries.shape[2]
    frame_tok = tile_tok * tile_count
    picker = (jnp.arange(STEPS, dtype=jnp.int32) == step_index[0]).astype(jnp.float32)
    head_gains = jnp.dot(picker, step_gain, precision=lax.Precision.HIGHEST)
    my_gains = lax.dynamic_slice_in_dim(head_gains, tile_id * head_share, head_share)
    my_masks = lax.dynamic_slice_in_dim(window_mask, tile_id * head_share, head_share, axis=0)
    kv = lax.all_to_all(
        jnp.stack([keys[0, 0], values[0, 0]]), "tile", split_axis=2, concat_axis=1, tiled=True
    )
    q = lax.all_to_all(queries[0, 0], "tile", split_axis=1, concat_axis=0, tiled=True)
    q = q.reshape(frame_tok, head_share, HD)
    kv = kv.reshape(2, frame_tok, head_share, HD)
    allowed = window_allowed(tile_count, tile_tok, my_masks)
    state = (
        jnp.full((head_share, frame_tok), NEG_BIG, jnp.float32),
        jnp.zeros((head_share, frame_tok), jnp.float32),
        jnp.zeros((head_share, frame_tok, HD), jnp.float32),
    )
    state = blend(state, q, kv[0], kv[1], allowed)
    held = kv
    for distance in range(1, WIN + 1):
        held = next_frame(held)
        usable = (
            (history_mask[0, distance - 1] == 1)
            & (distance <= frame_index[0])
            & (group_id - distance >= 0)
        )
        state = blend(state, q, held[0], held[1], usable)
    _, normaliser, summed = state
    finished = summed / normaliser[:, :, None] * my_gains[:, None, None]
    finished = jnp.transpose(finished.astype(jnp.bfloat16), (1, 0, 2)).reshape(frame_tok, head_share * HD)
    out = lax.all_to_all(finished, "tile", split_axis=0, concat_axis=1, tiled=True)
    return out.reshape(1, 1, tile_tok, channels)


def solution(mesh):
    return jax.shard_map(
        shards,
        mesh=mesh,
        in_specs=(
            P("frame", "tile", None, None),
            P("frame", "tile", None, None),
            P("frame", "tile", None, None),
            P("frame"),
            P("frame"),
            P(),
            P("frame", None),
            P(),
        ),
        out_specs=P("frame", "tile", None, None),
        check_vma=False,
    )
```

```python
import functools
import math

import jax
import jax.numpy as jnp
from jax import lax
from jax.experimental import pallas as pl
from jax.experimental.pallas import tpu as pltpu
from jax.sharding import PartitionSpec as P

HEADS = 40
HD = 128
TH = 8
TW = 8
BLK = 4
WIN = 5
STEPS = 4
CHUNK = 256

NEG_BIG = -1e30
MESH_ID = pl.DeviceIdType.MESH


def window_allowed(tile_count, tile_tok, head_masks, anchor):
    tile_cols = min(tile_count, 4)
    positions = jnp.arange(tile_count * tile_tok, dtype=jnp.int32) + anchor
    tile_of = positions // tile_tok
    within = positions % tile_tok
    row = tile_of // tile_cols * TH + within // TW
    col = tile_of % tile_cols * TW + within % TW
    row_step = row[None, :] // BLK - row[:, None] // BLK
    across = col[None, :] // BLK - col[:, None] // BLK
    nearby = (jnp.abs(row_step) <= 1) & (jnp.abs(across) <= 1)
    code = jnp.where(nearby, (row_step + 1) * 3 + across + 1, -1)
    allowed = (code == 4)[None]
    for offset in range(9):
        allowed = allowed | ((code == offset)[None] & (head_masks[:, offset] == 1)[:, None, None])
    return allowed


def relay_kernel(frames, use_ref, gain_ref, q_ref, kv_ref, mask_ref, out_ref,
                 slots, m_scr, l_scr, acc_scr, send_sem, recv_sem):
    me = lax.axis_index("frame")
    tile = lax.axis_index("tile")
    right = lax.rem(me + 1, frames)
    left = lax.rem(me + frames - 1, frames)
    head_share = acc_scr.shape[0]
    frame_tok = q_ref.shape[0]
    scale = 1.0 / math.sqrt(HD)

    barrier = pltpu.get_barrier_semaphore()
    for other in (left, right):
        pl.semaphore_signal(barrier, inc=1, device_id=(other, tile), device_id_type=MESH_ID)
    pl.semaphore_wait(barrier, 2)

    def copy_for(step):
        source = kv_ref if step == 0 else slots.at[step - 1]
        return pltpu.make_async_remote_copy(
            src_ref=source,
            dst_ref=slots.at[step],
            send_sem=send_sem.at[step],
            recv_sem=recv_sem.at[step],
            device_id=(right, tile),
            device_id_type=MESH_ID,
        )

    copies = [copy_for(step) for step in range(WIN)]

    @pl.when(me < frames - 1)
    def _():
        copies[0].start()

    m_scr[...] = jnp.full(m_scr.shape, NEG_BIG, jnp.float32)
    l_scr[...] = jnp.zeros(l_scr.shape, jnp.float32)
    acc_scr[...] = jnp.zeros(acc_scr.shape, jnp.float32)

    def attend(block, use):
        def head_body(h, carry):
            col = pl.multiple_of(h * HD, HD)
            key_h = block[0, :, pl.ds(col, HD)]
            value_h = block[1, :, pl.ds(col, HD)]
            for c in range(frame_tok // CHUNK):
                rows = pl.ds(c * CHUNK, CHUNK)
                query_h = q_ref[rows, pl.ds(col, HD)]
                scores = lax.dot_general(
                    query_h, key_h, (((1,), (1,)), ((), ())),
                    preferred_element_type=jnp.float32,
                ) * scale
                if use is None:
                    allowed = mask_ref[h, rows, :] > 0
                else:
                    allowed = jnp.broadcast_to(use > 0, scores.shape)
                scores = jnp.where(allowed, scores, NEG_BIG)
                old_max = m_scr[h, rows, :]
                new_max = jnp.maximum(old_max, jnp.max(scores, axis=1, keepdims=True))
                weights = jnp.where(allowed, jnp.exp(scores - new_max), 0.0)
                factor = jnp.exp(old_max - new_max)
                l_scr[h, rows, :] = l_scr[h, rows, :] * factor + jnp.sum(weights, axis=1, keepdims=True)
                acc_scr[h, rows, :] = acc_scr[h, rows, :] * factor + jnp.dot(
                    weights.astype(jnp.bfloat16), value_h, preferred_element_type=jnp.float32
                )
                m_scr[h, rows, :] = new_max
            return carry

        lax.fori_loop(0, head_share, head_body, 0)

    attend(kv_ref, None)
    for step in range(1, WIN + 1):
        @pl.when(me >= step)
        def _():
            copies[step - 1].wait_recv()
            if step < WIN:
                @pl.when(me < frames - 1)
                def _():
                    copies[step].start()
            attend(slots.at[step - 1], use_ref[step - 1])

    for step in range(WIN):
        @pl.when((me < frames - 1) & (me >= step))
        def _():
            copies[step].wait_send()

    def finish(h, carry):
        col = pl.multiple_of(h * HD, HD)
        out_ref[:, pl.ds(col, HD)] = (
            acc_scr[h] / l_scr[h] * gain_ref[h]
        ).astype(out_ref.dtype)
        return carry

    lax.fori_loop(0, head_share, finish, 0)


def relay_attend(frames, use, gains, q, kv, mask):
    head_share = gains.shape[0]
    frame_tok = q.shape[0]
    flops = 4 * (WIN + 1) * frame_tok * frame_tok * q.shape[1]
    smem = pl.BlockSpec(memory_space=pltpu.SMEM)
    vmem = pl.BlockSpec(memory_space=pltpu.VMEM)
    return pl.pallas_call(
        functools.partial(relay_kernel, frames),
        out_shape=jax.ShapeDtypeStruct(q.shape, jnp.bfloat16),
        in_specs=[smem, smem, vmem, vmem, vmem],
        out_specs=vmem,
        scratch_shapes=[
            pltpu.VMEM((WIN,) + kv.shape, kv.dtype),
            pltpu.VMEM((head_share, frame_tok, 1), jnp.float32),
            pltpu.VMEM((head_share, frame_tok, 1), jnp.float32),
            pltpu.VMEM((head_share, frame_tok, HD), jnp.float32),
            pltpu.SemaphoreType.DMA((WIN,)),
            pltpu.SemaphoreType.DMA((WIN,)),
        ],
        compiler_params=pltpu.CompilerParams(
            collective_id=0, has_side_effects=True, vmem_limit_bytes=48 * 1024 * 1024
        ),
        cost_estimate=pl.CostEstimate(
            flops=flops,
            transcendentals=(WIN + 1) * head_share * frame_tok * frame_tok,
            bytes_accessed=(WIN + 2) * kv.size * 2,
        ),
    )(use, gains, q, kv, mask)


def shards(queries, keys, values, step_index, frame_index, window_mask, history_mask, step_gain):
    tile_count = lax.axis_size("tile")
    frames = lax.axis_size("frame")
    tile_id = lax.axis_index("tile")
    group_id = lax.axis_index("frame")
    channels = queries.shape[-1]
    head_share = HEADS // tile_count
    tile_tok = queries.shape[2]
    frame_tok = tile_tok * tile_count
    picker = (jnp.arange(STEPS, dtype=jnp.int32) == step_index[0]).astype(jnp.float32)
    head_gains = jnp.dot(picker, step_gain, precision=lax.Precision.HIGHEST)
    my_gains = lax.dynamic_slice_in_dim(head_gains, tile_id * head_share, head_share)
    my_masks = lax.dynamic_slice_in_dim(window_mask, tile_id * head_share, head_share, axis=0)
    distance = jnp.arange(1, WIN + 1, dtype=jnp.int32)
    use = (
        (history_mask[0] == 1) & (distance <= frame_index[0]) & (group_id - distance >= 0)
    ).astype(jnp.int32)
    kv = lax.all_to_all(
        jnp.stack([keys[0, 0], values[0, 0]]), "tile", split_axis=2, concat_axis=1, tiled=True
    )
    q = lax.all_to_all(queries[0, 0], "tile", split_axis=1, concat_axis=0, tiled=True)
    anchor = jnp.minimum(step_index[0], 0) * 0
    mask = window_allowed(tile_count, tile_tok, my_masks, anchor).astype(jnp.bfloat16)
    finished = relay_attend(frames, use, my_gains, q, kv, mask)
    out = lax.all_to_all(finished, "tile", split_axis=0, concat_axis=1, tiled=True)
    return out.reshape(1, 1, tile_tok, channels)


def solution(mesh):
    return jax.shard_map(
        shards,
        mesh=mesh,
        in_specs=(
            P("frame", "tile", None, None),
            P("frame", "tile", None, None),
            P("frame", "tile", None, None),
            P("frame"),
            P("frame"),
            P(),
            P("frame", None),
            P(),
        ),
        out_specs=P("frame", "tile", None, None),
        check_vma=False,
    )
```

```python
import functools
import math

import jax
import jax.numpy as jnp
from jax import lax
from jax.experimental import pallas as pl
from jax.experimental.pallas import tpu as pltpu
from jax.sharding import PartitionSpec as P

HEADS = 40
HD = 128
TH = 8
TW = 8
BLK = 4
WIN = 5
STEPS = 4
CHUNK = 256

NEG_BIG = -1e30
MESH_ID = pl.DeviceIdType.MESH


def window_allowed(tile_count, tile_tok, head_masks, anchor):
    tile_cols = min(tile_count, 4)
    positions = jnp.arange(tile_count * tile_tok, dtype=jnp.int32) + anchor
    tile_of = positions // tile_tok
    within = positions % tile_tok
    row = tile_of // tile_cols * TH + within // TW
    col = tile_of % tile_cols * TW + within % TW
    row_step = row[None, :] // BLK - row[:, None] // BLK
    across = col[None, :] // BLK - col[:, None] // BLK
    nearby = (jnp.abs(row_step) <= 1) & (jnp.abs(across) <= 1)
    code = jnp.where(nearby, (row_step + 1) * 3 + across + 1, -1)
    allowed = (code == 4)[None]
    for offset in range(9):
        allowed = allowed | ((code == offset)[None] & (head_masks[:, offset] == 1)[:, None, None])
    return allowed


def fused_kernel(frames, tiles, use_ref, gain_ref, q_ref, k_ref, v_ref, mask_ref, out_ref,
                 own_kv, own_q, slots, fin, got_out, m_scr, l_scr, acc_scr,
                 piece_send, piece_recv, local_sem, send_sem, recv_sem):
    me = lax.axis_index("frame")
    tile = lax.axis_index("tile")
    right = lax.rem(me + 1, frames)
    left = lax.rem(me + frames - 1, frames)
    head_share = acc_scr.shape[0]
    frame_tok = own_q.shape[0]
    share = own_q.shape[1]
    tile_tok = q_ref.shape[0]
    scale = 1.0 / math.sqrt(HD)

    barrier = pltpu.get_barrier_semaphore()
    for other in (left, right):
        pl.semaphore_signal(barrier, inc=1, device_id=(other, tile), device_id_type=MESH_ID)
    for offset in range(1, tiles):
        peer = lax.rem(tile + offset, tiles)
        pl.semaphore_signal(barrier, inc=1, device_id=(me, peer), device_id_type=MESH_ID)
    pl.semaphore_wait(barrier, 2 + tiles - 1)

    def channels_of(p):
        return pl.ds(pl.multiple_of(p * share, 128), share)

    def tokens_of(p):
        return pl.ds(pl.multiple_of(p * tile_tok, tile_tok), tile_tok)

    sources = [k_ref, v_ref, q_ref]
    targets = [lambda rows: own_kv.at[0, rows, :], lambda rows: own_kv.at[1, rows, :],
               lambda rows: own_q.at[rows, :]]

    def piece_out(which, offset):
        peer = lax.rem(tile + offset, tiles)
        return pltpu.make_async_remote_copy(
            src_ref=sources[which].at[:, channels_of(peer)],
            dst_ref=targets[which](tokens_of(tile)),
            send_sem=piece_send.at[which, offset],
            recv_sem=piece_recv.at[which, tile],
            device_id=(me, peer),
            device_id_type=MESH_ID,
        )

    def piece_in(which, offset):
        sender = lax.rem(tile + tiles - offset, tiles)
        return pltpu.make_async_remote_copy(
            src_ref=sources[which].at[:, channels_of(tile)],
            dst_ref=targets[which](tokens_of(sender)),
            send_sem=piece_send.at[which, offset],
            recv_sem=piece_recv.at[which, sender],
            device_id=(me, sender),
            device_id_type=MESH_ID,
        )

    locals_ = [
        pltpu.make_async_copy(
            sources[which].at[:, channels_of(tile)], targets[which](tokens_of(tile)),
            local_sem.at[which],
        )
        for which in range(3)
    ]
    for which in range(3):
        locals_[which].start()
        for offset in range(1, tiles):
            piece_out(which, offset).start()

    for which in range(2):
        locals_[which].wait()
        for offset in range(1, tiles):
            piece_in(which, offset).wait_recv()

    def copy_for(step):
        source = own_kv if step == 0 else slots.at[step - 1]
        return pltpu.make_async_remote_copy(
            src_ref=source,
            dst_ref=slots.at[step],
            send_sem=send_sem.at[step],
            recv_sem=recv_sem.at[step],
            device_id=(right, tile),
            device_id_type=MESH_ID,
        )

    copies = [copy_for(step) for step in range(WIN)]

    @pl.when(me < frames - 1)
    def _():
        copies[0].start()

    m_scr[...] = jnp.full(m_scr.shape, NEG_BIG, jnp.float32)
    l_scr[...] = jnp.zeros(l_scr.shape, jnp.float32)
    acc_scr[...] = jnp.zeros(acc_scr.shape, jnp.float32)

    locals_[2].wait()
    for offset in range(1, tiles):
        piece_in(2, offset).wait_recv()

    def attend(block, use):
        def head_body(h, carry):
            col = pl.multiple_of(h * HD, HD)
            key_h = block[0, :, pl.ds(col, HD)]
            value_h = block[1, :, pl.ds(col, HD)]
            for c in range(frame_tok // CHUNK):
                rows = pl.ds(c * CHUNK, CHUNK)
                query_h = own_q[rows, pl.ds(col, HD)]
                scores = lax.dot_general(
                    query_h, key_h, (((1,), (1,)), ((), ())),
                    preferred_element_type=jnp.float32,
                ) * scale
                if use is None:
                    allowed = mask_ref[h, rows, :] > 0
                else:
                    allowed = jnp.broadcast_to(use > 0, scores.shape)
                scores = jnp.where(allowed, scores, NEG_BIG)
                old_max = m_scr[h, rows, :]
                new_max = jnp.maximum(old_max, jnp.max(scores, axis=1, keepdims=True))
                weights = jnp.where(allowed, jnp.exp(scores - new_max), 0.0)
                factor = jnp.exp(old_max - new_max)
                l_scr[h, rows, :] = l_scr[h, rows, :] * factor + jnp.sum(weights, axis=1, keepdims=True)
                acc_scr[h, rows, :] = acc_scr[h, rows, :] * factor + jnp.dot(
                    weights.astype(jnp.bfloat16), value_h, preferred_element_type=jnp.float32
                )
                m_scr[h, rows, :] = new_max
            return carry

        lax.fori_loop(0, head_share, head_body, 0)

    attend(own_kv, None)
    for step in range(1, WIN + 1):
        @pl.when(me >= step)
        def _():
            copies[step - 1].wait_recv()
            if step < WIN:
                @pl.when(me < frames - 1)
                def _():
                    copies[step].start()
            attend(slots.at[step - 1], use_ref[step - 1])

    def finish(h, carry):
        col = pl.multiple_of(h * HD, HD)
        fin[:, pl.ds(col, HD)] = (acc_scr[h] / l_scr[h] * gain_ref[h]).astype(fin.dtype)
        return carry

    lax.fori_loop(0, head_share, finish, 0)

    def back_out(offset):
        peer = lax.rem(tile + offset, tiles)
        return pltpu.make_async_remote_copy(
            src_ref=fin.at[tokens_of(peer), :],
            dst_ref=got_out.at[:, channels_of(tile)],
            send_sem=piece_send.at[3, offset],
            recv_sem=piece_recv.at[3, tile],
            device_id=(me, peer),
            device_id_type=MESH_ID,
        )

    def back_in(offset):
        sender = lax.rem(tile + tiles - offset, tiles)
        return pltpu.make_async_remote_copy(
            src_ref=fin.at[tokens_of(tile), :],
            dst_ref=got_out.at[:, channels_of(sender)],
            send_sem=piece_send.at[3, offset],
            recv_sem=piece_recv.at[3, sender],
            device_id=(me, sender),
            device_id_type=MESH_ID,
        )

    home = pltpu.make_async_copy(fin.at[tokens_of(tile), :], got_out.at[:, channels_of(tile)],
                                 local_sem.at[3])
    home.start()
    for offset in range(1, tiles):
        back_out(offset).start()
    home.wait()
    for offset in range(1, tiles):
        back_in(offset).wait_recv()
    out_ref[...] = got_out[...]

    for which in range(3):
        for offset in range(1, tiles):
            piece_out(which, offset).wait_send()
    for offset in range(1, tiles):
        back_out(offset).wait_send()
    for step in range(WIN):
        @pl.when((me < frames - 1) & (me >= step))
        def _():
            copies[step].wait_send()


def fused_attend(frames, tiles, use, gains, q, k, v, mask):
    head_share = gains.shape[0]
    tile_tok, channels = q.shape
    frame_tok = tile_tok * tiles
    share = channels // tiles
    flops = 4 * (WIN + 1) * frame_tok * frame_tok * share
    smem = pl.BlockSpec(memory_space=pltpu.SMEM)
    vmem = pl.BlockSpec(memory_space=pltpu.VMEM)
    return pl.pallas_call(
        functools.partial(fused_kernel, frames, tiles),
        out_shape=jax.ShapeDtypeStruct(q.shape, jnp.bfloat16),
        in_specs=[smem, smem, vmem, vmem, vmem, vmem],
        out_specs=vmem,
        scratch_shapes=[
            pltpu.VMEM((2, frame_tok, share), jnp.bfloat16),
            pltpu.VMEM((frame_tok, share), jnp.bfloat16),
            pltpu.VMEM((WIN, 2, frame_tok, share), jnp.bfloat16),
            pltpu.VMEM((frame_tok, share), jnp.bfloat16),
            pltpu.VMEM((tile_tok, channels), jnp.bfloat16),
            pltpu.VMEM((head_share, frame_tok, 1), jnp.float32),
            pltpu.VMEM((head_share, frame_tok, 1), jnp.float32),
            pltpu.VMEM((head_share, frame_tok, HD), jnp.float32),
            pltpu.SemaphoreType.DMA((4, tiles)),
            pltpu.SemaphoreType.DMA((4, tiles)),
            pltpu.SemaphoreType.DMA((4,)),
            pltpu.SemaphoreType.DMA((WIN,)),
            pltpu.SemaphoreType.DMA((WIN,)),
        ],
        compiler_params=pltpu.CompilerParams(
            collective_id=0, has_side_effects=True, vmem_limit_bytes=56 * 1024 * 1024
        ),
        cost_estimate=pl.CostEstimate(
            flops=flops,
            transcendentals=(WIN + 1) * head_share * frame_tok * frame_tok,
            bytes_accessed=(WIN + 6) * 2 * frame_tok * share * 2,
        ),
    )(use, gains, q, k, v, mask)


def shards(queries, keys, values, step_index, frame_index, window_mask, history_mask, step_gain):
    tile_count = lax.axis_size("tile")
    frames = lax.axis_size("frame")
    tile_id = lax.axis_index("tile")
    group_id = lax.axis_index("frame")
    channels = queries.shape[-1]
    head_share = HEADS // tile_count
    tile_tok = queries.shape[2]
    frame_tok = tile_tok * tile_count
    picker = (jnp.arange(STEPS, dtype=jnp.int32) == step_index[0]).astype(jnp.float32)
    head_gains = jnp.dot(picker, step_gain, precision=lax.Precision.HIGHEST)
    my_gains = lax.dynamic_slice_in_dim(head_gains, tile_id * head_share, head_share)
    my_masks = lax.dynamic_slice_in_dim(window_mask, tile_id * head_share, head_share, axis=0)
    distance = jnp.arange(1, WIN + 1, dtype=jnp.int32)
    use = (
        (history_mask[0] == 1) & (distance <= frame_index[0]) & (group_id - distance >= 0)
    ).astype(jnp.int32)
    anchor = jnp.minimum(step_index[0], 0) * 0
    mask = window_allowed(tile_count, tile_tok, my_masks, anchor).astype(jnp.bfloat16)
    finished = fused_attend(
        frames, tile_count, use, my_gains, queries[0, 0], keys[0, 0], values[0, 0], mask
    )
    return finished.reshape(1, 1, tile_tok, channels)


def solution(mesh):
    return jax.shard_map(
        shards,
        mesh=mesh,
        in_specs=(
            P("frame", "tile", None, None),
            P("frame", "tile", None, None),
            P("frame", "tile", None, None),
            P("frame"),
            P("frame"),
            P(),
            P("frame", None),
            P(),
        ),
        out_specs=P("frame", "tile", None, None),
        check_vma=False,
    )
```

```python
import functools
import math

import jax
import jax.numpy as jnp
from jax import lax
from jax.experimental import pallas as pl
from jax.experimental.pallas import tpu as pltpu
from jax.sharding import PartitionSpec as P

HEADS = 40
HD = 128
TH = 8
TW = 8
BLK = 4
WIN = 5
STEPS = 4
CHUNK = 256

NEG_BIG = -1e30
MESH_ID = pl.DeviceIdType.MESH


def block_place(positions, tile_count, tile_tok):
    tile_cols = min(tile_count, 4)
    tile_of = positions // tile_tok
    within = positions % tile_tok
    row = tile_of // tile_cols * TH + within // TW
    col = tile_of % tile_cols * TW + within % TW
    return row // BLK, col // BLK


def fused_kernel(frames, tiles, use_ref, gain_ref, bits_ref, q_ref, k_ref, v_ref, out_ref,
                 own_kv, own_q, slots, fin, got_out, code_scr, m_scr, l_scr, acc_scr,
                 piece_send, piece_recv, local_sem, send_sem, recv_sem, hop_send, hop_recv):
    me = lax.axis_index("frame")
    tile = lax.axis_index("tile")
    right = lax.rem(me + 1, frames)
    left = lax.rem(me + frames - 1, frames)
    head_share = acc_scr.shape[0]
    frame_tok = own_q.shape[0]
    share = own_q.shape[1]
    tile_tok = q_ref.shape[0]
    scale = 1.0 / math.sqrt(HD)

    barrier = pltpu.get_barrier_semaphore()
    for other in (left, right):
        pl.semaphore_signal(barrier, inc=1, device_id=(other, tile), device_id_type=MESH_ID)
    for offset in range(1, tiles):
        peer = lax.rem(tile + offset, tiles)
        pl.semaphore_signal(barrier, inc=1, device_id=(me, peer), device_id_type=MESH_ID)
    pl.semaphore_wait(barrier, 2 + tiles - 1)

    def channels_of(p):
        return pl.ds(pl.multiple_of(p * share, 128), share)

    def tokens_of(p):
        return pl.ds(pl.multiple_of(p * tile_tok, tile_tok), tile_tok)

    sources = [k_ref, v_ref, q_ref]
    targets = [lambda rows: own_kv.at[0, rows, :], lambda rows: own_kv.at[1, rows, :],
               lambda rows: own_q.at[rows, :]]

    def piece_out(which, offset):
        peer = lax.rem(tile + offset, tiles)
        return pltpu.make_async_remote_copy(
            src_ref=sources[which].at[:, channels_of(peer)],
            dst_ref=targets[which](tokens_of(tile)),
            send_sem=piece_send.at[which, offset],
            recv_sem=piece_recv.at[which, tile],
            device_id=(me, peer),
            device_id_type=MESH_ID,
        )

    def piece_in(which, offset):
        sender = lax.rem(tile + tiles - offset, tiles)
        return pltpu.make_async_remote_copy(
            src_ref=sources[which].at[:, channels_of(tile)],
            dst_ref=targets[which](tokens_of(sender)),
            send_sem=piece_send.at[which, offset],
            recv_sem=piece_recv.at[which, sender],
            device_id=(me, sender),
            device_id_type=MESH_ID,
        )

    locals_ = [
        pltpu.make_async_copy(
            sources[which].at[:, channels_of(tile)], targets[which](tokens_of(tile)),
            local_sem.at[which],
        )
        for which in range(3)
    ]
    far_first = [j for j in range(1, tiles) if j % 2] + [j for j in range(1, tiles) if j % 2 == 0]
    near_first = far_first[::-1]
    for which in range(3):
        locals_[which].start()
        for offset in far_first:
            piece_out(which, offset).start()

    for c in range(frame_tok // CHUNK):
        query_pos = c * CHUNK + lax.broadcasted_iota(jnp.int32, (CHUNK, frame_tok), 0)
        key_pos = lax.broadcasted_iota(jnp.int32, (CHUNK, frame_tok), 1)
        query_row, query_col = block_place(query_pos, tiles, tile_tok)
        key_row, key_col = block_place(key_pos, tiles, tile_tok)
        row_step = key_row - query_row
        across = key_col - query_col
        nearby = (row_step >= -1) & (row_step <= 1) & (across >= -1) & (across <= 1)
        code_scr[pl.ds(c * CHUNK, CHUNK), :] = jnp.where(nearby, (row_step + 1) * 3 + across + 1, 15)

    def first_hop(p):
        return pltpu.make_async_remote_copy(
            src_ref=own_kv.at[:, tokens_of(p), :],
            dst_ref=slots.at[0, :, tokens_of(p), :],
            send_sem=hop_send.at[p],
            recv_sem=hop_recv.at[p],
            device_id=(right, tile),
            device_id_type=MESH_ID,
        )

    for which in range(2):
        locals_[which].wait()

    @pl.when(me < frames - 1)
    def _():
        first_hop(tile).start()

    for offset in near_first:
        for which in range(2):
            piece_in(which, offset).wait_recv()

        @pl.when(me < frames - 1)
        def _():
            first_hop(lax.rem(tile + tiles - offset, tiles)).start()

    def copy_for(step):
        source = own_kv if step == 0 else slots.at[step - 1]
        return pltpu.make_async_remote_copy(
            src_ref=source,
            dst_ref=slots.at[step],
            send_sem=send_sem.at[step],
            recv_sem=recv_sem.at[step],
            device_id=(right, tile),
            device_id_type=MESH_ID,
        )

    copies = [None] + [copy_for(step) for step in range(1, WIN)]

    m_scr[...] = jnp.full(m_scr.shape, NEG_BIG, jnp.float32)
    l_scr[...] = jnp.zeros(l_scr.shape, jnp.float32)
    acc_scr[...] = jnp.zeros(acc_scr.shape, jnp.float32)

    locals_[2].wait()
    for offset in range(1, tiles):
        piece_in(2, offset).wait_recv()

    def attend(block, use):
        def head_body(h, carry):
            col = pl.multiple_of(h * HD, HD)
            key_h = block[0, :, pl.ds(col, HD)]
            value_h = block[1, :, pl.ds(col, HD)]
            for c in range(frame_tok // CHUNK):
                rows = pl.ds(c * CHUNK, CHUNK)
                query_h = own_q[rows, pl.ds(col, HD)]
                scores = lax.dot_general(
                    query_h, key_h, (((1,), (1,)), ((), ())),
                    preferred_element_type=jnp.float32,
                ) * scale
                if use is None:
                    code = code_scr[rows, :]
                    shifted = lax.shift_right_logical(jnp.broadcast_to(bits_ref[h], code.shape), code)
                    allowed = (shifted & 1) == 1
                else:
                    allowed = jnp.broadcast_to(use > 0, scores.shape)
                scores = jnp.where(allowed, scores, NEG_BIG)
                old_max = m_scr[h, rows, :]
                new_max = jnp.maximum(old_max, jnp.max(scores, axis=1, keepdims=True))
                weights = jnp.where(allowed, jnp.exp(scores - new_max), 0.0)
                factor = jnp.exp(old_max - new_max)
                l_scr[h, rows, :] = l_scr[h, rows, :] * factor + jnp.sum(weights, axis=1, keepdims=True)
                acc_scr[h, rows, :] = acc_scr[h, rows, :] * factor + jnp.dot(
                    weights.astype(jnp.bfloat16), value_h, preferred_element_type=jnp.float32
                )
                m_scr[h, rows, :] = new_max
            return carry

        lax.fori_loop(0, head_share, head_body, 0)

    attend(own_kv, None)
    for step in range(1, WIN + 1):
        @pl.when(me >= step)
        def _():
            if step == 1:
                for p in range(tiles):
                    first_hop(p).wait_recv()
            else:
                copies[step - 1].wait_recv()
            if step < WIN:
                @pl.when(me < frames - 1)
                def _():
                    copies[step].start()
            attend(slots.at[step - 1], use_ref[step - 1])

    def finish(h, carry):
        col = pl.multiple_of(h * HD, HD)
        fin[:, pl.ds(col, HD)] = (acc_scr[h] / l_scr[h] * gain_ref[h]).astype(fin.dtype)
        return carry

    lax.fori_loop(0, head_share, finish, 0)

    def back_out(offset):
        peer = lax.rem(tile + offset, tiles)
        return pltpu.make_async_remote_copy(
            src_ref=fin.at[tokens_of(peer), :],
            dst_ref=got_out.at[:, channels_of(tile)],
            send_sem=piece_send.at[3, offset],
            recv_sem=piece_recv.at[3, tile],
            device_id=(me, peer),
            device_id_type=MESH_ID,
        )

    def back_in(offset):
        sender = lax.rem(tile + tiles - offset, tiles)
        return pltpu.make_async_remote_copy(
            src_ref=fin.at[tokens_of(tile), :],
            dst_ref=got_out.at[:, channels_of(sender)],
            send_sem=piece_send.at[3, offset],
            recv_sem=piece_recv.at[3, sender],
            device_id=(me, sender),
            device_id_type=MESH_ID,
        )

    home = pltpu.make_async_copy(fin.at[tokens_of(tile), :], got_out.at[:, channels_of(tile)],
                                 local_sem.at[3])
    home.start()
    for offset in range(1, tiles):
        back_out(offset).start()
    home.wait()
    for offset in range(1, tiles):
        back_in(offset).wait_recv()
    out_ref[...] = got_out[...]

    for which in range(3):
        for offset in range(1, tiles):
            piece_out(which, offset).wait_send()
    for offset in range(1, tiles):
        back_out(offset).wait_send()
    for step in range(1, WIN):
        @pl.when((me < frames - 1) & (me >= step))
        def _():
            copies[step].wait_send()

    @pl.when(me < frames - 1)
    def _():
        for p in range(tiles):
            first_hop(p).wait_send()


def fused_attend(frames, tiles, use, gains, bits, q, k, v):
    head_share = gains.shape[0]
    tile_tok, channels = q.shape
    frame_tok = tile_tok * tiles
    share = channels // tiles
    flops = 4 * (WIN + 1) * frame_tok * frame_tok * share
    smem = pl.BlockSpec(memory_space=pltpu.SMEM)
    vmem = pl.BlockSpec(memory_space=pltpu.VMEM)
    return pl.pallas_call(
        functools.partial(fused_kernel, frames, tiles),
        out_shape=jax.ShapeDtypeStruct(q.shape, jnp.bfloat16),
        in_specs=[smem, smem, smem, vmem, vmem, vmem],
        out_specs=vmem,
        scratch_shapes=[
            pltpu.VMEM((2, frame_tok, share), jnp.bfloat16),
            pltpu.VMEM((frame_tok, share), jnp.bfloat16),
            pltpu.VMEM((WIN, 2, frame_tok, share), jnp.bfloat16),
            pltpu.VMEM((frame_tok, share), jnp.bfloat16),
            pltpu.VMEM((tile_tok, channels), jnp.bfloat16),
            pltpu.VMEM((frame_tok, frame_tok), jnp.int32),
            pltpu.VMEM((head_share, frame_tok, 1), jnp.float32),
            pltpu.VMEM((head_share, frame_tok, 1), jnp.float32),
            pltpu.VMEM((head_share, frame_tok, HD), jnp.float32),
            pltpu.SemaphoreType.DMA((4, tiles)),
            pltpu.SemaphoreType.DMA((4, tiles)),
            pltpu.SemaphoreType.DMA((4,)),
            pltpu.SemaphoreType.DMA((WIN,)),
            pltpu.SemaphoreType.DMA((WIN,)),
            pltpu.SemaphoreType.DMA((tiles,)),
            pltpu.SemaphoreType.DMA((tiles,)),
        ],
        compiler_params=pltpu.CompilerParams(
            collective_id=0, has_side_effects=True, vmem_limit_bytes=56 * 1024 * 1024
        ),
        cost_estimate=pl.CostEstimate(
            flops=flops,
            transcendentals=(WIN + 1) * head_share * frame_tok * frame_tok,
            bytes_accessed=(WIN + 6) * 2 * frame_tok * share * 2,
        ),
    )(use, gains, bits, q, k, v)


def shards(queries, keys, values, step_index, frame_index, window_mask, history_mask, step_gain):
    tile_count = lax.axis_size("tile")
    frames = lax.axis_size("frame")
    tile_id = lax.axis_index("tile")
    group_id = lax.axis_index("frame")
    channels = queries.shape[-1]
    head_share = HEADS // tile_count
    tile_tok = queries.shape[2]
    frame_tok = tile_tok * tile_count
    picker = (jnp.arange(STEPS, dtype=jnp.int32) == step_index[0]).astype(jnp.float32)
    head_gains = jnp.dot(picker, step_gain, precision=lax.Precision.HIGHEST)
    my_gains = lax.dynamic_slice_in_dim(head_gains, tile_id * head_share, head_share)
    my_masks = lax.dynamic_slice_in_dim(window_mask, tile_id * head_share, head_share, axis=0)
    distance = jnp.arange(1, WIN + 1, dtype=jnp.int32)
    use = (
        (history_mask[0] == 1) & (distance <= frame_index[0]) & (group_id - distance >= 0)
    ).astype(jnp.int32)
    bits = jnp.sum(
        jnp.where(my_masks == 1, jnp.left_shift(1, jnp.arange(9, dtype=jnp.int32)), 0), axis=1
    ) | 16
    finished = fused_attend(
        frames, tile_count, use, my_gains, bits.astype(jnp.int32),
        queries[0, 0], keys[0, 0], values[0, 0],
    )
    return finished.reshape(1, 1, tile_tok, channels)


def solution(mesh):
    return jax.shard_map(
        shards,
        mesh=mesh,
        in_specs=(
            P("frame", "tile", None, None),
            P("frame", "tile", None, None),
            P("frame", "tile", None, None),
            P("frame"),
            P("frame"),
            P(),
            P("frame", None),
            P(),
        ),
        out_specs=P("frame", "tile", None, None),
        check_vma=False,
    )
```

```python
import functools
import math

import jax
import jax.numpy as jnp
from jax import lax
from jax.experimental import pallas as pl
from jax.experimental.pallas import tpu as pltpu
from jax.sharding import PartitionSpec as P

HEADS = 40
HD = 128
TH = 8
TW = 8
BLK = 4
WIN = 5
STEPS = 4
CHUNK = 256

NEG_BIG = -1e30
MESH_ID = pl.DeviceIdType.MESH


def block_place(positions, tile_count, tile_tok):
    tile_cols = min(tile_count, 4)
    tile_of = positions // tile_tok
    within = positions % tile_tok
    row = tile_of // tile_cols * TH + within // TW
    col = tile_of % tile_cols * TW + within % TW
    return row // BLK, col // BLK


def fused_kernel(frames, tiles, use_ref, gain_ref, bits_ref, q_ref, k_ref, v_ref, out_ref,
                 own_kv, own_q, slots, fin, got_out, code_scr, m_scr, l_scr, acc_scr,
                 piece_send, piece_recv, local_sem, hop_send, hop_recv):
    me = lax.axis_index("frame")
    tile = lax.axis_index("tile")
    right = lax.rem(me + 1, frames)
    left = lax.rem(me + frames - 1, frames)
    head_share = acc_scr.shape[0]
    frame_tok = own_q.shape[0]
    share = own_q.shape[1]
    tile_tok = q_ref.shape[0]
    scale = 1.0 / math.sqrt(HD)

    barrier = pltpu.get_barrier_semaphore()
    for other in (left, right):
        pl.semaphore_signal(barrier, inc=1, device_id=(other, tile), device_id_type=MESH_ID)
    for offset in range(1, tiles):
        peer = lax.rem(tile + offset, tiles)
        pl.semaphore_signal(barrier, inc=1, device_id=(me, peer), device_id_type=MESH_ID)
    pl.semaphore_wait(barrier, 2 + tiles - 1)

    def channels_of(p):
        return pl.ds(pl.multiple_of(p * share, 128), share)

    def tokens_of(p):
        return pl.ds(pl.multiple_of(p * tile_tok, tile_tok), tile_tok)

    sources = [k_ref, v_ref, q_ref]
    targets = [lambda rows: own_kv.at[0, rows, :], lambda rows: own_kv.at[1, rows, :],
               lambda rows: own_q.at[rows, :]]

    def piece_out(which, offset):
        peer = lax.rem(tile + offset, tiles)
        return pltpu.make_async_remote_copy(
            src_ref=sources[which].at[:, channels_of(peer)],
            dst_ref=targets[which](tokens_of(tile)),
            send_sem=piece_send.at[which, offset],
            recv_sem=piece_recv.at[which, tile],
            device_id=(me, peer),
            device_id_type=MESH_ID,
        )

    def piece_in(which, offset):
        sender = lax.rem(tile + tiles - offset, tiles)
        return pltpu.make_async_remote_copy(
            src_ref=sources[which].at[:, channels_of(tile)],
            dst_ref=targets[which](tokens_of(sender)),
            send_sem=piece_send.at[which, offset],
            recv_sem=piece_recv.at[which, sender],
            device_id=(me, sender),
            device_id_type=MESH_ID,
        )

    locals_ = [
        pltpu.make_async_copy(
            sources[which].at[:, channels_of(tile)], targets[which](tokens_of(tile)),
            local_sem.at[which],
        )
        for which in range(3)
    ]
    far_first = [j for j in range(1, tiles) if j % 2] + [j for j in range(1, tiles) if j % 2 == 0]
    near_first = far_first[::-1]
    for which in range(3):
        locals_[which].start()
        for offset in far_first:
            piece_out(which, offset).start()

    def hop(step, p):
        source = own_kv if step == 0 else slots.at[step - 1]
        return pltpu.make_async_remote_copy(
            src_ref=source.at[:, tokens_of(p), :],
            dst_ref=slots.at[step, :, tokens_of(p), :],
            send_sem=hop_send.at[step, p],
            recv_sem=hop_recv.at[step, p],
            device_id=(right, tile),
            device_id_type=MESH_ID,
        )

    def pass_on(step, p):
        @pl.when((me < frames - 1) & (me >= step))
        def _():
            hop(step, p).start()

    def take(step, p):
        @pl.when(me >= step + 1)
        def _():
            hop(step, p).wait_recv()

    def sender_of(offset):
        return lax.rem(tile + tiles - offset, tiles)

    early = [0] + [j for j in near_first if j % 2 == 0]
    late = [j for j in range(1, tiles) if j % 2]

    for which in range(2):
        locals_[which].wait()
    for offset in early:
        p = sender_of(offset)
        if offset:
            for which in range(2):
                piece_in(which, offset).wait_recv()
        pass_on(0, p)
        for step in range(1, WIN):
            take(step - 1, p)
            pass_on(step, p)
        take(WIN - 1, p)

    for c in range(frame_tok // CHUNK):
        query_pos = c * CHUNK + lax.broadcasted_iota(jnp.int32, (CHUNK, frame_tok), 0)
        key_pos = lax.broadcasted_iota(jnp.int32, (CHUNK, frame_tok), 1)
        query_row, query_col = block_place(query_pos, tiles, tile_tok)
        key_row, key_col = block_place(key_pos, tiles, tile_tok)
        row_step = key_row - query_row
        across = key_col - query_col
        nearby = (row_step >= -1) & (row_step <= 1) & (across >= -1) & (across <= 1)
        code_scr[pl.ds(c * CHUNK, CHUNK), :] = jnp.where(nearby, (row_step + 1) * 3 + across + 1, 15)
    m_scr[...] = jnp.full(m_scr.shape, NEG_BIG, jnp.float32)
    l_scr[...] = jnp.zeros(l_scr.shape, jnp.float32)
    acc_scr[...] = jnp.zeros(acc_scr.shape, jnp.float32)

    for offset in late:
        for which in range(2):
            piece_in(which, offset).wait_recv()
        pass_on(0, sender_of(offset))

    locals_[2].wait()
    for offset in range(1, tiles):
        piece_in(2, offset).wait_recv()

    def attend(block, use):
        def head_body(h, carry):
            col = pl.multiple_of(h * HD, HD)
            key_h = block[0, :, pl.ds(col, HD)]
            value_h = block[1, :, pl.ds(col, HD)]
            for c in range(frame_tok // CHUNK):
                rows = pl.ds(c * CHUNK, CHUNK)
                query_h = own_q[rows, pl.ds(col, HD)]
                scores = lax.dot_general(
                    query_h, key_h, (((1,), (1,)), ((), ())),
                    preferred_element_type=jnp.float32,
                ) * scale
                if use is None:
                    code = code_scr[rows, :]
                    shifted = lax.shift_right_logical(jnp.broadcast_to(bits_ref[h], code.shape), code)
                    scores = jnp.where((shifted & 1) == 1, scores, NEG_BIG)
                else:
                    scores = scores + jnp.where(use > 0, 0.0, NEG_BIG)
                old_max = m_scr[h, rows, :]
                new_max = jnp.maximum(old_max, jnp.max(scores, axis=1, keepdims=True))
                weights = jnp.exp(scores - new_max)
                factor = jnp.exp(old_max - new_max)
                l_scr[h, rows, :] = l_scr[h, rows, :] * factor + jnp.sum(weights, axis=1, keepdims=True)
                acc_scr[h, rows, :] = acc_scr[h, rows, :] * factor + jnp.dot(
                    weights.astype(jnp.bfloat16), value_h, preferred_element_type=jnp.float32
                )
                m_scr[h, rows, :] = new_max
            return carry

        lax.fori_loop(0, head_share, head_body, 0)

    attend(own_kv, None)
    for step in range(1, WIN + 1):
        for offset in late:
            take(step - 1, sender_of(offset))
            if step < WIN:
                pass_on(step, sender_of(offset))

        @pl.when(me >= step)
        def _():
            attend(slots.at[step - 1], use_ref[step - 1])

    def finish(h, carry):
        col = pl.multiple_of(h * HD, HD)
        fin[:, pl.ds(col, HD)] = (acc_scr[h] / l_scr[h] * gain_ref[h]).astype(fin.dtype)
        return carry

    lax.fori_loop(0, head_share, finish, 0)

    def back_out(offset):
        peer = lax.rem(tile + offset, tiles)
        return pltpu.make_async_remote_copy(
            src_ref=fin.at[tokens_of(peer), :],
            dst_ref=got_out.at[:, channels_of(tile)],
            send_sem=piece_send.at[3, offset],
            recv_sem=piece_recv.at[3, tile],
            device_id=(me, peer),
            device_id_type=MESH_ID,
        )

    def back_in(offset):
        sender = lax.rem(tile + tiles - offset, tiles)
        return pltpu.make_async_remote_copy(
            src_ref=fin.at[tokens_of(tile), :],
            dst_ref=got_out.at[:, channels_of(sender)],
            send_sem=piece_send.at[3, offset],
            recv_sem=piece_recv.at[3, sender],
            device_id=(me, sender),
            device_id_type=MESH_ID,
        )

    home = pltpu.make_async_copy(fin.at[tokens_of(tile), :], got_out.at[:, channels_of(tile)],
                                 local_sem.at[3])
    home.start()
    for offset in range(1, tiles):
        back_out(offset).start()
    home.wait()
    for offset in range(1, tiles):
        back_in(offset).wait_recv()
    out_ref[...] = got_out[...]

    for which in range(3):
        for offset in range(1, tiles):
            piece_out(which, offset).wait_send()
    for offset in range(1, tiles):
        back_out(offset).wait_send()
    for step in range(WIN):
        for p in range(tiles):
            @pl.when((me < frames - 1) & (me >= step))
            def _():
                hop(step, p).wait_send()


def fused_attend(frames, tiles, use, gains, bits, q, k, v):
    head_share = gains.shape[0]
    tile_tok, channels = q.shape
    frame_tok = tile_tok * tiles
    share = channels // tiles
    flops = 4 * (WIN + 1) * frame_tok * frame_tok * share
    smem = pl.BlockSpec(memory_space=pltpu.SMEM)
    vmem = pl.BlockSpec(memory_space=pltpu.VMEM)
    return pl.pallas_call(
        functools.partial(fused_kernel, frames, tiles),
        out_shape=jax.ShapeDtypeStruct(q.shape, jnp.bfloat16),
        in_specs=[smem, smem, smem, vmem, vmem, vmem],
        out_specs=vmem,
        scratch_shapes=[
            pltpu.VMEM((2, frame_tok, share), jnp.bfloat16),
            pltpu.VMEM((frame_tok, share), jnp.bfloat16),
            pltpu.VMEM((WIN, 2, frame_tok, share), jnp.bfloat16),
            pltpu.VMEM((frame_tok, share), jnp.bfloat16),
            pltpu.VMEM((tile_tok, channels), jnp.bfloat16),
            pltpu.VMEM((frame_tok, frame_tok), jnp.int32),
            pltpu.VMEM((head_share, frame_tok, 1), jnp.float32),
            pltpu.VMEM((head_share, frame_tok, 1), jnp.float32),
            pltpu.VMEM((head_share, frame_tok, HD), jnp.float32),
            pltpu.SemaphoreType.DMA((4, tiles)),
            pltpu.SemaphoreType.DMA((4, tiles)),
            pltpu.SemaphoreType.DMA((4,)),
            pltpu.SemaphoreType.DMA((WIN, tiles)),
            pltpu.SemaphoreType.DMA((WIN, tiles)),
        ],
        compiler_params=pltpu.CompilerParams(
            collective_id=0, has_side_effects=True, vmem_limit_bytes=56 * 1024 * 1024
        ),
        cost_estimate=pl.CostEstimate(
            flops=flops,
            transcendentals=(WIN + 1) * head_share * frame_tok * frame_tok,
            bytes_accessed=(WIN + 6) * 2 * frame_tok * share * 2,
        ),
    )(use, gains, bits, q, k, v)


def shards(queries, keys, values, step_index, frame_index, window_mask, history_mask, step_gain):
    tile_count = lax.axis_size("tile")
    frames = lax.axis_size("frame")
    tile_id = lax.axis_index("tile")
    group_id = lax.axis_index("frame")
    channels = queries.shape[-1]
    head_share = HEADS // tile_count
    tile_tok = queries.shape[2]
    frame_tok = tile_tok * tile_count
    picker = (jnp.arange(STEPS, dtype=jnp.int32) == step_index[0]).astype(jnp.float32)
    head_gains = jnp.dot(picker, step_gain, precision=lax.Precision.HIGHEST)
    my_gains = lax.dynamic_slice_in_dim(head_gains, tile_id * head_share, head_share)
    my_masks = lax.dynamic_slice_in_dim(window_mask, tile_id * head_share, head_share, axis=0)
    distance = jnp.arange(1, WIN + 1, dtype=jnp.int32)
    use = (
        (history_mask[0] == 1) & (distance <= frame_index[0]) & (group_id - distance >= 0)
    ).astype(jnp.int32)
    bits = jnp.sum(
        jnp.where(my_masks == 1, jnp.left_shift(1, jnp.arange(9, dtype=jnp.int32)), 0), axis=1
    ) | 16
    finished = fused_attend(
        frames, tile_count, use, my_gains, bits.astype(jnp.int32),
        queries[0, 0], keys[0, 0], values[0, 0],
    )
    return finished.reshape(1, 1, tile_tok, channels)


def solution(mesh):
    return jax.shard_map(
        shards,
        mesh=mesh,
        in_specs=(
            P("frame", "tile", None, None),
            P("frame", "tile", None, None),
            P("frame", "tile", None, None),
            P("frame"),
            P("frame"),
            P(),
            P("frame", None),
            P(),
        ),
        out_specs=P("frame", "tile", None, None),
        check_vma=False,
    )
```

```python
import functools
import math

import jax
import jax.numpy as jnp
from jax import lax
from jax.experimental import pallas as pl
from jax.experimental.pallas import tpu as pltpu
from jax.sharding import PartitionSpec as P

HEADS = 40
HD = 128
TH = 8
TW = 8
BLK = 4
WIN = 5
STEPS = 4
CHUNK = 256

NEG_BIG = -1e30
MESH_ID = pl.DeviceIdType.MESH


def block_place(positions, tile_count, tile_tok):
    tile_cols = min(tile_count, 4)
    tile_of = positions // tile_tok
    within = positions % tile_tok
    row = tile_of // tile_cols * TH + within // TW
    col = tile_of % tile_cols * TW + within % TW
    return row // BLK, col // BLK


def fused_kernel(frames, tiles, use_ref, gain_ref, bits_ref, q_ref, k_ref, v_ref, out_ref,
                 own_kv, own_q, slots, fin, got_out, code_scr, m_scr, l_scr, acc_scr,
                 piece_send, piece_recv, local_sem, hop_send, hop_recv):
    me = lax.axis_index("frame")
    tile = lax.axis_index("tile")
    right = lax.rem(me + 1, frames)
    left = lax.rem(me + frames - 1, frames)
    head_share = acc_scr.shape[0]
    frame_tok = own_q.shape[0]
    share = own_q.shape[1]
    tile_tok = q_ref.shape[0]
    scale = 1.0 / math.sqrt(HD)

    barrier = pltpu.get_barrier_semaphore()
    for other in (left, right):
        pl.semaphore_signal(barrier, inc=1, device_id=(other, tile), device_id_type=MESH_ID)
    for offset in range(1, tiles):
        peer = lax.rem(tile + offset, tiles)
        pl.semaphore_signal(barrier, inc=1, device_id=(me, peer), device_id_type=MESH_ID)
    pl.semaphore_wait(barrier, 2 + tiles - 1)

    def channels_of(p):
        return pl.ds(pl.multiple_of(p * share, 128), share)

    def tokens_of(p):
        return pl.ds(pl.multiple_of(p * tile_tok, tile_tok), tile_tok)

    sources = [k_ref, v_ref, q_ref]
    targets = [lambda rows: own_kv.at[0, rows, :], lambda rows: own_kv.at[1, rows, :],
               lambda rows: own_q.at[rows, :]]

    def piece_out(which, offset):
        peer = lax.rem(tile + offset, tiles)
        return pltpu.make_async_remote_copy(
            src_ref=sources[which].at[:, channels_of(peer)],
            dst_ref=targets[which](tokens_of(tile)),
            send_sem=piece_send.at[which, offset],
            recv_sem=piece_recv.at[which, tile],
            device_id=(me, peer),
            device_id_type=MESH_ID,
        )

    def piece_in(which, offset):
        sender = lax.rem(tile + tiles - offset, tiles)
        return pltpu.make_async_remote_copy(
            src_ref=sources[which].at[:, channels_of(tile)],
            dst_ref=targets[which](tokens_of(sender)),
            send_sem=piece_send.at[which, offset],
            recv_sem=piece_recv.at[which, sender],
            device_id=(me, sender),
            device_id_type=MESH_ID,
        )

    locals_ = [
        pltpu.make_async_copy(
            sources[which].at[:, channels_of(tile)], targets[which](tokens_of(tile)),
            local_sem.at[which],
        )
        for which in range(3)
    ]
    far_first = [j for j in range(1, tiles) if j % 2] + [j for j in range(1, tiles) if j % 2 == 0]
    near_first = far_first[::-1]
    for which in range(3):
        locals_[which].start()
        for offset in far_first:
            piece_out(which, offset).start()

    def hop(step, p):
        source = own_kv if step == 0 else slots.at[step - 1]
        return pltpu.make_async_remote_copy(
            src_ref=source.at[:, tokens_of(p), :],
            dst_ref=slots.at[step, :, tokens_of(p), :],
            send_sem=hop_send.at[step, p],
            recv_sem=hop_recv.at[step, p],
            device_id=(right, tile),
            device_id_type=MESH_ID,
        )

    def pass_on(step, p):
        @pl.when((me < frames - 1) & (me >= step))
        def _():
            hop(step, p).start()

    def take(step, p):
        @pl.when(me >= step + 1)
        def _():
            hop(step, p).wait_recv()

    def sender_of(offset):
        return lax.rem(tile + tiles - offset, tiles)

    early = [0] + [j for j in near_first if j % 2 == 0]
    late = [j for j in range(1, tiles) if j % 2]

    for which in range(2):
        locals_[which].wait()
    for offset in early:
        if offset:
            for which in range(2):
                piece_in(which, offset).wait_recv()
        pass_on(0, sender_of(offset))
    for step in range(1, WIN + 1):
        for offset in early:
            take(step - 1, sender_of(offset))
            if step < WIN:
                pass_on(step, sender_of(offset))

    for c in range(frame_tok // CHUNK):
        query_pos = c * CHUNK + lax.broadcasted_iota(jnp.int32, (CHUNK, frame_tok), 0)
        key_pos = lax.broadcasted_iota(jnp.int32, (CHUNK, frame_tok), 1)
        query_row, query_col = block_place(query_pos, tiles, tile_tok)
        key_row, key_col = block_place(key_pos, tiles, tile_tok)
        row_step = key_row - query_row
        across = key_col - query_col
        nearby = (row_step >= -1) & (row_step <= 1) & (across >= -1) & (across <= 1)
        code_scr[pl.ds(c * CHUNK, CHUNK), :] = jnp.where(nearby, (row_step + 1) * 3 + across + 1, 15)
    m_scr[...] = jnp.full(m_scr.shape, NEG_BIG, jnp.float32)
    l_scr[...] = jnp.zeros(l_scr.shape, jnp.float32)
    acc_scr[...] = jnp.zeros(acc_scr.shape, jnp.float32)

    for offset in late:
        for which in range(2):
            piece_in(which, offset).wait_recv()
        pass_on(0, sender_of(offset))

    locals_[2].wait()
    for offset in range(1, tiles):
        piece_in(2, offset).wait_recv()

    def attend(block, use):
        def head_body(h, carry):
            col = pl.multiple_of(h * HD, HD)
            key_h = block[0, :, pl.ds(col, HD)]
            value_h = block[1, :, pl.ds(col, HD)]
            for c in range(frame_tok // CHUNK):
                rows = pl.ds(c * CHUNK, CHUNK)
                query_h = own_q[rows, pl.ds(col, HD)]
                scores = lax.dot_general(
                    query_h, key_h, (((1,), (1,)), ((), ())),
                    preferred_element_type=jnp.float32,
                ) * scale
                if use is None:
                    code = code_scr[rows, :]
                    shifted = lax.shift_right_logical(jnp.broadcast_to(bits_ref[h], code.shape), code)
                    scores = jnp.where((shifted & 1) == 1, scores, NEG_BIG)
                else:
                    scores = scores + jnp.where(use > 0, 0.0, NEG_BIG)
                old_max = m_scr[h, rows, :]
                new_max = jnp.maximum(old_max, jnp.max(scores, axis=1, keepdims=True))
                weights = jnp.exp(scores - new_max)
                factor = jnp.exp(old_max - new_max)
                l_scr[h, rows, :] = l_scr[h, rows, :] * factor + jnp.sum(weights, axis=1, keepdims=True)
                acc_scr[h, rows, :] = acc_scr[h, rows, :] * factor + jnp.dot(
                    weights.astype(jnp.bfloat16), value_h, preferred_element_type=jnp.float32
                )
                m_scr[h, rows, :] = new_max
            return carry

        lax.fori_loop(0, head_share, head_body, 0)

    attend(own_kv, None)
    for step in range(1, WIN + 1):
        for offset in late:
            take(step - 1, sender_of(offset))
            if step < WIN:
                pass_on(step, sender_of(offset))

        @pl.when(me >= step)
        def _():
            attend(slots.at[step - 1], use_ref[step - 1])

    def finish(h, carry):
        col = pl.multiple_of(h * HD, HD)
        fin[:, pl.ds(col, HD)] = (acc_scr[h] / l_scr[h] * gain_ref[h]).astype(fin.dtype)
        return carry

    lax.fori_loop(0, head_share, finish, 0)

    def back_out(offset):
        peer = lax.rem(tile + offset, tiles)
        return pltpu.make_async_remote_copy(
            src_ref=fin.at[tokens_of(peer), :],
            dst_ref=got_out.at[:, channels_of(tile)],
            send_sem=piece_send.at[3, offset],
            recv_sem=piece_recv.at[3, tile],
            device_id=(me, peer),
            device_id_type=MESH_ID,
        )

    def back_in(offset):
        sender = lax.rem(tile + tiles - offset, tiles)
        return pltpu.make_async_remote_copy(
            src_ref=fin.at[tokens_of(tile), :],
            dst_ref=got_out.at[:, channels_of(sender)],
            send_sem=piece_send.at[3, offset],
            recv_sem=piece_recv.at[3, sender],
            device_id=(me, sender),
            device_id_type=MESH_ID,
        )

    home = pltpu.make_async_copy(fin.at[tokens_of(tile), :], got_out.at[:, channels_of(tile)],
                                 local_sem.at[3])
    home.start()
    for offset in range(1, tiles):
        back_out(offset).start()
    home.wait()
    for offset in range(1, tiles):
        back_in(offset).wait_recv()
    out_ref[...] = got_out[...]

    for which in range(3):
        for offset in range(1, tiles):
            piece_out(which, offset).wait_send()
    for offset in range(1, tiles):
        back_out(offset).wait_send()
    for step in range(WIN):
        for p in range(tiles):
            @pl.when((me < frames - 1) & (me >= step))
            def _():
                hop(step, p).wait_send()


def fused_attend(frames, tiles, use, gains, bits, q, k, v):
    head_share = gains.shape[0]
    tile_tok, channels = q.shape
    frame_tok = tile_tok * tiles
    share = channels // tiles
    flops = 4 * (WIN + 1) * frame_tok * frame_tok * share
    smem = pl.BlockSpec(memory_space=pltpu.SMEM)
    vmem = pl.BlockSpec(memory_space=pltpu.VMEM)
    return pl.pallas_call(
        functools.partial(fused_kernel, frames, tiles),
        out_shape=jax.ShapeDtypeStruct(q.shape, jnp.bfloat16),
        in_specs=[smem, smem, smem, vmem, vmem, vmem],
        out_specs=vmem,
        scratch_shapes=[
            pltpu.VMEM((2, frame_tok, share), jnp.bfloat16),
            pltpu.VMEM((frame_tok, share), jnp.bfloat16),
            pltpu.VMEM((WIN, 2, frame_tok, share), jnp.bfloat16),
            pltpu.VMEM((frame_tok, share), jnp.bfloat16),
            pltpu.VMEM((tile_tok, channels), jnp.bfloat16),
            pltpu.VMEM((frame_tok, frame_tok), jnp.int32),
            pltpu.VMEM((head_share, frame_tok, 1), jnp.float32),
            pltpu.VMEM((head_share, frame_tok, 1), jnp.float32),
            pltpu.VMEM((head_share, frame_tok, HD), jnp.float32),
            pltpu.SemaphoreType.DMA((4, tiles)),
            pltpu.SemaphoreType.DMA((4, tiles)),
            pltpu.SemaphoreType.DMA((4,)),
            pltpu.SemaphoreType.DMA((WIN, tiles)),
            pltpu.SemaphoreType.DMA((WIN, tiles)),
        ],
        compiler_params=pltpu.CompilerParams(
            collective_id=0, has_side_effects=True, vmem_limit_bytes=56 * 1024 * 1024
        ),
        cost_estimate=pl.CostEstimate(
            flops=flops,
            transcendentals=(WIN + 1) * head_share * frame_tok * frame_tok,
            bytes_accessed=(WIN + 6) * 2 * frame_tok * share * 2,
        ),
    )(use, gains, bits, q, k, v)


def shards(queries, keys, values, step_index, frame_index, window_mask, history_mask, step_gain):
    tile_count = lax.axis_size("tile")
    frames = lax.axis_size("frame")
    tile_id = lax.axis_index("tile")
    group_id = lax.axis_index("frame")
    channels = queries.shape[-1]
    head_share = HEADS // tile_count
    tile_tok = queries.shape[2]
    frame_tok = tile_tok * tile_count
    picker = (jnp.arange(STEPS, dtype=jnp.int32) == step_index[0]).astype(jnp.float32)
    head_gains = jnp.dot(picker, step_gain, precision=lax.Precision.HIGHEST)
    my_gains = lax.dynamic_slice_in_dim(head_gains, tile_id * head_share, head_share)
    my_masks = lax.dynamic_slice_in_dim(window_mask, tile_id * head_share, head_share, axis=0)
    distance = jnp.arange(1, WIN + 1, dtype=jnp.int32)
    use = (
        (history_mask[0] == 1) & (distance <= frame_index[0]) & (group_id - distance >= 0)
    ).astype(jnp.int32)
    bits = jnp.sum(
        jnp.where(my_masks == 1, jnp.left_shift(1, jnp.arange(9, dtype=jnp.int32)), 0), axis=1
    ) | 16
    finished = fused_attend(
        frames, tile_count, use, my_gains, bits.astype(jnp.int32),
        queries[0, 0], keys[0, 0], values[0, 0],
    )
    return finished.reshape(1, 1, tile_tok, channels)


def solution(mesh):
    return jax.shard_map(
        shards,
        mesh=mesh,
        in_specs=(
            P("frame", "tile", None, None),
            P("frame", "tile", None, None),
            P("frame", "tile", None, None),
            P("frame"),
            P("frame"),
            P(),
            P("frame", None),
            P(),
        ),
        out_specs=P("frame", "tile", None, None),
        check_vma=False,
    )
```

```python
import functools
import math

import jax
import jax.numpy as jnp
from jax import lax
from jax.experimental import pallas as pl
from jax.experimental.pallas import tpu as pltpu
from jax.sharding import PartitionSpec as P

HEADS = 40
HD = 128
TH = 8
TW = 8
BLK = 4
WIN = 5
STEPS = 4
CHUNK = 128

NEG_BIG = -1e30
MESH_ID = pl.DeviceIdType.MESH


def block_place(positions, tile_count, tile_tok):
    tile_cols = min(tile_count, 4)
    tile_of = positions // tile_tok
    within = positions % tile_tok
    row = tile_of // tile_cols * TH + within // TW
    col = tile_of % tile_cols * TW + within % TW
    return row // BLK, col // BLK


def fused_kernel(frames, tiles, use_ref, gain_ref, bits_ref, q_ref, k_ref, v_ref, out_ref,
                 own_kv, own_q, slots, fin, got_out, code_scr, m_scr, l_scr, acc_scr,
                 piece_send, piece_recv, local_sem, send_sem, recv_sem, hop_send, hop_recv):
    me = lax.axis_index("frame")
    tile = lax.axis_index("tile")
    right = lax.rem(me + 1, frames)
    left = lax.rem(me + frames - 1, frames)
    head_share = acc_scr.shape[0]
    frame_tok = own_q.shape[0]
    share = own_q.shape[1]
    tile_tok = q_ref.shape[0]
    scale = 1.0 / math.sqrt(HD)

    barrier = pltpu.get_barrier_semaphore()
    for other in (left, right):
        pl.semaphore_signal(barrier, inc=1, device_id=(other, tile), device_id_type=MESH_ID)
    for offset in range(1, tiles):
        peer = lax.rem(tile + offset, tiles)
        pl.semaphore_signal(barrier, inc=1, device_id=(me, peer), device_id_type=MESH_ID)
    pl.semaphore_wait(barrier, 2 + tiles - 1)

    def channels_of(p):
        return pl.ds(pl.multiple_of(p * share, 128), share)

    def tokens_of(p):
        return pl.ds(pl.multiple_of(p * tile_tok, tile_tok), tile_tok)

    sources = [k_ref, v_ref, q_ref]
    targets = [lambda rows: own_kv.at[0, rows, :], lambda rows: own_kv.at[1, rows, :],
               lambda rows: own_q.at[rows, :]]

    def piece_out(which, offset):
        peer = lax.rem(tile + offset, tiles)
        return pltpu.make_async_remote_copy(
            src_ref=sources[which].at[:, channels_of(peer)],
            dst_ref=targets[which](tokens_of(tile)),
            send_sem=piece_send.at[which, offset],
            recv_sem=piece_recv.at[which, tile],
            device_id=(me, peer),
            device_id_type=MESH_ID,
        )

    def piece_in(which, offset):
        sender = lax.rem(tile + tiles - offset, tiles)
        return pltpu.make_async_remote_copy(
            src_ref=sources[which].at[:, channels_of(tile)],
            dst_ref=targets[which](tokens_of(sender)),
            send_sem=piece_send.at[which, offset],
            recv_sem=piece_recv.at[which, sender],
            device_id=(me, sender),
            device_id_type=MESH_ID,
        )

    locals_ = [
        pltpu.make_async_copy(
            sources[which].at[:, channels_of(tile)], targets[which](tokens_of(tile)),
            local_sem.at[which],
        )
        for which in range(3)
    ]
    far_first = [j for j in range(1, tiles) if j % 2] + [j for j in range(1, tiles) if j % 2 == 0]
    near_first = far_first[::-1]
    for which in range(3):
        locals_[which].start()
        for offset in far_first:
            piece_out(which, offset).start()

    for c in range(frame_tok // CHUNK):
        query_pos = c * CHUNK + lax.broadcasted_iota(jnp.int32, (CHUNK, frame_tok), 0)
        key_pos = lax.broadcasted_iota(jnp.int32, (CHUNK, frame_tok), 1)
        query_row, query_col = block_place(query_pos, tiles, tile_tok)
        key_row, key_col = block_place(key_pos, tiles, tile_tok)
        row_step = key_row - query_row
        across = key_col - query_col
        nearby = (row_step >= -1) & (row_step <= 1) & (across >= -1) & (across <= 1)
        code_scr[pl.ds(c * CHUNK, CHUNK), :] = jnp.where(nearby, (row_step + 1) * 3 + across + 1, 15)

    def first_hop(p):
        return pltpu.make_async_remote_copy(
            src_ref=own_kv.at[:, tokens_of(p), :],
            dst_ref=slots.at[0, :, tokens_of(p), :],
            send_sem=hop_send.at[p],
            recv_sem=hop_recv.at[p],
            device_id=(right, tile),
            device_id_type=MESH_ID,
        )

    for which in range(2):
        locals_[which].wait()

    @pl.when(me < frames - 1)
    def _():
        first_hop(tile).start()

    for offset in near_first:
        for which in range(2):
            piece_in(which, offset).wait_recv()

        @pl.when(me < frames - 1)
        def _():
            first_hop(lax.rem(tile + tiles - offset, tiles)).start()

    def copy_for(step):
        source = own_kv if step == 0 else slots.at[step - 1]
        return pltpu.make_async_remote_copy(
            src_ref=source,
            dst_ref=slots.at[step],
            send_sem=send_sem.at[step],
            recv_sem=recv_sem.at[step],
            device_id=(right, tile),
            device_id_type=MESH_ID,
        )

    copies = [None] + [copy_for(step) for step in range(1, WIN)]

    m_scr[...] = jnp.full(m_scr.shape, NEG_BIG, jnp.float32)
    l_scr[...] = jnp.zeros(l_scr.shape, jnp.float32)
    acc_scr[...] = jnp.zeros(acc_scr.shape, jnp.float32)

    locals_[2].wait()
    for offset in range(1, tiles):
        piece_in(2, offset).wait_recv()

    def attend(block, use):
        def head_body(h, carry):
            col = pl.multiple_of(h * HD, HD)
            key_h = block[0, :, pl.ds(col, HD)]
            value_h = block[1, :, pl.ds(col, HD)]
            for c in range(frame_tok // CHUNK):
                rows = pl.ds(c * CHUNK, CHUNK)
                query_h = own_q[rows, pl.ds(col, HD)]
                scores = lax.dot_general(
                    query_h, key_h, (((1,), (1,)), ((), ())),
                    preferred_element_type=jnp.float32,
                ) * scale
                if use is None:
                    code = code_scr[rows, :]
                    shifted = lax.shift_right_logical(jnp.broadcast_to(bits_ref[h], code.shape), code)
                    scores = jnp.where((shifted & 1) == 1, scores, NEG_BIG)
                else:
                    scores = scores + jnp.where(use > 0, 0.0, NEG_BIG)
                old_max = m_scr[h, rows, :]
                new_max = jnp.maximum(old_max, jnp.max(scores, axis=1, keepdims=True))
                weights = jnp.exp(scores - new_max)
                factor = jnp.exp(old_max - new_max)
                l_scr[h, rows, :] = l_scr[h, rows, :] * factor + jnp.sum(weights, axis=1, keepdims=True)
                acc_scr[h, rows, :] = acc_scr[h, rows, :] * factor + jnp.dot(
                    weights.astype(jnp.bfloat16), value_h, preferred_element_type=jnp.float32
                )
                m_scr[h, rows, :] = new_max
            return carry

        lax.fori_loop(0, head_share, head_body, 0)

    attend(own_kv, None)
    for step in range(1, WIN + 1):
        @pl.when(me >= step)
        def _():
            if step == 1:
                for p in range(tiles):
                    first_hop(p).wait_recv()
            else:
                copies[step - 1].wait_recv()
            if step < WIN:
                @pl.when(me < frames - 1)
                def _():
                    copies[step].start()
            attend(slots.at[step - 1], use_ref[step - 1])

    def finish(h, carry):
        col = pl.multiple_of(h * HD, HD)
        fin[:, pl.ds(col, HD)] = (acc_scr[h] / l_scr[h] * gain_ref[h]).astype(fin.dtype)
        return carry

    lax.fori_loop(0, head_share, finish, 0)

    def back_out(offset):
        peer = lax.rem(tile + offset, tiles)
        return pltpu.make_async_remote_copy(
            src_ref=fin.at[tokens_of(peer), :],
            dst_ref=got_out.at[:, channels_of(tile)],
            send_sem=piece_send.at[3, offset],
            recv_sem=piece_recv.at[3, tile],
            device_id=(me, peer),
            device_id_type=MESH_ID,
        )

    def back_in(offset):
        sender = lax.rem(tile + tiles - offset, tiles)
        return pltpu.make_async_remote_copy(
            src_ref=fin.at[tokens_of(tile), :],
            dst_ref=got_out.at[:, channels_of(sender)],
            send_sem=piece_send.at[3, offset],
            recv_sem=piece_recv.at[3, sender],
            device_id=(me, sender),
            device_id_type=MESH_ID,
        )

    home = pltpu.make_async_copy(fin.at[tokens_of(tile), :], got_out.at[:, channels_of(tile)],
                                 local_sem.at[3])
    home.start()
    for offset in range(1, tiles):
        back_out(offset).start()
    home.wait()
    for offset in range(1, tiles):
        back_in(offset).wait_recv()
    out_ref[...] = got_out[...]

    for which in range(3):
        for offset in range(1, tiles):
            piece_out(which, offset).wait_send()
    for offset in range(1, tiles):
        back_out(offset).wait_send()
    for step in range(1, WIN):
        @pl.when((me < frames - 1) & (me >= step))
        def _():
            copies[step].wait_send()

    @pl.when(me < frames - 1)
    def _():
        for p in range(tiles):
            first_hop(p).wait_send()


def fused_attend(frames, tiles, use, gains, bits, q, k, v):
    head_share = gains.shape[0]
    tile_tok, channels = q.shape
    frame_tok = tile_tok * tiles
    share = channels // tiles
    flops = 4 * (WIN + 1) * frame_tok * frame_tok * share
    smem = pl.BlockSpec(memory_space=pltpu.SMEM)
    vmem = pl.BlockSpec(memory_space=pltpu.VMEM)
    return pl.pallas_call(
        functools.partial(fused_kernel, frames, tiles),
        out_shape=jax.ShapeDtypeStruct(q.shape, jnp.bfloat16),
        in_specs=[smem, smem, smem, vmem, vmem, vmem],
        out_specs=vmem,
        scratch_shapes=[
            pltpu.VMEM((2, frame_tok, share), jnp.bfloat16),
            pltpu.VMEM((frame_tok, share), jnp.bfloat16),
            pltpu.VMEM((WIN, 2, frame_tok, share), jnp.bfloat16),
            pltpu.VMEM((frame_tok, share), jnp.bfloat16),
            pltpu.VMEM((tile_tok, channels), jnp.bfloat16),
            pltpu.VMEM((frame_tok, frame_tok), jnp.int32),
            pltpu.VMEM((head_share, frame_tok, 1), jnp.float32),
            pltpu.VMEM((head_share, frame_tok, 1), jnp.float32),
            pltpu.VMEM((head_share, frame_tok, HD), jnp.float32),
            pltpu.SemaphoreType.DMA((4, tiles)),
            pltpu.SemaphoreType.DMA((4, tiles)),
            pltpu.SemaphoreType.DMA((4,)),
            pltpu.SemaphoreType.DMA((WIN,)),
            pltpu.SemaphoreType.DMA((WIN,)),
            pltpu.SemaphoreType.DMA((tiles,)),
            pltpu.SemaphoreType.DMA((tiles,)),
        ],
        compiler_params=pltpu.CompilerParams(
            collective_id=0, has_side_effects=True, vmem_limit_bytes=56 * 1024 * 1024
        ),
        cost_estimate=pl.CostEstimate(
            flops=flops,
            transcendentals=(WIN + 1) * head_share * frame_tok * frame_tok,
            bytes_accessed=(WIN + 6) * 2 * frame_tok * share * 2,
        ),
    )(use, gains, bits, q, k, v)


def shards(queries, keys, values, step_index, frame_index, window_mask, history_mask, step_gain):
    tile_count = lax.axis_size("tile")
    frames = lax.axis_size("frame")
    tile_id = lax.axis_index("tile")
    group_id = lax.axis_index("frame")
    channels = queries.shape[-1]
    head_share = HEADS // tile_count
    tile_tok = queries.shape[2]
    frame_tok = tile_tok * tile_count
    picker = (jnp.arange(STEPS, dtype=jnp.int32) == step_index[0]).astype(jnp.float32)
    head_gains = jnp.dot(picker, step_gain, precision=lax.Precision.HIGHEST)
    my_gains = lax.dynamic_slice_in_dim(head_gains, tile_id * head_share, head_share)
    my_masks = lax.dynamic_slice_in_dim(window_mask, tile_id * head_share, head_share, axis=0)
    distance = jnp.arange(1, WIN + 1, dtype=jnp.int32)
    use = (
        (history_mask[0] == 1) & (distance <= frame_index[0]) & (group_id - distance >= 0)
    ).astype(jnp.int32)
    bits = jnp.sum(
        jnp.where(my_masks == 1, jnp.left_shift(1, jnp.arange(9, dtype=jnp.int32)), 0), axis=1
    ) | 16
    finished = fused_attend(
        frames, tile_count, use, my_gains, bits.astype(jnp.int32),
        queries[0, 0], keys[0, 0], values[0, 0],
    )
    return finished.reshape(1, 1, tile_tok, channels)


def solution(mesh):
    return jax.shard_map(
        shards,
        mesh=mesh,
        in_specs=(
            P("frame", "tile", None, None),
            P("frame", "tile", None, None),
            P("frame", "tile", None, None),
            P("frame"),
            P("frame"),
            P(),
            P("frame", None),
            P(),
        ),
        out_specs=P("frame", "tile", None, None),
        check_vma=False,
    )
```

```python
import functools
import math

import jax
import jax.numpy as jnp
from jax import lax
from jax.experimental import pallas as pl
from jax.experimental.pallas import tpu as pltpu
from jax.sharding import PartitionSpec as P

HEADS = 40
HD = 128
TH = 8
TW = 8
BLK = 4
WIN = 5
STEPS = 4
CHUNK = 128

NEG_BIG = -1e30
MESH_ID = pl.DeviceIdType.MESH


def block_place(positions, tile_count, tile_tok):
    tile_cols = min(tile_count, 4)
    tile_of = positions // tile_tok
    within = positions % tile_tok
    row = tile_of // tile_cols * TH + within // TW
    col = tile_of % tile_cols * TW + within % TW
    return row // BLK, col // BLK


def fused_kernel(frames, tiles, use_ref, gain_ref, bits_ref, q_ref, k_ref, v_ref, out_ref,
                 own_kv, own_q, slots, fin, got_out, code_scr, m_scr, l_scr, acc_scr,
                 piece_send, piece_recv, local_sem, send_sem, recv_sem, hop_send, hop_recv,
                 out_send, out_recv, home_sem):
    me = lax.axis_index("frame")
    tile = lax.axis_index("tile")
    right = lax.rem(me + 1, frames)
    left = lax.rem(me + frames - 1, frames)
    head_share = acc_scr.shape[0]
    frame_tok = own_q.shape[0]
    share = own_q.shape[1]
    tile_tok = q_ref.shape[0]
    scale = 1.0 / math.sqrt(HD)

    barrier = pltpu.get_barrier_semaphore()
    for other in (left, right):
        pl.semaphore_signal(barrier, inc=1, device_id=(other, tile), device_id_type=MESH_ID)
    for offset in range(1, tiles):
        peer = lax.rem(tile + offset, tiles)
        pl.semaphore_signal(barrier, inc=1, device_id=(me, peer), device_id_type=MESH_ID)
    pl.semaphore_wait(barrier, 2 + tiles - 1)

    def channels_of(p):
        return pl.ds(pl.multiple_of(p * share, 128), share)

    def tokens_of(p):
        return pl.ds(pl.multiple_of(p * tile_tok, tile_tok), tile_tok)

    sources = [k_ref, v_ref, q_ref]
    targets = [lambda rows: own_kv.at[0, rows, :], lambda rows: own_kv.at[1, rows, :],
               lambda rows: own_q.at[rows, :]]

    def piece_out(which, offset):
        peer = lax.rem(tile + offset, tiles)
        return pltpu.make_async_remote_copy(
            src_ref=sources[which].at[:, channels_of(peer)],
            dst_ref=targets[which](tokens_of(tile)),
            send_sem=piece_send.at[which, offset],
            recv_sem=piece_recv.at[which, tile],
            device_id=(me, peer),
            device_id_type=MESH_ID,
        )

    def piece_in(which, offset):
        sender = lax.rem(tile + tiles - offset, tiles)
        return pltpu.make_async_remote_copy(
            src_ref=sources[which].at[:, channels_of(tile)],
            dst_ref=targets[which](tokens_of(sender)),
            send_sem=piece_send.at[which, offset],
            recv_sem=piece_recv.at[which, sender],
            device_id=(me, sender),
            device_id_type=MESH_ID,
        )

    locals_ = [
        pltpu.make_async_copy(
            sources[which].at[:, channels_of(tile)], targets[which](tokens_of(tile)),
            local_sem.at[which],
        )
        for which in range(3)
    ]
    far_first = [j for j in range(1, tiles) if j % 2] + [j for j in range(1, tiles) if j % 2 == 0]
    near_first = far_first[::-1]
    for which in range(3):
        locals_[which].start()
        for offset in far_first:
            piece_out(which, offset).start()

    for c in range(frame_tok // CHUNK):
        query_pos = c * CHUNK + lax.broadcasted_iota(jnp.int32, (CHUNK, frame_tok), 0)
        key_pos = lax.broadcasted_iota(jnp.int32, (CHUNK, frame_tok), 1)
        query_row, query_col = block_place(query_pos, tiles, tile_tok)
        key_row, key_col = block_place(key_pos, tiles, tile_tok)
        row_step = key_row - query_row
        across = key_col - query_col
        nearby = (row_step >= -1) & (row_step <= 1) & (across >= -1) & (across <= 1)
        code_scr[pl.ds(c * CHUNK, CHUNK), :] = jnp.where(nearby, (row_step + 1) * 3 + across + 1, 15)

    def first_hop(p):
        return pltpu.make_async_remote_copy(
            src_ref=own_kv.at[:, tokens_of(p), :],
            dst_ref=slots.at[0, :, tokens_of(p), :],
            send_sem=hop_send.at[p],
            recv_sem=hop_recv.at[p],
            device_id=(right, tile),
            device_id_type=MESH_ID,
        )

    for which in range(2):
        locals_[which].wait()

    @pl.when(me < frames - 1)
    def _():
        first_hop(tile).start()

    for offset in near_first:
        for which in range(2):
            piece_in(which, offset).wait_recv()

        @pl.when(me < frames - 1)
        def _():
            first_hop(lax.rem(tile + tiles - offset, tiles)).start()

    def copy_for(step):
        source = own_kv if step == 0 else slots.at[step - 1]
        return pltpu.make_async_remote_copy(
            src_ref=source,
            dst_ref=slots.at[step],
            send_sem=send_sem.at[step],
            recv_sem=recv_sem.at[step],
            device_id=(right, tile),
            device_id_type=MESH_ID,
        )

    copies = [None] + [copy_for(step) for step in range(1, WIN)]

    m_scr[...] = jnp.full(m_scr.shape, NEG_BIG, jnp.float32)
    l_scr[...] = jnp.zeros(l_scr.shape, jnp.float32)
    acc_scr[...] = jnp.zeros(acc_scr.shape, jnp.float32)

    locals_[2].wait()
    for offset in range(1, tiles):
        piece_in(2, offset).wait_recv()

    def attend_head(block, use, h):
        if True:
            col = pl.multiple_of(h * HD, HD)
            key_h = block[0, :, pl.ds(col, HD)]
            value_h = block[1, :, pl.ds(col, HD)]
            for c in range(frame_tok // CHUNK):
                rows = pl.ds(c * CHUNK, CHUNK)
                query_h = own_q[rows, pl.ds(col, HD)]
                scores = lax.dot_general(
                    query_h, key_h, (((1,), (1,)), ((), ())),
                    preferred_element_type=jnp.float32,
                ) * scale
                if use is None:
                    code = code_scr[rows, :]
                    shifted = lax.shift_right_logical(jnp.broadcast_to(bits_ref[h], code.shape), code)
                    scores = jnp.where((shifted & 1) == 1, scores, NEG_BIG)
                else:
                    scores = scores + jnp.where(use > 0, 0.0, NEG_BIG)
                old_max = m_scr[h, rows, :]
                new_max = jnp.maximum(old_max, jnp.max(scores, axis=1, keepdims=True))
                weights = jnp.exp(scores - new_max)
                factor = jnp.exp(old_max - new_max)
                l_scr[h, rows, :] = l_scr[h, rows, :] * factor + jnp.sum(weights, axis=1, keepdims=True)
                acc_scr[h, rows, :] = acc_scr[h, rows, :] * factor + jnp.dot(
                    weights.astype(jnp.bfloat16), value_h, preferred_element_type=jnp.float32
                )
                m_scr[h, rows, :] = new_max

    def attend(block, use):
        def head_body(h, carry):
            attend_head(block, use, h)
            return carry

        lax.fori_loop(0, head_share, head_body, 0)

    attend(own_kv, None)
    for step in range(1, WIN + 1):
        @pl.when(me >= step)
        def _():
            if step == 1:
                for p in range(tiles):
                    first_hop(p).wait_recv()
            else:
                copies[step - 1].wait_recv()
            if step < WIN:
                @pl.when(me < frames - 1)
                def _():
                    copies[step].start()
                attend(slots.at[step - 1], use_ref[step - 1])

    def head_cols(p, h):
        return pl.ds(pl.multiple_of(p * share + h * HD, HD), HD)

    def back_out(offset, h):
        peer = lax.rem(tile + offset, tiles)
        return pltpu.make_async_remote_copy(
            src_ref=fin.at[tokens_of(peer), pl.ds(h * HD, HD)],
            dst_ref=got_out.at[:, head_cols(tile, h)],
            send_sem=out_send.at[offset, h],
            recv_sem=out_recv.at[tile, h],
            device_id=(me, peer),
            device_id_type=MESH_ID,
        )

    def back_in(offset, h):
        sender = lax.rem(tile + tiles - offset, tiles)
        return pltpu.make_async_remote_copy(
            src_ref=fin.at[tokens_of(tile), pl.ds(h * HD, HD)],
            dst_ref=got_out.at[:, head_cols(sender, h)],
            send_sem=out_send.at[offset, h],
            recv_sem=out_recv.at[sender, h],
            device_id=(me, sender),
            device_id_type=MESH_ID,
        )

    def home(h):
        return pltpu.make_async_copy(
            fin.at[tokens_of(tile), pl.ds(h * HD, HD)], got_out.at[:, head_cols(tile, h)],
            home_sem.at[h],
        )

    for h in range(head_share):
        @pl.when(me >= WIN)
        def _():
            attend_head(slots.at[WIN - 1], use_ref[WIN - 1], h)

        fin[:, pl.ds(h * HD, HD)] = (acc_scr[h] / l_scr[h] * gain_ref[h]).astype(fin.dtype)
        home(h).start()
        for offset in far_first:
            back_out(offset, h).start()

    for h in range(head_share):
        home(h).wait()
        for offset in near_first:
            back_in(offset, h).wait_recv()
    out_ref[...] = got_out[...]

    for which in range(3):
        for offset in range(1, tiles):
            piece_out(which, offset).wait_send()
    for h in range(head_share):
        for offset in range(1, tiles):
            back_out(offset, h).wait_send()
    for step in range(1, WIN):
        @pl.when((me < frames - 1) & (me >= step))
        def _():
            copies[step].wait_send()

    @pl.when(me < frames - 1)
    def _():
        for p in range(tiles):
            first_hop(p).wait_send()


def fused_attend(frames, tiles, use, gains, bits, q, k, v):
    head_share = gains.shape[0]
    tile_tok, channels = q.shape
    frame_tok = tile_tok * tiles
    share = channels // tiles
    flops = 4 * (WIN + 1) * frame_tok * frame_tok * share
    smem = pl.BlockSpec(memory_space=pltpu.SMEM)
    vmem = pl.BlockSpec(memory_space=pltpu.VMEM)
    return pl.pallas_call(
        functools.partial(fused_kernel, frames, tiles),
        out_shape=jax.ShapeDtypeStruct(q.shape, jnp.bfloat16),
        in_specs=[smem, smem, smem, vmem, vmem, vmem],
        out_specs=vmem,
        scratch_shapes=[
            pltpu.VMEM((2, frame_tok, share), jnp.bfloat16),
            pltpu.VMEM((frame_tok, share), jnp.bfloat16),
            pltpu.VMEM((WIN, 2, frame_tok, share), jnp.bfloat16),
            pltpu.VMEM((frame_tok, share), jnp.bfloat16),
            pltpu.VMEM((tile_tok, channels), jnp.bfloat16),
            pltpu.VMEM((frame_tok, frame_tok), jnp.int32),
            pltpu.VMEM((head_share, frame_tok, 1), jnp.float32),
            pltpu.VMEM((head_share, frame_tok, 1), jnp.float32),
            pltpu.VMEM((head_share, frame_tok, HD), jnp.float32),
            pltpu.SemaphoreType.DMA((4, tiles)),
            pltpu.SemaphoreType.DMA((4, tiles)),
            pltpu.SemaphoreType.DMA((4,)),
            pltpu.SemaphoreType.DMA((WIN,)),
            pltpu.SemaphoreType.DMA((WIN,)),
            pltpu.SemaphoreType.DMA((tiles,)),
            pltpu.SemaphoreType.DMA((tiles,)),
            pltpu.SemaphoreType.DMA((tiles, head_share)),
            pltpu.SemaphoreType.DMA((tiles, head_share)),
            pltpu.SemaphoreType.DMA((head_share,)),
        ],
        compiler_params=pltpu.CompilerParams(
            collective_id=0, has_side_effects=True, vmem_limit_bytes=56 * 1024 * 1024
        ),
        cost_estimate=pl.CostEstimate(
            flops=flops,
            transcendentals=(WIN + 1) * head_share * frame_tok * frame_tok,
            bytes_accessed=(WIN + 6) * 2 * frame_tok * share * 2,
        ),
    )(use, gains, bits, q, k, v)


def shards(queries, keys, values, step_index, frame_index, window_mask, history_mask, step_gain):
    tile_count = lax.axis_size("tile")
    frames = lax.axis_size("frame")
    tile_id = lax.axis_index("tile")
    group_id = lax.axis_index("frame")
    channels = queries.shape[-1]
    head_share = HEADS // tile_count
    tile_tok = queries.shape[2]
    frame_tok = tile_tok * tile_count
    picker = (jnp.arange(STEPS, dtype=jnp.int32) == step_index[0]).astype(jnp.float32)
    head_gains = jnp.dot(picker, step_gain, precision=lax.Precision.HIGHEST)
    my_gains = lax.dynamic_slice_in_dim(head_gains, tile_id * head_share, head_share)
    my_masks = lax.dynamic_slice_in_dim(window_mask, tile_id * head_share, head_share, axis=0)
    distance = jnp.arange(1, WIN + 1, dtype=jnp.int32)
    use = (
        (history_mask[0] == 1) & (distance <= frame_index[0]) & (group_id - distance >= 0)
    ).astype(jnp.int32)
    bits = jnp.sum(
        jnp.where(my_masks == 1, jnp.left_shift(1, jnp.arange(9, dtype=jnp.int32)), 0), axis=1
    ) | 16
    finished = fused_attend(
        frames, tile_count, use, my_gains, bits.astype(jnp.int32),
        queries[0, 0], keys[0, 0], values[0, 0],
    )
    return finished.reshape(1, 1, tile_tok, channels)


def solution(mesh):
    return jax.shard_map(
        shards,
        mesh=mesh,
        in_specs=(
            P("frame", "tile", None, None),
            P("frame", "tile", None, None),
            P("frame", "tile", None, None),
            P("frame"),
            P("frame"),
            P(),
            P("frame", None),
            P(),
        ),
        out_specs=P("frame", "tile", None, None),
        check_vma=False,
    )
```

```python
import functools
import math

import jax
import jax.numpy as jnp
from jax import lax
from jax.experimental import pallas as pl
from jax.experimental.pallas import tpu as pltpu
from jax.sharding import PartitionSpec as P

HEADS = 40
HD = 128
TH = 8
TW = 8
BLK = 4
WIN = 5
STEPS = 4
CHUNK = 128

NEG_BIG = -1e30
MESH_ID = pl.DeviceIdType.MESH


def block_place(positions, tile_count, tile_tok):
    tile_cols = min(tile_count, 4)
    tile_of = positions // tile_tok
    within = positions % tile_tok
    row = tile_of // tile_cols * TH + within // TW
    col = tile_of % tile_cols * TW + within % TW
    return row // BLK, col // BLK


def fused_kernel(frames, tiles, step_ref, fidx_ref, wm_ref, hm_ref, sg_ref, q_ref, k_ref, v_ref, out_ref,
                 own_kv, own_q, slots, fin, got_out, code_scr, m_scr, l_scr, acc_scr,
                 piece_send, piece_recv, local_sem, send_sem, recv_sem, hop_send, hop_recv):
    me = lax.axis_index("frame")
    tile = lax.axis_index("tile")
    right = lax.rem(me + 1, frames)
    left = lax.rem(me + frames - 1, frames)
    head_share = acc_scr.shape[0]
    frame_tok = own_q.shape[0]
    share = own_q.shape[1]
    tile_tok = q_ref.shape[0]
    scale = 1.0 / math.sqrt(HD)

    def head_bits(h):
        row = tile * head_share + h
        bits = 16
        for offset in range(9):
            bits = bits | jnp.where(wm_ref[row, offset] == 1, 1 << offset, 0)
        return bits

    def usable(distance):
        return (hm_ref[0, distance - 1] == 1) & (distance <= fidx_ref[0]) & (me >= distance)

    def head_gain(h):
        return sg_ref[step_ref[0], tile * head_share + h]

    barrier = pltpu.get_barrier_semaphore()
    for other in (left, right):
        pl.semaphore_signal(barrier, inc=1, device_id=(other, tile), device_id_type=MESH_ID)
    for offset in range(1, tiles):
        peer = lax.rem(tile + offset, tiles)
        pl.semaphore_signal(barrier, inc=1, device_id=(me, peer), device_id_type=MESH_ID)
    pl.semaphore_wait(barrier, 2 + tiles - 1)

    def channels_of(p):
        return pl.ds(pl.multiple_of(p * share, 128), share)

    def tokens_of(p):
        return pl.ds(pl.multiple_of(p * tile_tok, tile_tok), tile_tok)

    sources = [k_ref, v_ref, q_ref]
    targets = [lambda rows: own_kv.at[0, rows, :], lambda rows: own_kv.at[1, rows, :],
               lambda rows: own_q.at[rows, :]]

    def piece_out(which, offset):
        peer = lax.rem(tile + offset, tiles)
        return pltpu.make_async_remote_copy(
            src_ref=sources[which].at[:, channels_of(peer)],
            dst_ref=targets[which](tokens_of(tile)),
            send_sem=piece_send.at[which, offset],
            recv_sem=piece_recv.at[which, tile],
            device_id=(me, peer),
            device_id_type=MESH_ID,
        )

    def piece_in(which, offset):
        sender = lax.rem(tile + tiles - offset, tiles)
        return pltpu.make_async_remote_copy(
            src_ref=sources[which].at[:, channels_of(tile)],
            dst_ref=targets[which](tokens_of(sender)),
            send_sem=piece_send.at[which, offset],
            recv_sem=piece_recv.at[which, sender],
            device_id=(me, sender),
            device_id_type=MESH_ID,
        )

    locals_ = [
        pltpu.make_async_copy(
            sources[which].at[:, channels_of(tile)], targets[which](tokens_of(tile)),
            local_sem.at[which],
        )
        for which in range(3)
    ]
    far_first = [j for j in range(1, tiles) if j % 2] + [j for j in range(1, tiles) if j % 2 == 0]
    near_first = far_first[::-1]
    for which in range(3):
        locals_[which].start()
        for offset in far_first:
            piece_out(which, offset).start()

    for c in range(frame_tok // CHUNK):
        query_pos = c * CHUNK + lax.broadcasted_iota(jnp.int32, (CHUNK, frame_tok), 0)
        key_pos = lax.broadcasted_iota(jnp.int32, (CHUNK, frame_tok), 1)
        query_row, query_col = block_place(query_pos, tiles, tile_tok)
        key_row, key_col = block_place(key_pos, tiles, tile_tok)
        row_step = key_row - query_row
        across = key_col - query_col
        nearby = (row_step >= -1) & (row_step <= 1) & (across >= -1) & (across <= 1)
        code_scr[pl.ds(c * CHUNK, CHUNK), :] = jnp.where(nearby, (row_step + 1) * 3 + across + 1, 15)

    def first_hop(p):
        return pltpu.make_async_remote_copy(
            src_ref=own_kv.at[:, tokens_of(p), :],
            dst_ref=slots.at[0, :, tokens_of(p), :],
            send_sem=hop_send.at[p],
            recv_sem=hop_recv.at[p],
            device_id=(right, tile),
            device_id_type=MESH_ID,
        )

    for which in range(2):
        locals_[which].wait()

    @pl.when(me < frames - 1)
    def _():
        first_hop(tile).start()

    for offset in near_first:
        for which in range(2):
            piece_in(which, offset).wait_recv()

        @pl.when(me < frames - 1)
        def _():
            first_hop(lax.rem(tile + tiles - offset, tiles)).start()

    def copy_for(step):
        source = own_kv if step == 0 else slots.at[step - 1]
        return pltpu.make_async_remote_copy(
            src_ref=source,
            dst_ref=slots.at[step],
            send_sem=send_sem.at[step],
            recv_sem=recv_sem.at[step],
            device_id=(right, tile),
            device_id_type=MESH_ID,
        )

    copies = [None] + [copy_for(step) for step in range(1, WIN)]

    m_scr[...] = jnp.full(m_scr.shape, NEG_BIG, jnp.float32)
    l_scr[...] = jnp.zeros(l_scr.shape, jnp.float32)
    acc_scr[...] = jnp.zeros(acc_scr.shape, jnp.float32)

    locals_[2].wait()
    for offset in range(1, tiles):
        piece_in(2, offset).wait_recv()

    def attend(block, use):
        def head_body(h, carry):
            col = pl.multiple_of(h * HD, HD)
            key_h = block[0, :, pl.ds(col, HD)]
            value_h = block[1, :, pl.ds(col, HD)]
            for c in range(frame_tok // CHUNK):
                rows = pl.ds(c * CHUNK, CHUNK)
                query_h = own_q[rows, pl.ds(col, HD)]
                scores = lax.dot_general(
                    query_h, key_h, (((1,), (1,)), ((), ())),
                    preferred_element_type=jnp.float32,
                ) * scale
                if use is None:
                    code = code_scr[rows, :]
                    shifted = lax.shift_right_logical(jnp.broadcast_to(head_bits(h), code.shape), code)
                    scores = jnp.where((shifted & 1) == 1, scores, NEG_BIG)
                else:
                    scores = scores + jnp.where(use, 0.0, NEG_BIG)
                old_max = m_scr[h, rows, :]
                new_max = jnp.maximum(old_max, jnp.max(scores, axis=1, keepdims=True))
                weights = jnp.exp(scores - new_max)
                factor = jnp.exp(old_max - new_max)
                l_scr[h, rows, :] = l_scr[h, rows, :] * factor + jnp.sum(weights, axis=1, keepdims=True)
                acc_scr[h, rows, :] = acc_scr[h, rows, :] * factor + jnp.dot(
                    weights.astype(jnp.bfloat16), value_h, preferred_element_type=jnp.float32
                )
                m_scr[h, rows, :] = new_max
            return carry

        lax.fori_loop(0, head_share, head_body, 0)

    attend(own_kv, None)
    for step in range(1, WIN + 1):
        @pl.when(me >= step)
        def _():
            if step == 1:
                for p in range(tiles):
                    first_hop(p).wait_recv()
            else:
                copies[step - 1].wait_recv()
            if step < WIN:
                @pl.when(me < frames - 1)
                def _():
                    copies[step].start()
            attend(slots.at[step - 1], usable(step))

    def finish(h, carry):
        col = pl.multiple_of(h * HD, HD)
        fin[:, pl.ds(col, HD)] = (acc_scr[h] / l_scr[h] * head_gain(h)).astype(fin.dtype)
        return carry

    lax.fori_loop(0, head_share, finish, 0)

    def back_out(offset):
        peer = lax.rem(tile + offset, tiles)
        return pltpu.make_async_remote_copy(
            src_ref=fin.at[tokens_of(peer), :],
            dst_ref=got_out.at[:, channels_of(tile)],
            send_sem=piece_send.at[3, offset],
            recv_sem=piece_recv.at[3, tile],
            device_id=(me, peer),
            device_id_type=MESH_ID,
        )

    def back_in(offset):
        sender = lax.rem(tile + tiles - offset, tiles)
        return pltpu.make_async_remote_copy(
            src_ref=fin.at[tokens_of(tile), :],
            dst_ref=got_out.at[:, channels_of(sender)],
            send_sem=piece_send.at[3, offset],
            recv_sem=piece_recv.at[3, sender],
            device_id=(me, sender),
            device_id_type=MESH_ID,
        )

    home = pltpu.make_async_copy(fin.at[tokens_of(tile), :], got_out.at[:, channels_of(tile)],
                                 local_sem.at[3])
    home.start()
    for offset in range(1, tiles):
        back_out(offset).start()
    home.wait()
    for offset in range(1, tiles):
        back_in(offset).wait_recv()
    out_ref[...] = got_out[...]

    for which in range(3):
        for offset in range(1, tiles):
            piece_out(which, offset).wait_send()
    for offset in range(1, tiles):
        back_out(offset).wait_send()
    for step in range(1, WIN):
        @pl.when((me < frames - 1) & (me >= step))
        def _():
            copies[step].wait_send()

    @pl.when(me < frames - 1)
    def _():
        for p in range(tiles):
            first_hop(p).wait_send()


def fused_attend(frames, tiles, scalars, q, k, v):
    head_share = HEADS // tiles
    tile_tok, channels = q.shape
    frame_tok = tile_tok * tiles
    share = channels // tiles
    flops = 4 * (WIN + 1) * frame_tok * frame_tok * share
    smem = pl.BlockSpec(memory_space=pltpu.SMEM)
    vmem = pl.BlockSpec(memory_space=pltpu.VMEM)
    hbm = pl.BlockSpec(memory_space=pl.ANY)
    return pl.pallas_call(
        functools.partial(fused_kernel, frames, tiles),
        out_shape=jax.ShapeDtypeStruct(q.shape, jnp.bfloat16),
        in_specs=[smem] * len(scalars) + [hbm] * 3,
        out_specs=vmem,
        scratch_shapes=[
            pltpu.VMEM((2, frame_tok, share), jnp.bfloat16),
            pltpu.VMEM((frame_tok, share), jnp.bfloat16),
            pltpu.VMEM((WIN, 2, frame_tok, share), jnp.bfloat16),
            pltpu.VMEM((frame_tok, share), jnp.bfloat16),
            pltpu.VMEM((tile_tok, channels), jnp.bfloat16),
            pltpu.VMEM((frame_tok, frame_tok), jnp.int32),
            pltpu.VMEM((head_share, frame_tok, 1), jnp.float32),
            pltpu.VMEM((head_share, frame_tok, 1), jnp.float32),
            pltpu.VMEM((head_share, frame_tok, HD), jnp.float32),
            pltpu.SemaphoreType.DMA((4, tiles)),
            pltpu.SemaphoreType.DMA((4, tiles)),
            pltpu.SemaphoreType.DMA((4,)),
            pltpu.SemaphoreType.DMA((WIN,)),
            pltpu.SemaphoreType.DMA((WIN,)),
            pltpu.SemaphoreType.DMA((tiles,)),
            pltpu.SemaphoreType.DMA((tiles,)),
        ],
        compiler_params=pltpu.CompilerParams(
            collective_id=0, has_side_effects=True, vmem_limit_bytes=56 * 1024 * 1024
        ),
        cost_estimate=pl.CostEstimate(
            flops=flops,
            transcendentals=(WIN + 1) * head_share * frame_tok * frame_tok,
            bytes_accessed=(WIN + 6) * 2 * frame_tok * share * 2,
        ),
    )(*scalars, q, k, v)


def shards(queries, keys, values, step_index, frame_index, window_mask, history_mask, step_gain):
    tile_count = lax.axis_size("tile")
    frames = lax.axis_size("frame")
    tile_id = lax.axis_index("tile")
    group_id = lax.axis_index("frame")
    channels = queries.shape[-1]
    head_share = HEADS // tile_count
    tile_tok = queries.shape[2]
    frame_tok = tile_tok * tile_count
    finished = fused_attend(
        frames, tile_count, (step_index, frame_index, window_mask, history_mask, step_gain),
        queries[0, 0], keys[0, 0], values[0, 0],
    )
    return finished.reshape(1, 1, tile_tok, channels)


def solution(mesh):
    return jax.shard_map(
        shards,
        mesh=mesh,
        in_specs=(
            P("frame", "tile", None, None),
            P("frame", "tile", None, None),
            P("frame", "tile", None, None),
            P("frame"),
            P("frame"),
            P(),
            P("frame", None),
            P(),
        ),
        out_specs=P("frame", "tile", None, None),
        check_vma=False,
    )
```

```python
import functools
import math

import jax
import jax.numpy as jnp
from jax import lax
from jax.experimental import pallas as pl
from jax.experimental.pallas import tpu as pltpu
from jax.sharding import PartitionSpec as P

HEADS = 40
HD = 128
TH = 8
TW = 8
BLK = 4
WIN = 5
STEPS = 4
CHUNK = 128
GROUP = 8

NEG_BIG = -1e30
MESH_ID = pl.DeviceIdType.MESH


def block_place(positions, tile_count, tile_tok):
    tile_cols = min(tile_count, 4)
    tile_of = positions // tile_tok
    within = positions % tile_tok
    row = tile_of // tile_cols * TH + within // TW
    col = tile_of % tile_cols * TW + within % TW
    return row // BLK, col // BLK


def fused_kernel(frames, tiles, step_ref, fidx_ref, wm_ref, hm_ref, sg_ref, q_ref, k_ref, v_ref, out_ref,
                 own_kv, own_q, slots, fin, got_out, code_scr, m_scr, l_scr, acc_scr,
                 piece_send, piece_recv, local_sem, send_sem, recv_sem, hop_send, hop_recv,
                 direct_send, direct_recv):
    me = lax.axis_index("frame")
    tile = lax.axis_index("tile")
    right = lax.rem(me + 1, frames)
    left = lax.rem(me + frames - 1, frames)
    head_share = acc_scr.shape[0]
    frame_tok = own_q.shape[0]
    share = own_q.shape[1]
    tile_tok = q_ref.shape[0]
    scale = 1.0 / math.sqrt(HD)

    def head_bits(h):
        row = tile * head_share + h
        bits = 16
        for offset in range(9):
            bits = bits | jnp.where(wm_ref[row, offset] == 1, 1 << offset, 0)
        return bits

    def usable(distance):
        return (hm_ref[0, distance - 1] == 1) & (distance <= fidx_ref[0]) & (me >= distance)

    def head_gain(h):
        return sg_ref[step_ref[0], tile * head_share + h]

    barrier = pltpu.get_barrier_semaphore()
    for distance in range(1, WIN + 1):
        for other in (lax.rem(me + frames - distance, frames), lax.rem(me + distance, frames)):
            pl.semaphore_signal(barrier, inc=1, device_id=(other, tile), device_id_type=MESH_ID)
    for offset in range(1, tiles):
        peer = lax.rem(tile + offset, tiles)
        pl.semaphore_signal(barrier, inc=1, device_id=(me, peer), device_id_type=MESH_ID)
    pl.semaphore_wait(barrier, 2 * WIN + tiles - 1)

    def channels_of(p):
        return pl.ds(pl.multiple_of(p * share, 128), share)

    def tokens_of(p):
        return pl.ds(pl.multiple_of(p * tile_tok, tile_tok), tile_tok)

    sources = [k_ref, v_ref, q_ref]
    targets = [lambda rows: own_kv.at[0, rows, :], lambda rows: own_kv.at[1, rows, :],
               lambda rows: own_q.at[rows, :]]

    def piece_out(which, offset):
        peer = lax.rem(tile + offset, tiles)
        return pltpu.make_async_remote_copy(
            src_ref=sources[which].at[:, channels_of(peer)],
            dst_ref=targets[which](tokens_of(tile)),
            send_sem=piece_send.at[which, offset],
            recv_sem=piece_recv.at[which, tile],
            device_id=(me, peer),
            device_id_type=MESH_ID,
        )

    def piece_in(which, offset):
        sender = lax.rem(tile + tiles - offset, tiles)
        return pltpu.make_async_remote_copy(
            src_ref=sources[which].at[:, channels_of(tile)],
            dst_ref=targets[which](tokens_of(sender)),
            send_sem=piece_send.at[which, offset],
            recv_sem=piece_recv.at[which, sender],
            device_id=(me, sender),
            device_id_type=MESH_ID,
        )

    locals_ = [
        pltpu.make_async_copy(
            sources[which].at[:, channels_of(tile)], targets[which](tokens_of(tile)),
            local_sem.at[which],
        )
        for which in range(3)
    ]
    far_first = [j for j in range(1, tiles) if j % 2] + [j for j in range(1, tiles) if j % 2 == 0]
    near_first = far_first[::-1]
    for which in range(3):
        locals_[which].start()
        for offset in far_first:
            piece_out(which, offset).start()

    for c in range(frame_tok // CHUNK):
        query_pos = c * CHUNK + lax.broadcasted_iota(jnp.int32, (CHUNK, frame_tok), 0)
        key_pos = lax.broadcasted_iota(jnp.int32, (CHUNK, frame_tok), 1)
        query_row, query_col = block_place(query_pos, tiles, tile_tok)
        key_row, key_col = block_place(key_pos, tiles, tile_tok)
        row_step = key_row - query_row
        across = key_col - query_col
        nearby = (row_step >= -1) & (row_step <= 1) & (across >= -1) & (across <= 1)
        code_scr[pl.ds(c * CHUNK, CHUNK), :] = jnp.where(nearby, (row_step + 1) * 3 + across + 1, 15)

    def first_hop(p):
        return pltpu.make_async_remote_copy(
            src_ref=own_kv.at[:, tokens_of(p), :],
            dst_ref=slots.at[0, :, tokens_of(p), :],
            send_sem=hop_send.at[p],
            recv_sem=hop_recv.at[p],
            device_id=(right, tile),
            device_id_type=MESH_ID,
        )

    for which in range(2):
        locals_[which].wait()

    @pl.when(me < frames - 1)
    def _():
        first_hop(tile).start()

    for offset in near_first:
        for which in range(2):
            piece_in(which, offset).wait_recv()

        @pl.when(me < frames - 1)
        def _():
            first_hop(lax.rem(tile + tiles - offset, tiles)).start()

    def copy_for(step):
        source = own_kv if step == 0 else slots.at[step - 1]
        return pltpu.make_async_remote_copy(
            src_ref=source,
            dst_ref=slots.at[step],
            send_sem=send_sem.at[step],
            recv_sem=recv_sem.at[step],
            device_id=(right, tile),
            device_id_type=MESH_ID,
        )

    copies = [None] + [copy_for(step) for step in range(1, WIN)]

    position = lax.rem(me, GROUP)
    group_start = (position == 0) & (me >= GROUP)
    before_start = position == GROUP - 1

    def direct(distance):
        return pltpu.make_async_remote_copy(
            src_ref=own_kv,
            dst_ref=slots.at[distance - 1],
            send_sem=direct_send.at[distance - 1],
            recv_sem=direct_recv.at[distance - 1],
            device_id=(lax.rem(me + distance, frames), tile),
            device_id_type=MESH_ID,
        )

    def direct_sender(distance):
        return (position == GROUP - distance) & (me + distance < frames)

    for distance in range(2, WIN + 1):
        @pl.when(direct_sender(distance))
        def _():
            direct(distance).start()

    m_scr[...] = jnp.full(m_scr.shape, NEG_BIG, jnp.float32)
    l_scr[...] = jnp.zeros(l_scr.shape, jnp.float32)
    acc_scr[...] = jnp.zeros(acc_scr.shape, jnp.float32)

    locals_[2].wait()
    for offset in range(1, tiles):
        piece_in(2, offset).wait_recv()

    def attend(block, use):
        def head_body(h, carry):
            col = pl.multiple_of(h * HD, HD)
            key_h = block[0, :, pl.ds(col, HD)]
            value_h = block[1, :, pl.ds(col, HD)]
            for c in range(frame_tok // CHUNK):
                rows = pl.ds(c * CHUNK, CHUNK)
                query_h = own_q[rows, pl.ds(col, HD)]
                scores = lax.dot_general(
                    query_h, key_h, (((1,), (1,)), ((), ())),
                    preferred_element_type=jnp.float32,
                ) * scale
                if use is None:
                    code = code_scr[rows, :]
                    shifted = lax.shift_right_logical(jnp.broadcast_to(head_bits(h), code.shape), code)
                    scores = jnp.where((shifted & 1) == 1, scores, NEG_BIG)
                else:
                    scores = scores + jnp.where(use, 0.0, NEG_BIG)
                old_max = m_scr[h, rows, :]
                new_max = jnp.maximum(old_max, jnp.max(scores, axis=1, keepdims=True))
                weights = jnp.exp(scores - new_max)
                factor = jnp.exp(old_max - new_max)
                l_scr[h, rows, :] = l_scr[h, rows, :] * factor + jnp.sum(weights, axis=1, keepdims=True)
                acc_scr[h, rows, :] = acc_scr[h, rows, :] * factor + jnp.dot(
                    weights.astype(jnp.bfloat16), value_h, preferred_element_type=jnp.float32
                )
                m_scr[h, rows, :] = new_max
            return carry

        lax.fori_loop(0, head_share, head_body, 0)

    attend(own_kv, None)
    for step in range(1, WIN + 1):
        @pl.when(me >= step)
        def _():
            if step == 1:
                for p in range(tiles):
                    first_hop(p).wait_recv()
            else:
                @pl.when(group_start)
                def _():
                    direct(step).wait_recv()

                @pl.when(jnp.logical_not(group_start))
                def _():
                    copies[step - 1].wait_recv()
            if step < WIN:
                @pl.when((me < frames - 1) & jnp.logical_not(before_start))
                def _():
                    copies[step].start()
            attend(slots.at[step - 1], usable(step))

    def finish(h, carry):
        col = pl.multiple_of(h * HD, HD)
        fin[:, pl.ds(col, HD)] = (acc_scr[h] / l_scr[h] * head_gain(h)).astype(fin.dtype)
        return carry

    lax.fori_loop(0, head_share, finish, 0)

    def back_out(offset):
        peer = lax.rem(tile + offset, tiles)
        return pltpu.make_async_remote_copy(
            src_ref=fin.at[tokens_of(peer), :],
            dst_ref=got_out.at[:, channels_of(tile)],
            send_sem=piece_send.at[3, offset],
            recv_sem=piece_recv.at[3, tile],
            device_id=(me, peer),
            device_id_type=MESH_ID,
        )

    def back_in(offset):
        sender = lax.rem(tile + tiles - offset, tiles)
        return pltpu.make_async_remote_copy(
            src_ref=fin.at[tokens_of(tile), :],
            dst_ref=got_out.at[:, channels_of(sender)],
            send_sem=piece_send.at[3, offset],
            recv_sem=piece_recv.at[3, sender],
            device_id=(me, sender),
            device_id_type=MESH_ID,
        )

    home = pltpu.make_async_copy(fin.at[tokens_of(tile), :], got_out.at[:, channels_of(tile)],
                                 local_sem.at[3])
    home.start()
    for offset in range(1, tiles):
        back_out(offset).start()
    home.wait()
    for offset in range(1, tiles):
        back_in(offset).wait_recv()
    out_ref[...] = got_out[...]

    for which in range(3):
        for offset in range(1, tiles):
            piece_out(which, offset).wait_send()
    for offset in range(1, tiles):
        back_out(offset).wait_send()
    for step in range(1, WIN):
        @pl.when((me < frames - 1) & (me >= step) & jnp.logical_not(before_start))
        def _():
            copies[step].wait_send()

    for distance in range(2, WIN + 1):
        @pl.when(direct_sender(distance))
        def _():
            direct(distance).wait_send()

    @pl.when(me < frames - 1)
    def _():
        for p in range(tiles):
            first_hop(p).wait_send()


def fused_attend(frames, tiles, scalars, q, k, v):
    head_share = HEADS // tiles
    tile_tok, channels = q.shape
    frame_tok = tile_tok * tiles
    share = channels // tiles
    flops = 4 * (WIN + 1) * frame_tok * frame_tok * share
    smem = pl.BlockSpec(memory_space=pltpu.SMEM)
    vmem = pl.BlockSpec(memory_space=pltpu.VMEM)
    hbm = pl.BlockSpec(memory_space=pl.ANY)
    return pl.pallas_call(
        functools.partial(fused_kernel, frames, tiles),
        out_shape=jax.ShapeDtypeStruct(q.shape, jnp.bfloat16),
        in_specs=[smem] * len(scalars) + [hbm] * 3,
        out_specs=vmem,
        scratch_shapes=[
            pltpu.VMEM((2, frame_tok, share), jnp.bfloat16),
            pltpu.VMEM((frame_tok, share), jnp.bfloat16),
            pltpu.VMEM((WIN, 2, frame_tok, share), jnp.bfloat16),
            pltpu.VMEM((frame_tok, share), jnp.bfloat16),
            pltpu.VMEM((tile_tok, channels), jnp.bfloat16),
            pltpu.VMEM((frame_tok, frame_tok), jnp.int32),
            pltpu.VMEM((head_share, frame_tok, 1), jnp.float32),
            pltpu.VMEM((head_share, frame_tok, 1), jnp.float32),
            pltpu.VMEM((head_share, frame_tok, HD), jnp.float32),
            pltpu.SemaphoreType.DMA((4, tiles)),
            pltpu.SemaphoreType.DMA((4, tiles)),
            pltpu.SemaphoreType.DMA((4,)),
            pltpu.SemaphoreType.DMA((WIN,)),
            pltpu.SemaphoreType.DMA((WIN,)),
            pltpu.SemaphoreType.DMA((tiles,)),
            pltpu.SemaphoreType.DMA((tiles,)),
            pltpu.SemaphoreType.DMA((WIN,)),
            pltpu.SemaphoreType.DMA((WIN,)),
        ],
        compiler_params=pltpu.CompilerParams(
            collective_id=0, has_side_effects=True, vmem_limit_bytes=56 * 1024 * 1024
        ),
        cost_estimate=pl.CostEstimate(
            flops=flops,
            transcendentals=(WIN + 1) * head_share * frame_tok * frame_tok,
            bytes_accessed=(WIN + 6) * 2 * frame_tok * share * 2,
        ),
    )(*scalars, q, k, v)


def shards(queries, keys, values, step_index, frame_index, window_mask, history_mask, step_gain):
    tile_count = lax.axis_size("tile")
    frames = lax.axis_size("frame")
    tile_id = lax.axis_index("tile")
    group_id = lax.axis_index("frame")
    channels = queries.shape[-1]
    head_share = HEADS // tile_count
    tile_tok = queries.shape[2]
    frame_tok = tile_tok * tile_count
    finished = fused_attend(
        frames, tile_count, (step_index, frame_index, window_mask, history_mask, step_gain),
        queries[0, 0], keys[0, 0], values[0, 0],
    )
    return finished.reshape(1, 1, tile_tok, channels)


def solution(mesh):
    return jax.shard_map(
        shards,
        mesh=mesh,
        in_specs=(
            P("frame", "tile", None, None),
            P("frame", "tile", None, None),
            P("frame", "tile", None, None),
            P("frame"),
            P("frame"),
            P(),
            P("frame", None),
            P(),
        ),
        out_specs=P("frame", "tile", None, None),
        check_vma=False,
    )
```

```python
import functools
import math

import jax
import jax.numpy as jnp
from jax import lax
from jax.experimental import pallas as pl
from jax.experimental.pallas import tpu as pltpu
from jax.sharding import PartitionSpec as P

HEADS = 40
HD = 128
TH = 8
TW = 8
BLK = 4
WIN = 5
STEPS = 4
CHUNK = 128

NEG_BIG = -1e30
MESH_ID = pl.DeviceIdType.MESH


def block_place(positions, tile_count, tile_tok):
    tile_cols = min(tile_count, 4)
    tile_of = positions // tile_tok
    within = positions % tile_tok
    row = tile_of // tile_cols * TH + within // TW
    col = tile_of % tile_cols * TW + within % TW
    return row // BLK, col // BLK


def fused_kernel(frames, tiles, step_ref, fidx_ref, wm_ref, hm_ref, sg_ref, q_ref, k_ref, v_ref, out_ref,
                 own_kv, own_q, slots, fin, got_out, code_scr, m_scr, l_scr, acc_scr,
                 piece_send, piece_recv, local_sem, send_sem, recv_sem, hop_send, hop_recv):
    me = lax.axis_index("frame")
    tile = lax.axis_index("tile")
    right = lax.rem(me + 1, frames)
    left = lax.rem(me + frames - 1, frames)
    head_share = acc_scr.shape[0]
    frame_tok = own_q.shape[0]
    share = own_q.shape[1]
    tile_tok = q_ref.shape[0]
    scale = 1.0 / math.sqrt(HD)

    def head_bits(h):
        row = tile * head_share + h
        bits = 16
        for offset in range(9):
            bits = bits | jnp.where(wm_ref[row, offset] == 1, 1 << offset, 0)
        return bits

    def usable(distance):
        return (hm_ref[0, distance - 1] == 1) & (distance <= fidx_ref[0]) & (me >= distance)

    def head_gain(h):
        return sg_ref[step_ref[0], tile * head_share + h]

    barrier = pltpu.get_barrier_semaphore()
    for other in (left, right):
        pl.semaphore_signal(barrier, inc=1, device_id=(other, tile), device_id_type=MESH_ID)
    for offset in range(1, tiles):
        peer = lax.rem(tile + offset, tiles)
        pl.semaphore_signal(barrier, inc=1, device_id=(me, peer), device_id_type=MESH_ID)
    pl.semaphore_wait(barrier, 2 + tiles - 1)

    def channels_of(p):
        return pl.ds(pl.multiple_of(p * share, 128), share)

    def tokens_of(p):
        return pl.ds(pl.multiple_of(p * tile_tok, tile_tok), tile_tok)

    sources = [k_ref, v_ref, q_ref]
    targets = [lambda rows: own_kv.at[0, rows, :], lambda rows: own_kv.at[1, rows, :],
               lambda rows: own_q.at[rows, :]]

    def piece_out(which, offset):
        peer = lax.rem(tile + offset, tiles)
        return pltpu.make_async_remote_copy(
            src_ref=sources[which].at[:, channels_of(peer)],
            dst_ref=targets[which](tokens_of(tile)),
            send_sem=piece_send.at[which, offset],
            recv_sem=piece_recv.at[which, tile],
            device_id=(me, peer),
            device_id_type=MESH_ID,
        )

    def piece_in(which, offset):
        sender = lax.rem(tile + tiles - offset, tiles)
        return pltpu.make_async_remote_copy(
            src_ref=sources[which].at[:, channels_of(tile)],
            dst_ref=targets[which](tokens_of(sender)),
            send_sem=piece_send.at[which, offset],
            recv_sem=piece_recv.at[which, sender],
            device_id=(me, sender),
            device_id_type=MESH_ID,
        )

    locals_ = [
        pltpu.make_async_copy(
            sources[which].at[:, channels_of(tile)], targets[which](tokens_of(tile)),
            local_sem.at[which],
        )
        for which in range(3)
    ]
    far_first = [j for j in range(1, tiles) if j % 2] + [j for j in range(1, tiles) if j % 2 == 0]
    near_first = far_first[::-1]
    for which in range(3):
        locals_[which].start()
        for offset in far_first:
            piece_out(which, offset).start()

    for c in range(frame_tok // CHUNK):
        query_pos = c * CHUNK + lax.broadcasted_iota(jnp.int32, (CHUNK, frame_tok), 0)
        key_pos = lax.broadcasted_iota(jnp.int32, (CHUNK, frame_tok), 1)
        query_row, query_col = block_place(query_pos, tiles, tile_tok)
        key_row, key_col = block_place(key_pos, tiles, tile_tok)
        row_step = key_row - query_row
        across = key_col - query_col
        nearby = (row_step >= -1) & (row_step <= 1) & (across >= -1) & (across <= 1)
        code_scr[pl.ds(c * CHUNK, CHUNK), :] = jnp.where(nearby, (row_step + 1) * 3 + across + 1, 15)

    def first_hop(p):
        return pltpu.make_async_remote_copy(
            src_ref=own_kv.at[:, tokens_of(p), :],
            dst_ref=slots.at[0, :, tokens_of(p), :],
            send_sem=hop_send.at[p],
            recv_sem=hop_recv.at[p],
            device_id=(right, tile),
            device_id_type=MESH_ID,
        )

    for which in range(2):
        locals_[which].wait()

    @pl.when(me < frames - 1)
    def _():
        first_hop(tile).start()

    for offset in near_first:
        for which in range(2):
            piece_in(which, offset).wait_recv()

        @pl.when(me < frames - 1)
        def _():
            first_hop(lax.rem(tile + tiles - offset, tiles)).start()

    def copy_for(step):
        source = own_kv if step == 0 else slots.at[step - 1]
        return pltpu.make_async_remote_copy(
            src_ref=source,
            dst_ref=slots.at[step],
            send_sem=send_sem.at[step],
            recv_sem=recv_sem.at[step],
            device_id=(right, tile),
            device_id_type=MESH_ID,
        )

    copies = [None] + [copy_for(step) for step in range(1, WIN)]

    m_scr[...] = jnp.full(m_scr.shape, NEG_BIG, jnp.float32)
    l_scr[...] = jnp.zeros(l_scr.shape, jnp.float32)
    acc_scr[...] = jnp.zeros(acc_scr.shape, jnp.float32)

    locals_[2].wait()
    for offset in range(1, tiles):
        piece_in(2, offset).wait_recv()

    def attend(block, use):
        def head_body(h, carry):
            col = pl.multiple_of(h * HD, HD)
            key_h = block[0, :, pl.ds(col, HD)]
            value_h = block[1, :, pl.ds(col, HD)]
            for c in range(frame_tok // CHUNK):
                rows = pl.ds(c * CHUNK, CHUNK)
                query_h = own_q[rows, pl.ds(col, HD)]
                scores = lax.dot_general(
                    query_h, key_h, (((1,), (1,)), ((), ())),
                    preferred_element_type=jnp.float32,
                ) * scale
                if use is None:
                    code = code_scr[rows, :]
                    shifted = lax.shift_right_logical(jnp.broadcast_to(head_bits(h), code.shape), code)
                    scores = jnp.where((shifted & 1) == 1, scores, NEG_BIG)
                else:
                    scores = scores + jnp.where(use, 0.0, NEG_BIG)
                old_max = m_scr[h, rows, :]
                new_max = jnp.maximum(old_max, jnp.max(scores, axis=1, keepdims=True))
                weights = jnp.exp(scores - new_max)
                factor = jnp.exp(old_max - new_max)
                l_scr[h, rows, :] = l_scr[h, rows, :] * factor + jnp.sum(weights, axis=1, keepdims=True)
                acc_scr[h, rows, :] = acc_scr[h, rows, :] * factor + jnp.dot(
                    weights.astype(jnp.bfloat16), value_h, preferred_element_type=jnp.float32
                )
                m_scr[h, rows, :] = new_max
            return carry

        lax.fori_loop(0, head_share, head_body, 0)

    attend(own_kv, None)
    for step in range(1, WIN + 1):
        @pl.when(me >= step)
        def _():
            if step == 1:
                for p in range(tiles):
                    first_hop(p).wait_recv()
            else:
                copies[step - 1].wait_recv()
            if step < WIN:
                @pl.when(me < frames - 1)
                def _():
                    copies[step].start()
            attend(slots.at[step - 1], usable(step))

    def finish(h, carry):
        col = pl.multiple_of(h * HD, HD)
        fin[:, pl.ds(col, HD)] = (acc_scr[h] / l_scr[h] * head_gain(h)).astype(fin.dtype)
        return carry

    lax.fori_loop(0, head_share, finish, 0)

    def back_out(offset):
        peer = lax.rem(tile + offset, tiles)
        return pltpu.make_async_remote_copy(
            src_ref=fin.at[tokens_of(peer), :],
            dst_ref=got_out.at[:, channels_of(tile)],
            send_sem=piece_send.at[3, offset],
            recv_sem=piece_recv.at[3, tile],
            device_id=(me, peer),
            device_id_type=MESH_ID,
        )

    def back_in(offset):
        sender = lax.rem(tile + tiles - offset, tiles)
        return pltpu.make_async_remote_copy(
            src_ref=fin.at[tokens_of(tile), :],
            dst_ref=got_out.at[:, channels_of(sender)],
            send_sem=piece_send.at[3, offset],
            recv_sem=piece_recv.at[3, sender],
            device_id=(me, sender),
            device_id_type=MESH_ID,
        )

    home = pltpu.make_async_copy(fin.at[tokens_of(tile), :], got_out.at[:, channels_of(tile)],
                                 local_sem.at[3])
    home.start()
    for offset in range(1, tiles):
        back_out(offset).start()
    home.wait()
    for offset in range(1, tiles):
        back_in(offset).wait_recv()
    out_ref[...] = got_out[...]

    for which in range(3):
        for offset in range(1, tiles):
            piece_out(which, offset).wait_send()
    for offset in range(1, tiles):
        back_out(offset).wait_send()
    for step in range(1, WIN):
        @pl.when((me < frames - 1) & (me >= step))
        def _():
            copies[step].wait_send()

    @pl.when(me < frames - 1)
    def _():
        for p in range(tiles):
            first_hop(p).wait_send()


def fused_attend(frames, tiles, scalars, q, k, v):
    head_share = HEADS // tiles
    tile_tok, channels = q.shape
    frame_tok = tile_tok * tiles
    share = channels // tiles
    flops = 4 * (WIN + 1) * frame_tok * frame_tok * share
    smem = pl.BlockSpec(memory_space=pltpu.SMEM)
    vmem = pl.BlockSpec(memory_space=pltpu.VMEM)
    hbm = pl.BlockSpec(memory_space=pl.ANY)
    return pl.pallas_call(
        functools.partial(fused_kernel, frames, tiles),
        out_shape=jax.ShapeDtypeStruct(q.shape, jnp.bfloat16),
        in_specs=[smem] * len(scalars) + [hbm] * 3,
        out_specs=vmem,
        scratch_shapes=[
            pltpu.VMEM((2, frame_tok, share), jnp.bfloat16),
            pltpu.VMEM((frame_tok, share), jnp.bfloat16),
            pltpu.VMEM((WIN, 2, frame_tok, share), jnp.bfloat16),
            pltpu.VMEM((frame_tok, share), jnp.bfloat16),
            pltpu.VMEM((tile_tok, channels), jnp.bfloat16),
            pltpu.VMEM((frame_tok, frame_tok), jnp.int32),
            pltpu.VMEM((head_share, frame_tok, 1), jnp.float32),
            pltpu.VMEM((head_share, frame_tok, 1), jnp.float32),
            pltpu.VMEM((head_share, frame_tok, HD), jnp.float32),
            pltpu.SemaphoreType.DMA((4, tiles)),
            pltpu.SemaphoreType.DMA((4, tiles)),
            pltpu.SemaphoreType.DMA((4,)),
            pltpu.SemaphoreType.DMA((WIN,)),
            pltpu.SemaphoreType.DMA((WIN,)),
            pltpu.SemaphoreType.DMA((tiles,)),
            pltpu.SemaphoreType.DMA((tiles,)),
        ],
        compiler_params=pltpu.CompilerParams(
            collective_id=0, has_side_effects=True, vmem_limit_bytes=56 * 1024 * 1024
        ),
        cost_estimate=pl.CostEstimate(
            flops=flops,
            transcendentals=(WIN + 1) * head_share * frame_tok * frame_tok,
            bytes_accessed=(WIN + 6) * 2 * frame_tok * share * 2,
        ),
    )(*scalars, q, k, v)


def hand_over_kernel(src_ref, dst_ref):
    dst_ref[...] = src_ref[...]


def hand_over(block):
    vmem = pl.BlockSpec(memory_space=pltpu.VMEM)
    return pl.pallas_call(
        hand_over_kernel,
        out_shape=jax.ShapeDtypeStruct(block.shape, block.dtype),
        in_specs=[vmem],
        out_specs=vmem,
        cost_estimate=pl.CostEstimate(flops=0, transcendentals=0, bytes_accessed=2 * block.size * 2),
    )(block)


def shards(queries, keys, values, step_index, frame_index, window_mask, history_mask, step_gain):
    tile_count = lax.axis_size("tile")
    frames = lax.axis_size("frame")
    tile_id = lax.axis_index("tile")
    group_id = lax.axis_index("frame")
    channels = queries.shape[-1]
    head_share = HEADS // tile_count
    tile_tok = queries.shape[2]
    frame_tok = tile_tok * tile_count
    finished = fused_attend(
        frames, tile_count, (step_index, frame_index, window_mask, history_mask, step_gain),
        queries[0, 0], keys[0, 0], values[0, 0],
    )
    return hand_over(finished).reshape(1, 1, tile_tok, channels)


def solution(mesh):
    return jax.shard_map(
        shards,
        mesh=mesh,
        in_specs=(
            P("frame", "tile", None, None),
            P("frame", "tile", None, None),
            P("frame", "tile", None, None),
            P("frame"),
            P("frame"),
            P(),
            P("frame", None),
            P(),
        ),
        out_specs=P("frame", "tile", None, None),
        check_vma=False,
    )
```

```python
import functools
import math

import jax
import jax.numpy as jnp
from jax import lax
from jax.experimental import pallas as pl
from jax.experimental.pallas import tpu as pltpu
from jax.sharding import PartitionSpec as P

HEADS = 40
HD = 128
TH = 8
TW = 8
BLK = 4
WIN = 5
STEPS = 4
CHUNK = 128

NEG_BIG = -1e30
MESH_ID = pl.DeviceIdType.MESH


def block_place(positions, tile_count, tile_tok):
    tile_cols = min(tile_count, 4)
    tile_of = positions // tile_tok
    within = positions % tile_tok
    row = tile_of // tile_cols * TH + within // TW
    col = tile_of % tile_cols * TW + within % TW
    return row // BLK, col // BLK


def fused_kernel(frames, tiles, step_ref, fidx_ref, wm_ref, hm_ref, sg_ref, q_ref, k_ref, v_ref, out_ref,
                 own_kv, own_q, slots, fin, got_out, code_scr, m_scr, l_scr, acc_scr,
                 piece_send, piece_recv, local_sem, send_sem, recv_sem, hop_send, hop_recv):
    me = lax.axis_index("frame")
    tile = lax.axis_index("tile")
    right = lax.rem(me + 1, frames)
    left = lax.rem(me + frames - 1, frames)
    head_share = acc_scr.shape[0]
    frame_tok = own_q.shape[0]
    share = own_q.shape[1]
    tile_tok = q_ref.shape[0]
    scale = 1.0 / math.sqrt(HD)

    def head_bits(h):
        row = tile * head_share + h
        bits = 16
        for offset in range(9):
            bits = bits | jnp.where(wm_ref[offset, row] == 1, 1 << offset, 0)
        return bits

    def usable(distance):
        return (hm_ref[0, distance - 1] == 1) & (distance <= fidx_ref[0]) & (me >= distance)

    def head_gain(h):
        return sg_ref[step_ref[0], tile * head_share + h]

    barrier = pltpu.get_barrier_semaphore()
    for other in (left, right):
        pl.semaphore_signal(barrier, inc=1, device_id=(other, tile), device_id_type=MESH_ID)
    for offset in range(1, tiles):
        peer = lax.rem(tile + offset, tiles)
        pl.semaphore_signal(barrier, inc=1, device_id=(me, peer), device_id_type=MESH_ID)
    pl.semaphore_wait(barrier, 2 + tiles - 1)

    def channels_of(p):
        return pl.ds(pl.multiple_of(p * share, 128), share)

    def tokens_of(p):
        return pl.ds(pl.multiple_of(p * tile_tok, tile_tok), tile_tok)

    sources = [k_ref, v_ref, q_ref]
    targets = [lambda rows: own_kv.at[0, rows, :], lambda rows: own_kv.at[1, rows, :],
               lambda rows: own_q.at[rows, :]]

    def piece_out(which, offset):
        peer = lax.rem(tile + offset, tiles)
        return pltpu.make_async_remote_copy(
            src_ref=sources[which].at[:, channels_of(peer)],
            dst_ref=targets[which](tokens_of(tile)),
            send_sem=piece_send.at[which, offset],
            recv_sem=piece_recv.at[which, tile],
            device_id=(me, peer),
            device_id_type=MESH_ID,
        )

    def piece_in(which, offset):
        sender = lax.rem(tile + tiles - offset, tiles)
        return pltpu.make_async_remote_copy(
            src_ref=sources[which].at[:, channels_of(tile)],
            dst_ref=targets[which](tokens_of(sender)),
            send_sem=piece_send.at[which, offset],
            recv_sem=piece_recv.at[which, sender],
            device_id=(me, sender),
            device_id_type=MESH_ID,
        )

    locals_ = [
        pltpu.make_async_copy(
            sources[which].at[:, channels_of(tile)], targets[which](tokens_of(tile)),
            local_sem.at[which],
        )
        for which in range(3)
    ]
    far_first = [j for j in range(1, tiles) if j % 2] + [j for j in range(1, tiles) if j % 2 == 0]
    near_first = far_first[::-1]
    for which in range(3):
        locals_[which].start()
        for offset in far_first:
            piece_out(which, offset).start()

    for c in range(frame_tok // CHUNK):
        query_pos = c * CHUNK + lax.broadcasted_iota(jnp.int32, (CHUNK, frame_tok), 0)
        key_pos = lax.broadcasted_iota(jnp.int32, (CHUNK, frame_tok), 1)
        query_row, query_col = block_place(query_pos, tiles, tile_tok)
        key_row, key_col = block_place(key_pos, tiles, tile_tok)
        row_step = key_row - query_row
        across = key_col - query_col
        nearby = (row_step >= -1) & (row_step <= 1) & (across >= -1) & (across <= 1)
        code_scr[pl.ds(c * CHUNK, CHUNK), :] = jnp.where(nearby, (row_step + 1) * 3 + across + 1, 15)

    def first_hop(p):
        return pltpu.make_async_remote_copy(
            src_ref=own_kv.at[:, tokens_of(p), :],
            dst_ref=slots.at[0, :, tokens_of(p), :],
            send_sem=hop_send.at[p],
            recv_sem=hop_recv.at[p],
            device_id=(right, tile),
            device_id_type=MESH_ID,
        )

    for which in range(2):
        locals_[which].wait()

    @pl.when(me < frames - 1)
    def _():
        first_hop(tile).start()

    for offset in near_first:
        for which in range(2):
            piece_in(which, offset).wait_recv()

        @pl.when(me < frames - 1)
        def _():
            first_hop(lax.rem(tile + tiles - offset, tiles)).start()

    def copy_for(step):
        source = own_kv if step == 0 else slots.at[step - 1]
        return pltpu.make_async_remote_copy(
            src_ref=source,
            dst_ref=slots.at[step],
            send_sem=send_sem.at[step],
            recv_sem=recv_sem.at[step],
            device_id=(right, tile),
            device_id_type=MESH_ID,
        )

    copies = [None] + [copy_for(step) for step in range(1, WIN)]

    m_scr[...] = jnp.full(m_scr.shape, NEG_BIG, jnp.float32)
    l_scr[...] = jnp.zeros(l_scr.shape, jnp.float32)
    acc_scr[...] = jnp.zeros(acc_scr.shape, jnp.float32)

    locals_[2].wait()
    for offset in range(1, tiles):
        piece_in(2, offset).wait_recv()

    def attend(block, use):
        def head_body(h, carry):
            col = pl.multiple_of(h * HD, HD)
            key_h = block[0, :, pl.ds(col, HD)]
            value_h = block[1, :, pl.ds(col, HD)]
            for c in range(frame_tok // CHUNK):
                rows = pl.ds(c * CHUNK, CHUNK)
                query_h = own_q[rows, pl.ds(col, HD)]
                scores = lax.dot_general(
                    query_h, key_h, (((1,), (1,)), ((), ())),
                    preferred_element_type=jnp.float32,
                ) * scale
                if use is None:
                    code = code_scr[rows, :]
                    shifted = lax.shift_right_logical(jnp.broadcast_to(head_bits(h), code.shape), code)
                    scores = jnp.where((shifted & 1) == 1, scores, NEG_BIG)
                else:
                    scores = scores + jnp.where(use, 0.0, NEG_BIG)
                old_max = m_scr[h, rows, :]
                new_max = jnp.maximum(old_max, jnp.max(scores, axis=1, keepdims=True))
                weights = jnp.exp(scores - new_max)
                factor = jnp.exp(old_max - new_max)
                l_scr[h, rows, :] = l_scr[h, rows, :] * factor + jnp.sum(weights, axis=1, keepdims=True)
                acc_scr[h, rows, :] = acc_scr[h, rows, :] * factor + jnp.dot(
                    weights.astype(jnp.bfloat16), value_h, preferred_element_type=jnp.float32
                )
                m_scr[h, rows, :] = new_max
            return carry

        lax.fori_loop(0, head_share, head_body, 0)

    attend(own_kv, None)
    for step in range(1, WIN + 1):
        @pl.when(me >= step)
        def _():
            if step == 1:
                for p in range(tiles):
                    first_hop(p).wait_recv()
            else:
                copies[step - 1].wait_recv()
            if step < WIN:
                @pl.when(me < frames - 1)
                def _():
                    copies[step].start()
            attend(slots.at[step - 1], usable(step))

    def finish(h, carry):
        col = pl.multiple_of(h * HD, HD)
        fin[:, pl.ds(col, HD)] = (acc_scr[h] / l_scr[h] * head_gain(h)).astype(fin.dtype)
        return carry

    lax.fori_loop(0, head_share, finish, 0)

    def back_out(offset):
        peer = lax.rem(tile + offset, tiles)
        return pltpu.make_async_remote_copy(
            src_ref=fin.at[tokens_of(peer), :],
            dst_ref=got_out.at[:, channels_of(tile)],
            send_sem=piece_send.at[3, offset],
            recv_sem=piece_recv.at[3, tile],
            device_id=(me, peer),
            device_id_type=MESH_ID,
        )

    def back_in(offset):
        sender = lax.rem(tile + tiles - offset, tiles)
        return pltpu.make_async_remote_copy(
            src_ref=fin.at[tokens_of(tile), :],
            dst_ref=got_out.at[:, channels_of(sender)],
            send_sem=piece_send.at[3, offset],
            recv_sem=piece_recv.at[3, sender],
            device_id=(me, sender),
            device_id_type=MESH_ID,
        )

    home = pltpu.make_async_copy(fin.at[tokens_of(tile), :], got_out.at[:, channels_of(tile)],
                                 local_sem.at[3])
    home.start()
    for offset in range(1, tiles):
        back_out(offset).start()
    home.wait()
    for offset in range(1, tiles):
        back_in(offset).wait_recv()
    out_ref[...] = got_out[...]

    for which in range(3):
        for offset in range(1, tiles):
            piece_out(which, offset).wait_send()
    for offset in range(1, tiles):
        back_out(offset).wait_send()
    for step in range(1, WIN):
        @pl.when((me < frames - 1) & (me >= step))
        def _():
            copies[step].wait_send()

    @pl.when(me < frames - 1)
    def _():
        for p in range(tiles):
            first_hop(p).wait_send()


def fused_attend(frames, tiles, scalars, q, k, v):
    head_share = HEADS // tiles
    tile_tok, channels = q.shape
    frame_tok = tile_tok * tiles
    share = channels // tiles
    flops = 4 * (WIN + 1) * frame_tok * frame_tok * share
    smem = pl.BlockSpec(memory_space=pltpu.SMEM)
    vmem = pl.BlockSpec(memory_space=pltpu.VMEM)
    hbm = pl.BlockSpec(memory_space=pl.ANY)
    return pl.pallas_call(
        functools.partial(fused_kernel, frames, tiles),
        out_shape=jax.ShapeDtypeStruct(q.shape, jnp.bfloat16),
        in_specs=[smem] * len(scalars) + [hbm] * 3,
        out_specs=vmem,
        scratch_shapes=[
            pltpu.VMEM((2, frame_tok, share), jnp.bfloat16),
            pltpu.VMEM((frame_tok, share), jnp.bfloat16),
            pltpu.VMEM((WIN, 2, frame_tok, share), jnp.bfloat16),
            pltpu.VMEM((frame_tok, share), jnp.bfloat16),
            pltpu.VMEM((tile_tok, channels), jnp.bfloat16),
            pltpu.VMEM((frame_tok, frame_tok), jnp.int32),
            pltpu.VMEM((head_share, frame_tok, 1), jnp.float32),
            pltpu.VMEM((head_share, frame_tok, 1), jnp.float32),
            pltpu.VMEM((head_share, frame_tok, HD), jnp.float32),
            pltpu.SemaphoreType.DMA((4, tiles)),
            pltpu.SemaphoreType.DMA((4, tiles)),
            pltpu.SemaphoreType.DMA((4,)),
            pltpu.SemaphoreType.DMA((WIN,)),
            pltpu.SemaphoreType.DMA((WIN,)),
            pltpu.SemaphoreType.DMA((tiles,)),
            pltpu.SemaphoreType.DMA((tiles,)),
        ],
        compiler_params=pltpu.CompilerParams(
            collective_id=0, has_side_effects=True, vmem_limit_bytes=56 * 1024 * 1024
        ),
        cost_estimate=pl.CostEstimate(
            flops=flops,
            transcendentals=(WIN + 1) * head_share * frame_tok * frame_tok,
            bytes_accessed=(WIN + 6) * 2 * frame_tok * share * 2,
        ),
    )(*scalars, q, k, v)


def hand_over_kernel(src_ref, dst_ref):
    dst_ref[...] = src_ref[...]


def hand_over(block):
    vmem = pl.BlockSpec(memory_space=pltpu.VMEM)
    return pl.pallas_call(
        hand_over_kernel,
        out_shape=jax.ShapeDtypeStruct(block.shape, block.dtype),
        in_specs=[vmem],
        out_specs=vmem,
        cost_estimate=pl.CostEstimate(flops=0, transcendentals=0, bytes_accessed=2 * block.size * 2),
    )(block)


def shards(queries, keys, values, step_index, frame_index, window_mask, history_mask, step_gain):
    tile_count = lax.axis_size("tile")
    frames = lax.axis_size("frame")
    tile_id = lax.axis_index("tile")
    group_id = lax.axis_index("frame")
    channels = queries.shape[-1]
    head_share = HEADS // tile_count
    tile_tok = queries.shape[2]
    frame_tok = tile_tok * tile_count
    finished = fused_attend(
        frames, tile_count, (step_index, frame_index, window_mask.T, history_mask, step_gain),
        queries[0, 0], keys[0, 0], values[0, 0],
    )
    return hand_over(finished).reshape(1, 1, tile_tok, channels)


def solution(mesh):
    return jax.shard_map(
        shards,
        mesh=mesh,
        in_specs=(
            P("frame", "tile", None, None),
            P("frame", "tile", None, None),
            P("frame", "tile", None, None),
            P("frame"),
            P("frame"),
            P(),
            P("frame", None),
            P(),
        ),
        out_specs=P("frame", "tile", None, None),
        check_vma=False,
    )
```

```python
import functools
import math

import jax
import jax.numpy as jnp
from jax import lax
from jax.experimental import pallas as pl
from jax.experimental.pallas import tpu as pltpu
from jax.sharding import PartitionSpec as P

HEADS = 40
HD = 128
TH = 8
TW = 8
BLK = 4
WIN = 5
STEPS = 4
CHUNK = 128

NEG_BIG = -1e30
MESH_ID = pl.DeviceIdType.MESH


def block_place(positions, tile_count, tile_tok):
    tile_cols = min(tile_count, 4)
    tile_of = positions // tile_tok
    within = positions % tile_tok
    row = tile_of // tile_cols * TH + within // TW
    col = tile_of % tile_cols * TW + within % TW
    return row // BLK, col // BLK


def fused_kernel(frames, tiles, step_ref, fidx_ref, wm_ref, hm_ref, sg_ref, q_ref, k_ref, v_ref, out_ref,
                 own_kv, own_q, slots, fin, got_out, code_scr, m_scr, l_scr, acc_scr,
                 piece_send, piece_recv, local_sem, send_sem, recv_sem, hop_send, hop_recv):
    me = lax.axis_index("frame")
    tile = lax.axis_index("tile")
    right = lax.rem(me + 1, frames)
    left = lax.rem(me + frames - 1, frames)
    head_share = acc_scr.shape[0]
    frame_tok = own_q.shape[0]
    share = own_q.shape[1]
    tile_tok = q_ref.shape[0]
    scale = 1.0 / math.sqrt(HD)

    def head_bits(h):
        row = tile * head_share + h
        bits = 16
        for offset in range(9):
            bits = bits | jnp.where(wm_ref[offset, row] == 1, 1 << offset, 0)
        return bits

    def usable(distance):
        return (hm_ref[0, distance - 1] == 1) & (distance <= fidx_ref[0]) & (me >= distance)

    def head_gain(h):
        return sg_ref[step_ref[0], tile * head_share + h]

    barrier = pltpu.get_barrier_semaphore()
    for other in (left, right):
        pl.semaphore_signal(barrier, inc=1, device_id=(other, tile), device_id_type=MESH_ID)
    for offset in range(1, tiles):
        peer = lax.rem(tile + offset, tiles)
        pl.semaphore_signal(barrier, inc=1, device_id=(me, peer), device_id_type=MESH_ID)
    pl.semaphore_wait(barrier, 2 + tiles - 1)

    def channels_of(p):
        return pl.ds(pl.multiple_of(p * share, 128), share)

    def tokens_of(p):
        return pl.ds(pl.multiple_of(p * tile_tok, tile_tok), tile_tok)

    sources = [k_ref, v_ref, q_ref]
    targets = [lambda rows: own_kv.at[0, rows, :], lambda rows: own_kv.at[1, rows, :],
               lambda rows: own_q.at[rows, :]]

    def piece_out(which, offset):
        peer = lax.rem(tile + offset, tiles)
        return pltpu.make_async_remote_copy(
            src_ref=sources[which].at[:, channels_of(peer)],
            dst_ref=targets[which](tokens_of(tile)),
            send_sem=piece_send.at[which, offset],
            recv_sem=piece_recv.at[which, tile],
            device_id=(me, peer),
            device_id_type=MESH_ID,
        )

    def piece_in(which, offset):
        sender = lax.rem(tile + tiles - offset, tiles)
        return pltpu.make_async_remote_copy(
            src_ref=sources[which].at[:, channels_of(tile)],
            dst_ref=targets[which](tokens_of(sender)),
            send_sem=piece_send.at[which, offset],
            recv_sem=piece_recv.at[which, sender],
            device_id=(me, sender),
            device_id_type=MESH_ID,
        )

    locals_ = [
        pltpu.make_async_copy(
            sources[which].at[:, channels_of(tile)], targets[which](tokens_of(tile)),
            local_sem.at[which],
        )
        for which in range(3)
    ]
    far_first = [j for j in range(1, tiles) if j % 2] + [j for j in range(1, tiles) if j % 2 == 0]
    near_first = far_first[::-1]
    for which in range(3):
        locals_[which].start()
        for offset in far_first:
            piece_out(which, offset).start()

    for c in range(frame_tok // CHUNK):
        query_pos = c * CHUNK + lax.broadcasted_iota(jnp.int32, (CHUNK, frame_tok), 0)
        key_pos = lax.broadcasted_iota(jnp.int32, (CHUNK, frame_tok), 1)
        query_row, query_col = block_place(query_pos, tiles, tile_tok)
        key_row, key_col = block_place(key_pos, tiles, tile_tok)
        row_step = key_row - query_row
        across = key_col - query_col
        nearby = (row_step >= -1) & (row_step <= 1) & (across >= -1) & (across <= 1)
        code_scr[pl.ds(c * CHUNK, CHUNK), :] = jnp.where(nearby, (row_step + 1) * 3 + across + 1, 15)

    def first_hop(p):
        return pltpu.make_async_remote_copy(
            src_ref=own_kv.at[:, tokens_of(p), :],
            dst_ref=slots.at[0, :, tokens_of(p), :],
            send_sem=hop_send.at[p],
            recv_sem=hop_recv.at[p],
            device_id=(right, tile),
            device_id_type=MESH_ID,
        )

    for which in range(2):
        locals_[which].wait()

    @pl.when(me < frames - 1)
    def _():
        first_hop(tile).start()

    for offset in near_first:
        for which in range(2):
            piece_in(which, offset).wait_recv()

        @pl.when(me < frames - 1)
        def _():
            first_hop(lax.rem(tile + tiles - offset, tiles)).start()

    def copy_for(step):
        source = own_kv if step == 0 else slots.at[step - 1]
        return pltpu.make_async_remote_copy(
            src_ref=source,
            dst_ref=slots.at[step],
            send_sem=send_sem.at[step],
            recv_sem=recv_sem.at[step],
            device_id=(right, tile),
            device_id_type=MESH_ID,
        )

    copies = [None] + [copy_for(step) for step in range(1, WIN)]

    m_scr[...] = jnp.full(m_scr.shape, NEG_BIG, jnp.float32)
    l_scr[...] = jnp.zeros(l_scr.shape, jnp.float32)
    acc_scr[...] = jnp.zeros(acc_scr.shape, jnp.float32)

    locals_[2].wait()
    for offset in range(1, tiles):
        piece_in(2, offset).wait_recv()

    def attend(block, use):
        def head_body(h, carry):
            col = pl.multiple_of(h * HD, HD)
            key_h = block[0, :, pl.ds(col, HD)]
            value_h = block[1, :, pl.ds(col, HD)]
            for c in range(frame_tok // CHUNK):
                rows = pl.ds(c * CHUNK, CHUNK)
                query_h = own_q[rows, pl.ds(col, HD)]
                scores = lax.dot_general(
                    query_h, key_h, (((1,), (1,)), ((), ())),
                    preferred_element_type=jnp.float32,
                ) * scale
                if use is None:
                    code = code_scr[rows, :]
                    shifted = lax.shift_right_logical(jnp.broadcast_to(head_bits(h), code.shape), code)
                    scores = jnp.where((shifted & 1) == 1, scores, NEG_BIG)
                else:
                    scores = scores + jnp.where(use, 0.0, NEG_BIG)
                old_max = m_scr[h, rows, :]
                new_max = jnp.maximum(old_max, jnp.max(scores, axis=1, keepdims=True))
                weights = jnp.exp(scores - new_max)
                factor = jnp.exp(old_max - new_max)
                l_scr[h, rows, :] = l_scr[h, rows, :] * factor + jnp.sum(weights, axis=1, keepdims=True)
                acc_scr[h, rows, :] = acc_scr[h, rows, :] * factor + jnp.dot(
                    weights.astype(jnp.bfloat16), value_h, preferred_element_type=jnp.float32
                )
                m_scr[h, rows, :] = new_max
            return carry

        lax.fori_loop(0, head_share, head_body, 0)

    attend(own_kv, None)
    for step in range(1, WIN + 1):
        @pl.when(me >= step)
        def _():
            if step == 1:
                for p in range(tiles):
                    first_hop(p).wait_recv()
            else:
                copies[step - 1].wait_recv()
            if step < WIN:
                @pl.when(me < frames - 1)
                def _():
                    copies[step].start()
            attend(slots.at[step - 1], usable(step))

    def finish(h, carry):
        col = pl.multiple_of(h * HD, HD)
        fin[:, pl.ds(col, HD)] = (acc_scr[h] / l_scr[h] * head_gain(h)).astype(fin.dtype)
        return carry

    lax.fori_loop(0, head_share, finish, 0)

    def back_out(offset):
        peer = lax.rem(tile + offset, tiles)
        return pltpu.make_async_remote_copy(
            src_ref=fin.at[tokens_of(peer), :],
            dst_ref=got_out.at[:, channels_of(tile)],
            send_sem=piece_send.at[3, offset],
            recv_sem=piece_recv.at[3, tile],
            device_id=(me, peer),
            device_id_type=MESH_ID,
        )

    def back_in(offset):
        sender = lax.rem(tile + tiles - offset, tiles)
        return pltpu.make_async_remote_copy(
            src_ref=fin.at[tokens_of(tile), :],
            dst_ref=got_out.at[:, channels_of(sender)],
            send_sem=piece_send.at[3, offset],
            recv_sem=piece_recv.at[3, sender],
            device_id=(me, sender),
            device_id_type=MESH_ID,
        )

    home = pltpu.make_async_copy(fin.at[tokens_of(tile), :], got_out.at[:, channels_of(tile)],
                                 local_sem.at[3])
    home.start()
    for offset in far_first:
        back_out(offset).start()
    home.wait()
    for offset in near_first:
        back_in(offset).wait_recv()
    out_ref[...] = got_out[...]

    for which in range(3):
        for offset in range(1, tiles):
            piece_out(which, offset).wait_send()
    for offset in range(1, tiles):
        back_out(offset).wait_send()
    for step in range(1, WIN):
        @pl.when((me < frames - 1) & (me >= step))
        def _():
            copies[step].wait_send()

    @pl.when(me < frames - 1)
    def _():
        for p in range(tiles):
            first_hop(p).wait_send()


def fused_attend(frames, tiles, scalars, q, k, v):
    head_share = HEADS // tiles
    tile_tok, channels = q.shape
    frame_tok = tile_tok * tiles
    share = channels // tiles
    flops = 4 * (WIN + 1) * frame_tok * frame_tok * share
    smem = pl.BlockSpec(memory_space=pltpu.SMEM)
    vmem = pl.BlockSpec(memory_space=pltpu.VMEM)
    hbm = pl.BlockSpec(memory_space=pl.ANY)
    return pl.pallas_call(
        functools.partial(fused_kernel, frames, tiles),
        out_shape=jax.ShapeDtypeStruct(q.shape, jnp.bfloat16),
        in_specs=[smem] * len(scalars) + [hbm] * 3,
        out_specs=vmem,
        scratch_shapes=[
            pltpu.VMEM((2, frame_tok, share), jnp.bfloat16),
            pltpu.VMEM((frame_tok, share), jnp.bfloat16),
            pltpu.VMEM((WIN, 2, frame_tok, share), jnp.bfloat16),
            pltpu.VMEM((frame_tok, share), jnp.bfloat16),
            pltpu.VMEM((tile_tok, channels), jnp.bfloat16),
            pltpu.VMEM((frame_tok, frame_tok), jnp.int32),
            pltpu.VMEM((head_share, frame_tok, 1), jnp.float32),
            pltpu.VMEM((head_share, frame_tok, 1), jnp.float32),
            pltpu.VMEM((head_share, frame_tok, HD), jnp.float32),
            pltpu.SemaphoreType.DMA((4, tiles)),
            pltpu.SemaphoreType.DMA((4, tiles)),
            pltpu.SemaphoreType.DMA((4,)),
            pltpu.SemaphoreType.DMA((WIN,)),
            pltpu.SemaphoreType.DMA((WIN,)),
            pltpu.SemaphoreType.DMA((tiles,)),
            pltpu.SemaphoreType.DMA((tiles,)),
        ],
        compiler_params=pltpu.CompilerParams(
            collective_id=0, has_side_effects=True, vmem_limit_bytes=56 * 1024 * 1024
        ),
        cost_estimate=pl.CostEstimate(
            flops=flops,
            transcendentals=(WIN + 1) * head_share * frame_tok * frame_tok,
            bytes_accessed=(WIN + 6) * 2 * frame_tok * share * 2,
        ),
    )(*scalars, q, k, v)


def hand_over_kernel(src_ref, dst_ref):
    dst_ref[...] = src_ref[...]


def hand_over(block):
    vmem = pl.BlockSpec(memory_space=pltpu.VMEM)
    return pl.pallas_call(
        hand_over_kernel,
        out_shape=jax.ShapeDtypeStruct(block.shape, block.dtype),
        in_specs=[vmem],
        out_specs=vmem,
        cost_estimate=pl.CostEstimate(flops=0, transcendentals=0, bytes_accessed=2 * block.size * 2),
    )(block)


def shards(queries, keys, values, step_index, frame_index, window_mask, history_mask, step_gain):
    tile_count = lax.axis_size("tile")
    frames = lax.axis_size("frame")
    tile_id = lax.axis_index("tile")
    group_id = lax.axis_index("frame")
    channels = queries.shape[-1]
    head_share = HEADS // tile_count
    tile_tok = queries.shape[2]
    frame_tok = tile_tok * tile_count
    finished = fused_attend(
        frames, tile_count, (step_index, frame_index, window_mask.T, history_mask, step_gain),
        queries[0, 0], keys[0, 0], values[0, 0],
    )
    return hand_over(finished).reshape(1, 1, tile_tok, channels)


def solution(mesh):
    return jax.shard_map(
        shards,
        mesh=mesh,
        in_specs=(
            P("frame", "tile", None, None),
            P("frame", "tile", None, None),
            P("frame", "tile", None, None),
            P("frame"),
            P("frame"),
            P(),
            P("frame", None),
            P(),
        ),
        out_specs=P("frame", "tile", None, None),
        check_vma=False,
    )
```

```python
import functools
import math

import jax
import jax.numpy as jnp
from jax import lax
from jax.experimental import pallas as pl
from jax.experimental.pallas import tpu as pltpu
from jax.sharding import PartitionSpec as P

HEADS = 40
HD = 128
TH = 8
TW = 8
BLK = 4
WIN = 5
STEPS = 4
CHUNK = 128

NEG_BIG = -1e30
MESH_ID = pl.DeviceIdType.MESH


def block_place(positions, tile_count, tile_tok):
    tile_cols = min(tile_count, 4)
    tile_of = positions // tile_tok
    within = positions % tile_tok
    row = tile_of // tile_cols * TH + within // TW
    col = tile_of % tile_cols * TW + within % TW
    return row // BLK, col // BLK


def fused_kernel(frames, tiles, step_ref, fidx_ref, wm_ref, hm_ref, sg_ref, q_ref, k_ref, v_ref, out_ref,
                 own_kv, own_q, slots, fin, got_out, code_scr, m_scr, l_scr, acc_scr,
                 piece_send, piece_recv, local_sem, send_sem, recv_sem, hop_send, hop_recv):
    me = lax.axis_index("frame")
    tile = lax.axis_index("tile")
    right = lax.rem(me + 1, frames)
    left = lax.rem(me + frames - 1, frames)
    head_share = acc_scr.shape[0]
    frame_tok = own_q.shape[0]
    share = own_q.shape[1]
    tile_tok = q_ref.shape[0]
    scale = 1.0 / math.sqrt(HD)

    def head_bits(h):
        row = tile * head_share + h
        bits = 16
        for offset in range(9):
            bits = bits | jnp.where(wm_ref[offset, row] == 1, 1 << offset, 0)
        return bits

    def usable(distance):
        return (hm_ref[0, distance - 1] == 1) & (distance <= fidx_ref[0]) & (me >= distance)

    def head_gain(h):
        return sg_ref[step_ref[0], tile * head_share + h]

    barrier = pltpu.get_barrier_semaphore()
    for other in (left, right):
        pl.semaphore_signal(barrier, inc=1, device_id=(other, tile), device_id_type=MESH_ID)
    for offset in range(1, tiles):
        peer = lax.rem(tile + offset, tiles)
        pl.semaphore_signal(barrier, inc=1, device_id=(me, peer), device_id_type=MESH_ID)
    pl.semaphore_wait(barrier, 2 + tiles - 1)

    def channels_of(p):
        return pl.ds(pl.multiple_of(p * share, 128), share)

    def tokens_of(p):
        return pl.ds(pl.multiple_of(p * tile_tok, tile_tok), tile_tok)

    sources = [k_ref, v_ref, q_ref]
    targets = [lambda rows: own_kv.at[0, rows, :], lambda rows: own_kv.at[1, rows, :],
               lambda rows: own_q.at[rows, :]]

    def piece_out(which, offset):
        peer = lax.rem(tile + offset, tiles)
        return pltpu.make_async_remote_copy(
            src_ref=sources[which].at[:, channels_of(peer)],
            dst_ref=targets[which](tokens_of(tile)),
            send_sem=piece_send.at[which, offset],
            recv_sem=piece_recv.at[which, tile],
            device_id=(me, peer),
            device_id_type=MESH_ID,
        )

    def piece_in(which, offset):
        sender = lax.rem(tile + tiles - offset, tiles)
        return pltpu.make_async_remote_copy(
            src_ref=sources[which].at[:, channels_of(tile)],
            dst_ref=targets[which](tokens_of(sender)),
            send_sem=piece_send.at[which, offset],
            recv_sem=piece_recv.at[which, sender],
            device_id=(me, sender),
            device_id_type=MESH_ID,
        )

    locals_ = [
        pltpu.make_async_copy(
            sources[which].at[:, channels_of(tile)], targets[which](tokens_of(tile)),
            local_sem.at[which],
        )
        for which in range(3)
    ]
    far_first = [j for j in range(1, tiles) if j % 2] + [j for j in range(1, tiles) if j % 2 == 0]
    near_first = far_first[::-1]
    for which in range(3):
        locals_[which].start()
    for group in ([j for j in far_first if j % 2], [j for j in far_first if j % 2 == 0]):
        for which in range(2):
            for offset in group:
                piece_out(which, offset).start()
    for offset in far_first:
        piece_out(2, offset).start()

    for c in range(frame_tok // CHUNK):
        query_pos = c * CHUNK + lax.broadcasted_iota(jnp.int32, (CHUNK, frame_tok), 0)
        key_pos = lax.broadcasted_iota(jnp.int32, (CHUNK, frame_tok), 1)
        query_row, query_col = block_place(query_pos, tiles, tile_tok)
        key_row, key_col = block_place(key_pos, tiles, tile_tok)
        row_step = key_row - query_row
        across = key_col - query_col
        nearby = (row_step >= -1) & (row_step <= 1) & (across >= -1) & (across <= 1)
        code_scr[pl.ds(c * CHUNK, CHUNK), :] = jnp.where(nearby, (row_step + 1) * 3 + across + 1, 15)

    def first_hop(p):
        return pltpu.make_async_remote_copy(
            src_ref=own_kv.at[:, tokens_of(p), :],
            dst_ref=slots.at[0, :, tokens_of(p), :],
            send_sem=hop_send.at[p],
            recv_sem=hop_recv.at[p],
            device_id=(right, tile),
            device_id_type=MESH_ID,
        )

    for which in range(2):
        locals_[which].wait()

    @pl.when(me < frames - 1)
    def _():
        first_hop(tile).start()

    for offset in near_first:
        for which in range(2):
            piece_in(which, offset).wait_recv()

        @pl.when(me < frames - 1)
        def _():
            first_hop(lax.rem(tile + tiles - offset, tiles)).start()

    def copy_for(step):
        source = own_kv if step == 0 else slots.at[step - 1]
        return pltpu.make_async_remote_copy(
            src_ref=source,
            dst_ref=slots.at[step],
            send_sem=send_sem.at[step],
            recv_sem=recv_sem.at[step],
            device_id=(right, tile),
            device_id_type=MESH_ID,
        )

    copies = [None] + [copy_for(step) for step in range(1, WIN)]

    m_scr[...] = jnp.full(m_scr.shape, NEG_BIG, jnp.float32)
    l_scr[...] = jnp.zeros(l_scr.shape, jnp.float32)
    acc_scr[...] = jnp.zeros(acc_scr.shape, jnp.float32)

    locals_[2].wait()
    for offset in range(1, tiles):
        piece_in(2, offset).wait_recv()

    def attend(block, use):
        def head_body(h, carry):
            col = pl.multiple_of(h * HD, HD)
            key_h = block[0, :, pl.ds(col, HD)]
            value_h = block[1, :, pl.ds(col, HD)]
            for c in range(frame_tok // CHUNK):
                rows = pl.ds(c * CHUNK, CHUNK)
                query_h = own_q[rows, pl.ds(col, HD)]
                scores = lax.dot_general(
                    query_h, key_h, (((1,), (1,)), ((), ())),
                    preferred_element_type=jnp.float32,
                ) * scale
                if use is None:
                    code = code_scr[rows, :]
                    shifted = lax.shift_right_logical(jnp.broadcast_to(head_bits(h), code.shape), code)
                    scores = jnp.where((shifted & 1) == 1, scores, NEG_BIG)
                else:
                    scores = scores + jnp.where(use, 0.0, NEG_BIG)
                old_max = m_scr[h, rows, :]
                new_max = jnp.maximum(old_max, jnp.max(scores, axis=1, keepdims=True))
                weights = jnp.exp(scores - new_max)
                factor = jnp.exp(old_max - new_max)
                l_scr[h, rows, :] = l_scr[h, rows, :] * factor + jnp.sum(weights, axis=1, keepdims=True)
                acc_scr[h, rows, :] = acc_scr[h, rows, :] * factor + jnp.dot(
                    weights.astype(jnp.bfloat16), value_h, preferred_element_type=jnp.float32
                )
                m_scr[h, rows, :] = new_max
            return carry

        lax.fori_loop(0, head_share, head_body, 0)

    attend(own_kv, None)
    for step in range(1, WIN + 1):
        @pl.when(me >= step)
        def _():
            if step == 1:
                for p in range(tiles):
                    first_hop(p).wait_recv()
            else:
                copies[step - 1].wait_recv()
            if step < WIN:
                @pl.when(me < frames - 1)
                def _():
                    copies[step].start()
            attend(slots.at[step - 1], usable(step))

    def finish(h, carry):
        col = pl.multiple_of(h * HD, HD)
        fin[:, pl.ds(col, HD)] = (acc_scr[h] / l_scr[h] * head_gain(h)).astype(fin.dtype)
        return carry

    lax.fori_loop(0, head_share, finish, 0)

    def back_out(offset):
        peer = lax.rem(tile + offset, tiles)
        return pltpu.make_async_remote_copy(
            src_ref=fin.at[tokens_of(peer), :],
            dst_ref=got_out.at[:, channels_of(tile)],
            send_sem=piece_send.at[3, offset],
            recv_sem=piece_recv.at[3, tile],
            device_id=(me, peer),
            device_id_type=MESH_ID,
        )

    def back_in(offset):
        sender = lax.rem(tile + tiles - offset, tiles)
        return pltpu.make_async_remote_copy(
            src_ref=fin.at[tokens_of(tile), :],
            dst_ref=got_out.at[:, channels_of(sender)],
            send_sem=piece_send.at[3, offset],
            recv_sem=piece_recv.at[3, sender],
            device_id=(me, sender),
            device_id_type=MESH_ID,
        )

    home = pltpu.make_async_copy(fin.at[tokens_of(tile), :], got_out.at[:, channels_of(tile)],
                                 local_sem.at[3])
    home.start()
    for offset in range(1, tiles):
        back_out(offset).start()
    home.wait()
    for offset in range(1, tiles):
        back_in(offset).wait_recv()
    out_ref[...] = got_out[...]

    for which in range(3):
        for offset in range(1, tiles):
            piece_out(which, offset).wait_send()
    for offset in range(1, tiles):
        back_out(offset).wait_send()
    for step in range(1, WIN):
        @pl.when((me < frames - 1) & (me >= step))
        def _():
            copies[step].wait_send()

    @pl.when(me < frames - 1)
    def _():
        for p in range(tiles):
            first_hop(p).wait_send()


def fused_attend(frames, tiles, scalars, q, k, v):
    head_share = HEADS // tiles
    tile_tok, channels = q.shape
    frame_tok = tile_tok * tiles
    share = channels // tiles
    flops = 4 * (WIN + 1) * frame_tok * frame_tok * share
    smem = pl.BlockSpec(memory_space=pltpu.SMEM)
    vmem = pl.BlockSpec(memory_space=pltpu.VMEM)
    hbm = pl.BlockSpec(memory_space=pl.ANY)
    return pl.pallas_call(
        functools.partial(fused_kernel, frames, tiles),
        out_shape=jax.ShapeDtypeStruct(q.shape, jnp.bfloat16),
        in_specs=[smem] * len(scalars) + [hbm] * 3,
        out_specs=vmem,
        scratch_shapes=[
            pltpu.VMEM((2, frame_tok, share), jnp.bfloat16),
            pltpu.VMEM((frame_tok, share), jnp.bfloat16),
            pltpu.VMEM((WIN, 2, frame_tok, share), jnp.bfloat16),
            pltpu.VMEM((frame_tok, share), jnp.bfloat16),
            pltpu.VMEM((tile_tok, channels), jnp.bfloat16),
            pltpu.VMEM((frame_tok, frame_tok), jnp.int32),
            pltpu.VMEM((head_share, frame_tok, 1), jnp.float32),
            pltpu.VMEM((head_share, frame_tok, 1), jnp.float32),
            pltpu.VMEM((head_share, frame_tok, HD), jnp.float32),
            pltpu.SemaphoreType.DMA((4, tiles)),
            pltpu.SemaphoreType.DMA((4, tiles)),
            pltpu.SemaphoreType.DMA((4,)),
            pltpu.SemaphoreType.DMA((WIN,)),
            pltpu.SemaphoreType.DMA((WIN,)),
            pltpu.SemaphoreType.DMA((tiles,)),
            pltpu.SemaphoreType.DMA((tiles,)),
        ],
        compiler_params=pltpu.CompilerParams(
            collective_id=0, has_side_effects=True, vmem_limit_bytes=56 * 1024 * 1024
        ),
        cost_estimate=pl.CostEstimate(
            flops=flops,
            transcendentals=(WIN + 1) * head_share * frame_tok * frame_tok,
            bytes_accessed=(WIN + 6) * 2 * frame_tok * share * 2,
        ),
    )(*scalars, q, k, v)


def hand_over_kernel(src_ref, dst_ref):
    dst_ref[...] = src_ref[...]


def hand_over(block):
    vmem = pl.BlockSpec(memory_space=pltpu.VMEM)
    return pl.pallas_call(
        hand_over_kernel,
        out_shape=jax.ShapeDtypeStruct(block.shape, block.dtype),
        in_specs=[vmem],
        out_specs=vmem,
        cost_estimate=pl.CostEstimate(flops=0, transcendentals=0, bytes_accessed=2 * block.size * 2),
    )(block)


def shards(queries, keys, values, step_index, frame_index, window_mask, history_mask, step_gain):
    tile_count = lax.axis_size("tile")
    frames = lax.axis_size("frame")
    tile_id = lax.axis_index("tile")
    group_id = lax.axis_index("frame")
    channels = queries.shape[-1]
    head_share = HEADS // tile_count
    tile_tok = queries.shape[2]
    frame_tok = tile_tok * tile_count
    finished = fused_attend(
        frames, tile_count, (step_index, frame_index, window_mask.T, history_mask, step_gain),
        queries[0, 0], keys[0, 0], values[0, 0],
    )
    return hand_over(finished).reshape(1, 1, tile_tok, channels)


def solution(mesh):
    return jax.shard_map(
        shards,
        mesh=mesh,
        in_specs=(
            P("frame", "tile", None, None),
            P("frame", "tile", None, None),
            P("frame", "tile", None, None),
            P("frame"),
            P("frame"),
            P(),
            P("frame", None),
            P(),
        ),
        out_specs=P("frame", "tile", None, None),
        check_vma=False,
    )
```

```python
import functools
import math

import jax
import jax.numpy as jnp
from jax import lax
from jax.experimental import pallas as pl
from jax.experimental.pallas import tpu as pltpu
from jax.sharding import PartitionSpec as P

HEADS = 40
HD = 128
TH = 8
TW = 8
BLK = 4
WIN = 5
STEPS = 4
CHUNK = 128

NEG_BIG = -1e30
MESH_ID = pl.DeviceIdType.MESH


def block_place(positions, tile_count, tile_tok):
    tile_cols = min(tile_count, 4)
    tile_of = positions // tile_tok
    within = positions % tile_tok
    row = tile_of // tile_cols * TH + within // TW
    col = tile_of % tile_cols * TW + within % TW
    return row // BLK, col // BLK


def fused_kernel(frames, tiles, step_ref, fidx_ref, wm_ref, hm_ref, sg_ref, q_ref, k_ref, v_ref, out_ref,
                 own_kv, own_q, slots, fin, got_out, code_scr, m_scr, l_scr, acc_scr,
                 piece_send, piece_recv, local_sem, send_sem, recv_sem, hop_send, hop_recv):
    me = lax.axis_index("frame")
    tile = lax.axis_index("tile")
    right = lax.rem(me + 1, frames)
    left = lax.rem(me + frames - 1, frames)
    head_share = acc_scr.shape[0]
    frame_tok = own_q.shape[0]
    share = own_q.shape[1]
    tile_tok = q_ref.shape[0]
    scale = 1.0 / math.sqrt(HD)

    def head_bits(h):
        row = tile * head_share + h
        bits = 16
        for offset in range(9):
            bits = bits | jnp.where(wm_ref[offset, row] == 1, 1 << offset, 0)
        return bits

    def usable(distance):
        return (hm_ref[0, distance - 1] == 1) & (distance <= fidx_ref[0]) & (me >= distance)

    def head_gain(h):
        return sg_ref[step_ref[0], tile * head_share + h]

    barrier = pltpu.get_barrier_semaphore()
    for other in (left, right):
        pl.semaphore_signal(barrier, inc=1, device_id=(other, tile), device_id_type=MESH_ID)
    for offset in range(1, tiles):
        peer = lax.rem(tile + offset, tiles)
        pl.semaphore_signal(barrier, inc=1, device_id=(me, peer), device_id_type=MESH_ID)
    pl.semaphore_wait(barrier, 2 + tiles - 1)

    def channels_of(p):
        return pl.ds(pl.multiple_of(p * share, 128), share)

    def tokens_of(p):
        return pl.ds(pl.multiple_of(p * tile_tok, tile_tok), tile_tok)

    sources = [k_ref, v_ref, q_ref]
    targets = [lambda rows: own_kv.at[0, rows, :], lambda rows: own_kv.at[1, rows, :],
               lambda rows: own_q.at[rows, :]]

    def piece_out(which, offset):
        peer = lax.rem(tile + offset, tiles)
        return pltpu.make_async_remote_copy(
            src_ref=sources[which].at[:, channels_of(peer)],
            dst_ref=targets[which](tokens_of(tile)),
            send_sem=piece_send.at[which, offset],
            recv_sem=piece_recv.at[which, tile],
            device_id=(me, peer),
            device_id_type=MESH_ID,
        )

    def piece_in(which, offset):
        sender = lax.rem(tile + tiles - offset, tiles)
        return pltpu.make_async_remote_copy(
            src_ref=sources[which].at[:, channels_of(tile)],
            dst_ref=targets[which](tokens_of(sender)),
            send_sem=piece_send.at[which, offset],
            recv_sem=piece_recv.at[which, sender],
            device_id=(me, sender),
            device_id_type=MESH_ID,
        )

    locals_ = [
        pltpu.make_async_copy(
            sources[which].at[:, channels_of(tile)], targets[which](tokens_of(tile)),
            local_sem.at[which],
        )
        for which in range(3)
    ]
    far_first = [j for j in range(1, tiles) if j % 2] + [j for j in range(1, tiles) if j % 2 == 0]
    near_first = far_first[::-1]
    for which in range(3):
        locals_[which].start()
        for offset in far_first:
            piece_out(which, offset).start()

    for c in range(frame_tok // CHUNK):
        query_pos = c * CHUNK + lax.broadcasted_iota(jnp.int32, (CHUNK, frame_tok), 0)
        key_pos = lax.broadcasted_iota(jnp.int32, (CHUNK, frame_tok), 1)
        query_row, query_col = block_place(query_pos, tiles, tile_tok)
        key_row, key_col = block_place(key_pos, tiles, tile_tok)
        row_step = key_row - query_row
        across = key_col - query_col
        nearby = (row_step >= -1) & (row_step <= 1) & (across >= -1) & (across <= 1)
        code_scr[pl.ds(c * CHUNK, CHUNK), :] = jnp.where(nearby, (row_step + 1) * 3 + across + 1, 15)

    def first_hop(p):
        return pltpu.make_async_remote_copy(
            src_ref=own_kv.at[:, tokens_of(p), :],
            dst_ref=slots.at[0, :, tokens_of(p), :],
            send_sem=hop_send.at[p],
            recv_sem=hop_recv.at[p],
            device_id=(right, tile),
            device_id_type=MESH_ID,
        )

    for which in range(2):
        locals_[which].wait()

    @pl.when(me < frames - 1)
    def _():
        first_hop(tile).start()

    for offset in near_first:
        for which in range(2):
            piece_in(which, offset).wait_recv()

        @pl.when(me < frames - 1)
        def _():
            first_hop(lax.rem(tile + tiles - offset, tiles)).start()

    def copy_for(step):
        source = own_kv if step == 0 else slots.at[step - 1]
        return pltpu.make_async_remote_copy(
            src_ref=source,
            dst_ref=slots.at[step],
            send_sem=send_sem.at[step],
            recv_sem=recv_sem.at[step],
            device_id=(right, tile),
            device_id_type=MESH_ID,
        )

    copies = [None] + [copy_for(step) for step in range(1, WIN)]

    m_scr[...] = jnp.full(m_scr.shape, NEG_BIG, jnp.float32)
    l_scr[...] = jnp.zeros(l_scr.shape, jnp.float32)
    acc_scr[...] = jnp.zeros(acc_scr.shape, jnp.float32)

    locals_[2].wait()
    for offset in range(1, tiles):
        piece_in(2, offset).wait_recv()

    def attend(block, use):
        def head_body(h, carry):
            col = pl.multiple_of(h * HD, HD)
            key_h = block[0, :, pl.ds(col, HD)]
            value_h = block[1, :, pl.ds(col, HD)]
            for c in range(frame_tok // CHUNK):
                rows = pl.ds(c * CHUNK, CHUNK)
                query_h = own_q[rows, pl.ds(col, HD)]
                scores = lax.dot_general(
                    query_h, key_h, (((1,), (1,)), ((), ())),
                    preferred_element_type=jnp.float32,
                ) * scale
                if use is None:
                    code = code_scr[rows, :]
                    shifted = lax.shift_right_logical(jnp.broadcast_to(head_bits(h), code.shape), code)
                    scores = jnp.where((shifted & 1) == 1, scores, NEG_BIG)
                else:
                    scores = scores + jnp.where(use, 0.0, NEG_BIG)
                old_max = m_scr[h, rows, :]
                new_max = jnp.maximum(old_max, jnp.max(scores, axis=1, keepdims=True))
                weights = jnp.exp(scores - new_max)
                factor = jnp.exp(old_max - new_max)
                l_scr[h, rows, :] = l_scr[h, rows, :] * factor + jnp.sum(weights, axis=1, keepdims=True)
                acc_scr[h, rows, :] = acc_scr[h, rows, :] * factor + jnp.dot(
                    weights.astype(jnp.bfloat16), value_h, preferred_element_type=jnp.float32
                )
                m_scr[h, rows, :] = new_max
            return carry

        lax.fori_loop(0, head_share, head_body, 0)

    attend(own_kv, None)
    for step in range(1, WIN + 1):
        @pl.when(me >= step)
        def _():
            if step == 1:
                for p in range(tiles):
                    first_hop(p).wait_recv()
            else:
                copies[step - 1].wait_recv()
            if step < WIN:
                @pl.when(me < frames - 1)
                def _():
                    copies[step].start()
            attend(slots.at[step - 1], usable(step))

    def finish(h, carry):
        col = pl.multiple_of(h * HD, HD)
        fin[:, pl.ds(col, HD)] = (acc_scr[h] / l_scr[h] * head_gain(h)).astype(fin.dtype)
        return carry

    lax.fori_loop(0, head_share, finish, 0)

    def back_out(offset):
        peer = lax.rem(tile + offset, tiles)
        return pltpu.make_async_remote_copy(
            src_ref=fin.at[tokens_of(peer), :],
            dst_ref=got_out.at[:, channels_of(tile)],
            send_sem=piece_send.at[3, offset],
            recv_sem=piece_recv.at[3, tile],
            device_id=(me, peer),
            device_id_type=MESH_ID,
        )

    def back_in(offset):
        sender = lax.rem(tile + tiles - offset, tiles)
        return pltpu.make_async_remote_copy(
            src_ref=fin.at[tokens_of(tile), :],
            dst_ref=got_out.at[:, channels_of(sender)],
            send_sem=piece_send.at[3, offset],
            recv_sem=piece_recv.at[3, sender],
            device_id=(me, sender),
            device_id_type=MESH_ID,
        )

    home = pltpu.make_async_copy(fin.at[tokens_of(tile), :], got_out.at[:, channels_of(tile)],
                                 local_sem.at[3])
    home.start()
    for offset in range(1, tiles):
        back_out(offset).start()
    home.wait()
    for offset in range(1, tiles):
        back_in(offset).wait_recv()
    out_ref[...] = got_out[...]

    for which in range(3):
        for offset in range(1, tiles):
            piece_out(which, offset).wait_send()
    for offset in range(1, tiles):
        back_out(offset).wait_send()
    for step in range(1, WIN):
        @pl.when((me < frames - 1) & (me >= step))
        def _():
            copies[step].wait_send()

    @pl.when(me < frames - 1)
    def _():
        for p in range(tiles):
            first_hop(p).wait_send()


def fused_attend(frames, tiles, scalars, q, k, v):
    head_share = HEADS // tiles
    tile_tok, channels = q.shape
    frame_tok = tile_tok * tiles
    share = channels // tiles
    flops = 4 * (WIN + 1) * frame_tok * frame_tok * share
    smem = pl.BlockSpec(memory_space=pltpu.SMEM)
    vmem = pl.BlockSpec(memory_space=pltpu.VMEM)
    hbm = pl.BlockSpec(memory_space=pl.ANY)
    return pl.pallas_call(
        functools.partial(fused_kernel, frames, tiles),
        out_shape=jax.ShapeDtypeStruct(q.shape, jnp.bfloat16),
        in_specs=[smem] * len(scalars) + [hbm] * 3,
        out_specs=vmem,
        scratch_shapes=[
            pltpu.VMEM((2, frame_tok, share), jnp.bfloat16),
            pltpu.VMEM((frame_tok, share), jnp.bfloat16),
            pltpu.VMEM((WIN, 2, frame_tok, share), jnp.bfloat16),
            pltpu.VMEM((frame_tok, share), jnp.bfloat16),
            pltpu.VMEM((tile_tok, channels), jnp.bfloat16),
            pltpu.VMEM((frame_tok, frame_tok), jnp.int32),
            pltpu.VMEM((head_share, frame_tok, 1), jnp.float32),
            pltpu.VMEM((head_share, frame_tok, 1), jnp.float32),
            pltpu.VMEM((head_share, frame_tok, HD), jnp.float32),
            pltpu.SemaphoreType.DMA((4, tiles)),
            pltpu.SemaphoreType.DMA((4, tiles)),
            pltpu.SemaphoreType.DMA((4,)),
            pltpu.SemaphoreType.DMA((WIN,)),
            pltpu.SemaphoreType.DMA((WIN,)),
            pltpu.SemaphoreType.DMA((tiles,)),
            pltpu.SemaphoreType.DMA((tiles,)),
        ],
        compiler_params=pltpu.CompilerParams(
            collective_id=0, has_side_effects=True, vmem_limit_bytes=56 * 1024 * 1024
        ),
        cost_estimate=pl.CostEstimate(
            flops=flops,
            transcendentals=(WIN + 1) * head_share * frame_tok * frame_tok,
            bytes_accessed=(WIN + 6) * 2 * frame_tok * share * 2,
        ),
    )(*scalars, q, k, v)


def hand_over_kernel(src_ref, dst_ref, sem):
    move = pltpu.make_async_copy(src_ref, dst_ref, sem)
    move.start()
    move.wait()


def hand_over(block):
    anywhere = pl.BlockSpec(memory_space=pl.ANY)
    return pl.pallas_call(
        hand_over_kernel,
        out_shape=jax.ShapeDtypeStruct(block.shape, block.dtype),
        in_specs=[anywhere],
        out_specs=anywhere,
        scratch_shapes=[pltpu.SemaphoreType.DMA(())],
        cost_estimate=pl.CostEstimate(flops=0, transcendentals=0, bytes_accessed=2 * block.size * 2),
    )(block)


def shards(queries, keys, values, step_index, frame_index, window_mask, history_mask, step_gain):
    tile_count = lax.axis_size("tile")
    frames = lax.axis_size("frame")
    tile_id = lax.axis_index("tile")
    group_id = lax.axis_index("frame")
    channels = queries.shape[-1]
    head_share = HEADS // tile_count
    tile_tok = queries.shape[2]
    frame_tok = tile_tok * tile_count
    finished = fused_attend(
        frames, tile_count, (step_index, frame_index, window_mask.T, history_mask, step_gain),
        queries[0, 0], keys[0, 0], values[0, 0],
    )
    return hand_over(finished).reshape(1, 1, tile_tok, channels)


def solution(mesh):
    return jax.shard_map(
        shards,
        mesh=mesh,
        in_specs=(
            P("frame", "tile", None, None),
            P("frame", "tile", None, None),
            P("frame", "tile", None, None),
            P("frame"),
            P("frame"),
            P(),
            P("frame", None),
            P(),
        ),
        out_specs=P("frame", "tile", None, None),
        check_vma=False,
    )
```

```python
import functools
import math

import jax
import jax.numpy as jnp
from jax import lax
from jax.experimental import pallas as pl
from jax.experimental.pallas import tpu as pltpu
from jax.sharding import PartitionSpec as P

HEADS = 40
HD = 128
TH = 8
TW = 8
BLK = 4
WIN = 5
STEPS = 4
CHUNK = 256

NEG_BIG = -1e30
MESH_ID = pl.DeviceIdType.MESH


def block_place(positions, tile_count, tile_tok):
    tile_cols = min(tile_count, 4)
    tile_of = positions // tile_tok
    within = positions % tile_tok
    row = tile_of // tile_cols * TH + within // TW
    col = tile_of % tile_cols * TW + within % TW
    return row // BLK, col // BLK


def fused_kernel(frames, tiles, step_ref, fidx_ref, wm_ref, hm_ref, sg_ref, q_ref, k_ref, v_ref, out_ref,
                 own_kv, own_q, slots, fin, got_out, code_scr, m_scr, l_scr, acc_scr,
                 piece_send, piece_recv, local_sem, send_sem, recv_sem, hop_send, hop_recv):
    me = lax.axis_index("frame")
    tile = lax.axis_index("tile")
    right = lax.rem(me + 1, frames)
    left = lax.rem(me + frames - 1, frames)
    head_share = acc_scr.shape[0]
    frame_tok = own_q.shape[0]
    share = own_q.shape[1]
    tile_tok = q_ref.shape[0]
    scale = 1.0 / math.sqrt(HD)

    def head_bits(h):
        row = tile * head_share + h
        bits = 16
        for offset in range(9):
            bits = bits | jnp.where(wm_ref[offset, row] == 1, 1 << offset, 0)
        return bits

    def usable(distance):
        return (hm_ref[0, distance - 1] == 1) & (distance <= fidx_ref[0]) & (me >= distance)

    def head_gain(h):
        return sg_ref[step_ref[0], tile * head_share + h]

    barrier = pltpu.get_barrier_semaphore()
    for other in (left, right):
        pl.semaphore_signal(barrier, inc=1, device_id=(other, tile), device_id_type=MESH_ID)
    for offset in range(1, tiles):
        peer = lax.rem(tile + offset, tiles)
        pl.semaphore_signal(barrier, inc=1, device_id=(me, peer), device_id_type=MESH_ID)
    pl.semaphore_wait(barrier, 2 + tiles - 1)

    def channels_of(p):
        return pl.ds(pl.multiple_of(p * share, 128), share)

    def tokens_of(p):
        return pl.ds(pl.multiple_of(p * tile_tok, tile_tok), tile_tok)

    sources = [k_ref, v_ref, q_ref]
    targets = [lambda rows: own_kv.at[0, rows, :], lambda rows: own_kv.at[1, rows, :],
               lambda rows: own_q.at[rows, :]]

    def piece_out(which, offset):
        peer = lax.rem(tile + offset, tiles)
        return pltpu.make_async_remote_copy(
            src_ref=sources[which].at[:, channels_of(peer)],
            dst_ref=targets[which](tokens_of(tile)),
            send_sem=piece_send.at[which, offset],
            recv_sem=piece_recv.at[which, tile],
            device_id=(me, peer),
            device_id_type=MESH_ID,
        )

    def piece_in(which, offset):
        sender = lax.rem(tile + tiles - offset, tiles)
        return pltpu.make_async_remote_copy(
            src_ref=sources[which].at[:, channels_of(tile)],
            dst_ref=targets[which](tokens_of(sender)),
            send_sem=piece_send.at[which, offset],
            recv_sem=piece_recv.at[which, sender],
            device_id=(me, sender),
            device_id_type=MESH_ID,
        )

    locals_ = [
        pltpu.make_async_copy(
            sources[which].at[:, channels_of(tile)], targets[which](tokens_of(tile)),
            local_sem.at[which],
        )
        for which in range(3)
    ]
    far_first = [j for j in range(1, tiles) if j % 2] + [j for j in range(1, tiles) if j % 2 == 0]
    near_first = far_first[::-1]
    for which in range(3):
        locals_[which].start()
        for offset in far_first:
            piece_out(which, offset).start()

    for c in range(frame_tok // CHUNK):
        query_pos = c * CHUNK + lax.broadcasted_iota(jnp.int32, (CHUNK, frame_tok), 0)
        key_pos = lax.broadcasted_iota(jnp.int32, (CHUNK, frame_tok), 1)
        query_row, query_col = block_place(query_pos, tiles, tile_tok)
        key_row, key_col = block_place(key_pos, tiles, tile_tok)
        row_step = key_row - query_row
        across = key_col - query_col
        nearby = (row_step >= -1) & (row_step <= 1) & (across >= -1) & (across <= 1)
        code_scr[pl.ds(c * CHUNK, CHUNK), :] = jnp.where(nearby, (row_step + 1) * 3 + across + 1, 15)

    def first_hop(p):
        return pltpu.make_async_remote_copy(
            src_ref=own_kv.at[:, tokens_of(p), :],
            dst_ref=slots.at[0, :, tokens_of(p), :],
            send_sem=hop_send.at[p],
            recv_sem=hop_recv.at[p],
            device_id=(right, tile),
            device_id_type=MESH_ID,
        )

    for which in range(2):
        locals_[which].wait()

    @pl.when(me < frames - 1)
    def _():
        first_hop(tile).start()

    for offset in near_first:
        for which in range(2):
            piece_in(which, offset).wait_recv()

        @pl.when(me < frames - 1)
        def _():
            first_hop(lax.rem(tile + tiles - offset, tiles)).start()

    def copy_for(step):
        source = own_kv if step == 0 else slots.at[step - 1]
        return pltpu.make_async_remote_copy(
            src_ref=source,
            dst_ref=slots.at[step],
            send_sem=send_sem.at[step],
            recv_sem=recv_sem.at[step],
            device_id=(right, tile),
            device_id_type=MESH_ID,
        )

    copies = [None] + [copy_for(step) for step in range(1, WIN)]

    m_scr[...] = jnp.full(m_scr.shape, NEG_BIG, jnp.float32)
    l_scr[...] = jnp.zeros(l_scr.shape, jnp.float32)
    acc_scr[...] = jnp.zeros(acc_scr.shape, jnp.float32)

    locals_[2].wait()
    for offset in range(1, tiles):
        piece_in(2, offset).wait_recv()

    def attend(block, use):
        def head_body(h, carry):
            col = pl.multiple_of(h * HD, HD)
            key_h = block[0, :, pl.ds(col, HD)]
            value_h = block[1, :, pl.ds(col, HD)]
            for c in range(frame_tok // CHUNK):
                rows = pl.ds(c * CHUNK, CHUNK)
                query_h = own_q[rows, pl.ds(col, HD)]
                scores = lax.dot_general(
                    query_h, key_h, (((1,), (1,)), ((), ())),
                    preferred_element_type=jnp.float32,
                ) * scale
                if use is None:
                    code = code_scr[rows, :]
                    shifted = lax.shift_right_logical(jnp.broadcast_to(head_bits(h), code.shape), code)
                    scores = jnp.where((shifted & 1) == 1, scores, NEG_BIG)
                else:
                    scores = scores + jnp.where(use, 0.0, NEG_BIG)
                old_max = m_scr[h, rows, :]
                new_max = jnp.maximum(old_max, jnp.max(scores, axis=1, keepdims=True))
                weights = jnp.exp(scores - new_max)
                factor = jnp.exp(old_max - new_max)
                l_scr[h, rows, :] = l_scr[h, rows, :] * factor + jnp.sum(weights, axis=1, keepdims=True)
                acc_scr[h, rows, :] = acc_scr[h, rows, :] * factor + jnp.dot(
                    weights.astype(jnp.bfloat16), value_h, preferred_element_type=jnp.float32
                )
                m_scr[h, rows, :] = new_max
            return carry

        lax.fori_loop(0, head_share, head_body, 0)

    attend(own_kv, None)
    for step in range(1, WIN + 1):
        @pl.when(me >= step)
        def _():
            if step == 1:
                for p in range(tiles):
                    first_hop(p).wait_recv()
            else:
                copies[step - 1].wait_recv()
            if step < WIN:
                @pl.when(me < frames - 1)
                def _():
                    copies[step].start()
            attend(slots.at[step - 1], usable(step))

    def finish(h, carry):
        col = pl.multiple_of(h * HD, HD)
        fin[:, pl.ds(col, HD)] = (acc_scr[h] / l_scr[h] * head_gain(h)).astype(fin.dtype)
        return carry

    lax.fori_loop(0, head_share, finish, 0)

    def back_out(offset):
        peer = lax.rem(tile + offset, tiles)
        return pltpu.make_async_remote_copy(
            src_ref=fin.at[tokens_of(peer), :],
            dst_ref=got_out.at[:, channels_of(tile)],
            send_sem=piece_send.at[3, offset],
            recv_sem=piece_recv.at[3, tile],
            device_id=(me, peer),
            device_id_type=MESH_ID,
        )

    def back_in(offset):
        sender = lax.rem(tile + tiles - offset, tiles)
        return pltpu.make_async_remote_copy(
            src_ref=fin.at[tokens_of(tile), :],
            dst_ref=got_out.at[:, channels_of(sender)],
            send_sem=piece_send.at[3, offset],
            recv_sem=piece_recv.at[3, sender],
            device_id=(me, sender),
            device_id_type=MESH_ID,
        )

    home = pltpu.make_async_copy(fin.at[tokens_of(tile), :], got_out.at[:, channels_of(tile)],
                                 local_sem.at[3])
    home.start()
    for offset in range(1, tiles):
        back_out(offset).start()
    home.wait()
    for offset in range(1, tiles):
        back_in(offset).wait_recv()
    out_ref[...] = got_out[...]

    for which in range(3):
        for offset in range(1, tiles):
            piece_out(which, offset).wait_send()
    for offset in range(1, tiles):
        back_out(offset).wait_send()
    for step in range(1, WIN):
        @pl.when((me < frames - 1) & (me >= step))
        def _():
            copies[step].wait_send()

    @pl.when(me < frames - 1)
    def _():
        for p in range(tiles):
            first_hop(p).wait_send()


def fused_attend(frames, tiles, scalars, q, k, v):
    head_share = HEADS // tiles
    tile_tok, channels = q.shape
    frame_tok = tile_tok * tiles
    share = channels // tiles
    flops = 4 * (WIN + 1) * frame_tok * frame_tok * share
    smem = pl.BlockSpec(memory_space=pltpu.SMEM)
    vmem = pl.BlockSpec(memory_space=pltpu.VMEM)
    hbm = pl.BlockSpec(memory_space=pl.ANY)
    return pl.pallas_call(
        functools.partial(fused_kernel, frames, tiles),
        out_shape=jax.ShapeDtypeStruct(q.shape, jnp.bfloat16),
        in_specs=[smem] * len(scalars) + [hbm] * 3,
        out_specs=vmem,
        scratch_shapes=[
            pltpu.VMEM((2, frame_tok, share), jnp.bfloat16),
            pltpu.VMEM((frame_tok, share), jnp.bfloat16),
            pltpu.VMEM((WIN, 2, frame_tok, share), jnp.bfloat16),
            pltpu.VMEM((frame_tok, share), jnp.bfloat16),
            pltpu.VMEM((tile_tok, channels), jnp.bfloat16),
            pltpu.VMEM((frame_tok, frame_tok), jnp.int32),
            pltpu.VMEM((head_share, frame_tok, 1), jnp.float32),
            pltpu.VMEM((head_share, frame_tok, 1), jnp.float32),
            pltpu.VMEM((head_share, frame_tok, HD), jnp.float32),
            pltpu.SemaphoreType.DMA((4, tiles)),
            pltpu.SemaphoreType.DMA((4, tiles)),
            pltpu.SemaphoreType.DMA((4,)),
            pltpu.SemaphoreType.DMA((WIN,)),
            pltpu.SemaphoreType.DMA((WIN,)),
            pltpu.SemaphoreType.DMA((tiles,)),
            pltpu.SemaphoreType.DMA((tiles,)),
        ],
        compiler_params=pltpu.CompilerParams(
            collective_id=0, has_side_effects=True, vmem_limit_bytes=56 * 1024 * 1024
        ),
        cost_estimate=pl.CostEstimate(
            flops=flops,
            transcendentals=(WIN + 1) * head_share * frame_tok * frame_tok,
            bytes_accessed=(WIN + 6) * 2 * frame_tok * share * 2,
        ),
    )(*scalars, q, k, v)


def hand_over_kernel(src_ref, dst_ref):
    dst_ref[...] = src_ref[...]


def hand_over(block):
    vmem = pl.BlockSpec(memory_space=pltpu.VMEM)
    return pl.pallas_call(
        hand_over_kernel,
        out_shape=jax.ShapeDtypeStruct(block.shape, block.dtype),
        in_specs=[vmem],
        out_specs=vmem,
        cost_estimate=pl.CostEstimate(flops=0, transcendentals=0, bytes_accessed=2 * block.size * 2),
    )(block)


def shards(queries, keys, values, step_index, frame_index, window_mask, history_mask, step_gain):
    tile_count = lax.axis_size("tile")
    frames = lax.axis_size("frame")
    tile_id = lax.axis_index("tile")
    group_id = lax.axis_index("frame")
    channels = queries.shape[-1]
    head_share = HEADS // tile_count
    tile_tok = queries.shape[2]
    frame_tok = tile_tok * tile_count
    finished = fused_attend(
        frames, tile_count, (step_index, frame_index, window_mask.T, history_mask, step_gain),
        queries[0, 0], keys[0, 0], values[0, 0],
    )
    return hand_over(finished).reshape(1, 1, tile_tok, channels)


def solution(mesh):
    return jax.shard_map(
        shards,
        mesh=mesh,
        in_specs=(
            P("frame", "tile", None, None),
            P("frame", "tile", None, None),
            P("frame", "tile", None, None),
            P("frame"),
            P("frame"),
            P(),
            P("frame", None),
            P(),
        ),
        out_specs=P("frame", "tile", None, None),
        check_vma=False,
    )
```

```python
import functools
import math

import jax
import jax.numpy as jnp
from jax import lax
from jax.experimental import pallas as pl
from jax.experimental.pallas import tpu as pltpu
from jax.sharding import PartitionSpec as P

HEADS = 40
HD = 128
TH = 8
TW = 8
BLK = 4
WIN = 5
STEPS = 4
CHUNK = 128

NEG_BIG = -1e30
MESH_ID = pl.DeviceIdType.MESH


def block_place(positions, tile_count, tile_tok):
    tile_cols = min(tile_count, 4)
    tile_of = positions // tile_tok
    within = positions % tile_tok
    row = tile_of // tile_cols * TH + within // TW
    col = tile_of % tile_cols * TW + within % TW
    return row // BLK, col // BLK


def fused_kernel(frames, tiles, step_ref, fidx_ref, wm_ref, hm_ref, sg_ref, q_ref, k_ref, v_ref, out_ref,
                 own_kv, own_q, slots, fin, got_out, code_scr, m_scr, l_scr, acc_scr,
                 piece_send, piece_recv, local_sem, send_sem, recv_sem, hop_send, hop_recv):
    me = lax.axis_index("frame")
    tile = lax.axis_index("tile")
    right = lax.rem(me + 1, frames)
    left = lax.rem(me + frames - 1, frames)
    head_share = acc_scr.shape[0]
    frame_tok = own_q.shape[0]
    share = own_q.shape[1]
    tile_tok = q_ref.shape[0]
    scale = 1.0 / math.sqrt(HD)

    def head_bits(h):
        row = tile * head_share + h
        bits = 16
        for offset in range(9):
            bits = bits | jnp.where(wm_ref[offset, row] == 1, 1 << offset, 0)
        return bits

    def usable(distance):
        return (hm_ref[0, distance - 1] == 1) & (distance <= fidx_ref[0]) & (me >= distance)

    def head_gain(h):
        return sg_ref[step_ref[0], tile * head_share + h]

    barrier = pltpu.get_barrier_semaphore()
    for other in (left, right):
        pl.semaphore_signal(barrier, inc=1, device_id=(other, tile), device_id_type=MESH_ID)
    for offset in range(1, tiles):
        peer = lax.rem(tile + offset, tiles)
        pl.semaphore_signal(barrier, inc=1, device_id=(me, peer), device_id_type=MESH_ID)
    pl.semaphore_wait(barrier, 2 + tiles - 1)

    def channels_of(p):
        return pl.ds(pl.multiple_of(p * share, 128), share)

    def tokens_of(p):
        return pl.ds(pl.multiple_of(p * tile_tok, tile_tok), tile_tok)

    sources = [k_ref, v_ref, q_ref]
    targets = [lambda rows: own_kv.at[0, rows, :], lambda rows: own_kv.at[1, rows, :],
               lambda rows: own_q.at[rows, :]]

    def piece_out(which, offset):
        peer = lax.rem(tile + offset, tiles)
        return pltpu.make_async_remote_copy(
            src_ref=sources[which].at[:, channels_of(peer)],
            dst_ref=targets[which](tokens_of(tile)),
            send_sem=piece_send.at[which, offset],
            recv_sem=piece_recv.at[which, tile],
            device_id=(me, peer),
            device_id_type=MESH_ID,
        )

    def piece_in(which, offset):
        sender = lax.rem(tile + tiles - offset, tiles)
        return pltpu.make_async_remote_copy(
            src_ref=sources[which].at[:, channels_of(tile)],
            dst_ref=targets[which](tokens_of(sender)),
            send_sem=piece_send.at[which, offset],
            recv_sem=piece_recv.at[which, sender],
            device_id=(me, sender),
            device_id_type=MESH_ID,
        )

    locals_ = [
        pltpu.make_async_copy(
            sources[which].at[:, channels_of(tile)], targets[which](tokens_of(tile)),
            local_sem.at[which],
        )
        for which in range(3)
    ]
    far_first = [j for j in range(1, tiles) if j % 2] + [j for j in range(1, tiles) if j % 2 == 0]
    near_first = far_first[::-1]
    for which in range(3):
        locals_[which].start()
        for offset in far_first:
            piece_out(which, offset).start()

    for c in range(frame_tok // CHUNK):
        query_pos = c * CHUNK + lax.broadcasted_iota(jnp.int32, (CHUNK, frame_tok), 0)
        key_pos = lax.broadcasted_iota(jnp.int32, (CHUNK, frame_tok), 1)
        query_row, query_col = block_place(query_pos, tiles, tile_tok)
        key_row, key_col = block_place(key_pos, tiles, tile_tok)
        row_step = key_row - query_row
        across = key_col - query_col
        nearby = (row_step >= -1) & (row_step <= 1) & (across >= -1) & (across <= 1)
        code_scr[pl.ds(c * CHUNK, CHUNK), :] = jnp.where(nearby, (row_step + 1) * 3 + across + 1, 15)

    def first_hop(p):
        return pltpu.make_async_remote_copy(
            src_ref=own_kv.at[:, tokens_of(p), :],
            dst_ref=slots.at[0, :, tokens_of(p), :],
            send_sem=hop_send.at[p],
            recv_sem=hop_recv.at[p],
            device_id=(right, tile),
            device_id_type=MESH_ID,
        )

    for which in range(2):
        locals_[which].wait()

    @pl.when(me < frames - 1)
    def _():
        first_hop(tile).start()

    for offset in near_first:
        for which in range(2):
            piece_in(which, offset).wait_recv()

        @pl.when(me < frames - 1)
        def _():
            first_hop(lax.rem(tile + tiles - offset, tiles)).start()

    def copy_for(step):
        source = own_kv if step == 0 else slots.at[step - 1]
        return pltpu.make_async_remote_copy(
            src_ref=source,
            dst_ref=slots.at[step],
            send_sem=send_sem.at[step],
            recv_sem=recv_sem.at[step],
            device_id=(right, tile),
            device_id_type=MESH_ID,
        )

    copies = [None] + [copy_for(step) for step in range(1, WIN)]

    m_scr[...] = jnp.full(m_scr.shape, NEG_BIG, jnp.float32)
    l_scr[...] = jnp.zeros(l_scr.shape, jnp.float32)
    acc_scr[...] = jnp.zeros(acc_scr.shape, jnp.float32)

    locals_[2].wait()
    for offset in range(1, tiles):
        piece_in(2, offset).wait_recv()

    def attend(block, use):
        def head_body(h, carry):
            col = pl.multiple_of(h * HD, HD)
            key_h = block[0, :, pl.ds(col, HD)]
            value_h = block[1, :, pl.ds(col, HD)]
            for c in range(frame_tok // CHUNK):
                rows = pl.ds(c * CHUNK, CHUNK)
                query_h = own_q[rows, pl.ds(col, HD)]
                scores = lax.dot_general(
                    query_h, key_h, (((1,), (1,)), ((), ())),
                    preferred_element_type=jnp.float32,
                ) * scale
                if use is None:
                    code = code_scr[rows, :]
                    shifted = lax.shift_right_logical(jnp.broadcast_to(head_bits(h), code.shape), code)
                    scores = jnp.where((shifted & 1) == 1, scores, NEG_BIG)
                else:
                    scores = scores + jnp.where(use, 0.0, NEG_BIG)
                old_max = m_scr[h, rows, :]
                new_max = jnp.maximum(old_max, jnp.max(scores, axis=1, keepdims=True))
                weights = jnp.exp(scores - new_max)
                factor = jnp.exp(old_max - new_max)
                l_scr[h, rows, :] = l_scr[h, rows, :] * factor + jnp.sum(weights, axis=1, keepdims=True)
                acc_scr[h, rows, :] = acc_scr[h, rows, :] * factor + jnp.dot(
                    weights.astype(jnp.bfloat16), value_h, preferred_element_type=jnp.float32
                )
                m_scr[h, rows, :] = new_max
            return carry

        lax.fori_loop(0, head_share, head_body, 0)

    attend(own_kv, None)
    for step in range(1, WIN + 1):
        @pl.when(me >= step)
        def _():
            if step == 1:
                for p in range(tiles):
                    first_hop(p).wait_recv()
            else:
                copies[step - 1].wait_recv()
            if step < WIN:
                @pl.when(me < frames - 1)
                def _():
                    copies[step].start()
            attend(slots.at[step - 1], usable(step))

    def finish(h, carry):
        col = pl.multiple_of(h * HD, HD)
        fin[:, pl.ds(col, HD)] = (acc_scr[h] / l_scr[h] * head_gain(h)).astype(fin.dtype)
        return carry

    lax.fori_loop(0, head_share, finish, 0)

    def back_out(offset):
        peer = lax.rem(tile + offset, tiles)
        return pltpu.make_async_remote_copy(
            src_ref=fin.at[tokens_of(peer), :],
            dst_ref=out_ref.at[:, channels_of(tile)],
            send_sem=piece_send.at[3, offset],
            recv_sem=piece_recv.at[3, tile],
            device_id=(me, peer),
            device_id_type=MESH_ID,
        )

    def back_in(offset):
        sender = lax.rem(tile + tiles - offset, tiles)
        return pltpu.make_async_remote_copy(
            src_ref=fin.at[tokens_of(tile), :],
            dst_ref=out_ref.at[:, channels_of(sender)],
            send_sem=piece_send.at[3, offset],
            recv_sem=piece_recv.at[3, sender],
            device_id=(me, sender),
            device_id_type=MESH_ID,
        )

    home = pltpu.make_async_copy(fin.at[tokens_of(tile), :], out_ref.at[:, channels_of(tile)],
                                 local_sem.at[3])
    home.start()
    for offset in range(1, tiles):
        back_out(offset).start()
    home.wait()
    for offset in range(1, tiles):
        back_in(offset).wait_recv()

    for which in range(3):
        for offset in range(1, tiles):
            piece_out(which, offset).wait_send()
    for offset in range(1, tiles):
        back_out(offset).wait_send()
    for step in range(1, WIN):
        @pl.when((me < frames - 1) & (me >= step))
        def _():
            copies[step].wait_send()

    @pl.when(me < frames - 1)
    def _():
        for p in range(tiles):
            first_hop(p).wait_send()


def fused_attend(frames, tiles, scalars, q, k, v):
    head_share = HEADS // tiles
    tile_tok, channels = q.shape
    frame_tok = tile_tok * tiles
    share = channels // tiles
    flops = 4 * (WIN + 1) * frame_tok * frame_tok * share
    smem = pl.BlockSpec(memory_space=pltpu.SMEM)
    vmem = pl.BlockSpec(memory_space=pltpu.VMEM)
    hbm = pl.BlockSpec(memory_space=pl.ANY)
    return pl.pallas_call(
        functools.partial(fused_kernel, frames, tiles),
        out_shape=jax.ShapeDtypeStruct(q.shape, jnp.bfloat16),
        in_specs=[smem] * len(scalars) + [hbm] * 3,
        out_specs=vmem,
        scratch_shapes=[
            pltpu.VMEM((2, frame_tok, share), jnp.bfloat16),
            pltpu.VMEM((frame_tok, share), jnp.bfloat16),
            pltpu.VMEM((WIN, 2, frame_tok, share), jnp.bfloat16),
            pltpu.VMEM((frame_tok, share), jnp.bfloat16),
            pltpu.VMEM((tile_tok, channels), jnp.bfloat16),
            pltpu.VMEM((frame_tok, frame_tok), jnp.int32),
            pltpu.VMEM((head_share, frame_tok, 1), jnp.float32),
            pltpu.VMEM((head_share, frame_tok, 1), jnp.float32),
            pltpu.VMEM((head_share, frame_tok, HD), jnp.float32),
            pltpu.SemaphoreType.DMA((4, tiles)),
            pltpu.SemaphoreType.DMA((4, tiles)),
            pltpu.SemaphoreType.DMA((4,)),
            pltpu.SemaphoreType.DMA((WIN,)),
            pltpu.SemaphoreType.DMA((WIN,)),
            pltpu.SemaphoreType.DMA((tiles,)),
            pltpu.SemaphoreType.DMA((tiles,)),
        ],
        compiler_params=pltpu.CompilerParams(
            collective_id=0, has_side_effects=True, vmem_limit_bytes=56 * 1024 * 1024
        ),
        cost_estimate=pl.CostEstimate(
            flops=flops,
            transcendentals=(WIN + 1) * head_share * frame_tok * frame_tok,
            bytes_accessed=(WIN + 6) * 2 * frame_tok * share * 2,
        ),
    )(*scalars, q, k, v)


def hand_over_kernel(src_ref, dst_ref):
    dst_ref[...] = src_ref[...]


def hand_over(block):
    vmem = pl.BlockSpec(memory_space=pltpu.VMEM)
    return pl.pallas_call(
        hand_over_kernel,
        out_shape=jax.ShapeDtypeStruct(block.shape, block.dtype),
        in_specs=[vmem],
        out_specs=vmem,
        cost_estimate=pl.CostEstimate(flops=0, transcendentals=0, bytes_accessed=2 * block.size * 2),
    )(block)


def shards(queries, keys, values, step_index, frame_index, window_mask, history_mask, step_gain):
    tile_count = lax.axis_size("tile")
    frames = lax.axis_size("frame")
    tile_id = lax.axis_index("tile")
    group_id = lax.axis_index("frame")
    channels = queries.shape[-1]
    head_share = HEADS // tile_count
    tile_tok = queries.shape[2]
    frame_tok = tile_tok * tile_count
    finished = fused_attend(
        frames, tile_count, (step_index, frame_index, window_mask.T, history_mask, step_gain),
        queries[0, 0], keys[0, 0], values[0, 0],
    )
    return hand_over(finished).reshape(1, 1, tile_tok, channels)


def solution(mesh):
    return jax.shard_map(
        shards,
        mesh=mesh,
        in_specs=(
            P("frame", "tile", None, None),
            P("frame", "tile", None, None),
            P("frame", "tile", None, None),
            P("frame"),
            P("frame"),
            P(),
            P("frame", None),
            P(),
        ),
        out_specs=P("frame", "tile", None, None),
        check_vma=False,
    )
```

```python
import functools
import math

import jax
import jax.numpy as jnp
from jax import lax
from jax.experimental import pallas as pl
from jax.experimental.pallas import tpu as pltpu
from jax.sharding import PartitionSpec as P

HEADS = 40
HD = 128
TH = 8
TW = 8
BLK = 4
WIN = 5
STEPS = 4
CHUNK = 128

NEG_BIG = -1e30
MESH_ID = pl.DeviceIdType.MESH


def block_place(positions, tile_count, tile_tok):
    tile_cols = min(tile_count, 4)
    tile_of = positions // tile_tok
    within = positions % tile_tok
    row = tile_of // tile_cols * TH + within // TW
    col = tile_of % tile_cols * TW + within % TW
    return row // BLK, col // BLK


def fused_kernel(frames, tiles, step_ref, fidx_ref, wm_ref, hm_ref, sg_ref, q_ref, k_ref, v_ref, out_ref,
                 own_kv, own_q, slots, fin, got_out, code_scr, m_scr, l_scr, acc_scr,
                 piece_send, piece_recv, local_sem, send_sem, recv_sem, hop_send, hop_recv):
    me = lax.axis_index("frame")
    tile = lax.axis_index("tile")
    right = lax.rem(me + 1, frames)
    left = lax.rem(me + frames - 1, frames)
    head_share = acc_scr.shape[0]
    frame_tok = own_q.shape[0]
    share = own_q.shape[1]
    tile_tok = q_ref.shape[0]
    scale = 1.0 / math.sqrt(HD)

    def head_bits(h):
        row = tile * head_share + h
        bits = 16
        for offset in range(9):
            bits = bits | jnp.where(wm_ref[offset, row] == 1, 1 << offset, 0)
        return bits

    def usable(distance):
        return (hm_ref[0, distance - 1] == 1) & (distance <= fidx_ref[0]) & (me >= distance)

    def head_gain(h):
        return sg_ref[step_ref[0], tile * head_share + h]

    barrier = pltpu.get_barrier_semaphore()
    for other in (left, right):
        pl.semaphore_signal(barrier, inc=1, device_id=(other, tile), device_id_type=MESH_ID)
    for offset in range(1, tiles):
        peer = lax.rem(tile + offset, tiles)
        pl.semaphore_signal(barrier, inc=1, device_id=(me, peer), device_id_type=MESH_ID)
    pl.semaphore_wait(barrier, 2 + tiles - 1)

    def channels_of(p):
        return pl.ds(pl.multiple_of(p * share, 128), share)

    def tokens_of(p):
        return pl.ds(pl.multiple_of(p * tile_tok, tile_tok), tile_tok)

    sources = [k_ref, v_ref, q_ref]
    targets = [lambda rows: own_kv.at[0, rows, :], lambda rows: own_kv.at[1, rows, :],
               lambda rows: own_q.at[rows, :]]

    def piece_out(which, offset):
        peer = lax.rem(tile + offset, tiles)
        return pltpu.make_async_remote_copy(
            src_ref=sources[which].at[:, channels_of(peer)],
            dst_ref=targets[which](tokens_of(tile)),
            send_sem=piece_send.at[which, offset],
            recv_sem=piece_recv.at[which, tile],
            device_id=(me, peer),
            device_id_type=MESH_ID,
        )

    def piece_in(which, offset):
        sender = lax.rem(tile + tiles - offset, tiles)
        return pltpu.make_async_remote_copy(
            src_ref=sources[which].at[:, channels_of(tile)],
            dst_ref=targets[which](tokens_of(sender)),
            send_sem=piece_send.at[which, offset],
            recv_sem=piece_recv.at[which, sender],
            device_id=(me, sender),
            device_id_type=MESH_ID,
        )

    locals_ = [
        pltpu.make_async_copy(
            sources[which].at[:, channels_of(tile)], targets[which](tokens_of(tile)),
            local_sem.at[which],
        )
        for which in range(3)
    ]
    far_first = [j for j in range(1, tiles) if j % 2] + [j for j in range(1, tiles) if j % 2 == 0]
    near_first = far_first[::-1]
    for which in range(3):
        locals_[which].start()
        for offset in far_first:
            piece_out(which, offset).start()

    for c in range(frame_tok // CHUNK):
        query_pos = c * CHUNK + lax.broadcasted_iota(jnp.int32, (CHUNK, frame_tok), 0)
        key_pos = lax.broadcasted_iota(jnp.int32, (CHUNK, frame_tok), 1)
        query_row, query_col = block_place(query_pos, tiles, tile_tok)
        key_row, key_col = block_place(key_pos, tiles, tile_tok)
        row_step = key_row - query_row
        across = key_col - query_col
        nearby = (row_step >= -1) & (row_step <= 1) & (across >= -1) & (across <= 1)
        code_scr[pl.ds(c * CHUNK, CHUNK), :] = jnp.where(nearby, (row_step + 1) * 3 + across + 1, 15)

    def hop(step, p):
        source = own_kv if step == 0 else slots.at[step - 1]
        return pltpu.make_async_remote_copy(
            src_ref=source.at[:, tokens_of(p), :],
            dst_ref=slots.at[step, :, tokens_of(p), :],
            send_sem=hop_send.at[step, p],
            recv_sem=hop_recv.at[step, p],
            device_id=(right, tile),
            device_id_type=MESH_ID,
        )

    for which in range(2):
        locals_[which].wait()

    @pl.when(me < frames - 1)
    def _():
        hop(0, tile).start()

    for offset in near_first:
        for which in range(2):
            piece_in(which, offset).wait_recv()

        @pl.when(me < frames - 1)
        def _():
            hop(0, lax.rem(tile + tiles - offset, tiles)).start()

    def copy_for(step):
        source = own_kv if step == 0 else slots.at[step - 1]
        return pltpu.make_async_remote_copy(
            src_ref=source,
            dst_ref=slots.at[step],
            send_sem=send_sem.at[step],
            recv_sem=recv_sem.at[step],
            device_id=(right, tile),
            device_id_type=MESH_ID,
        )


    m_scr[...] = jnp.full(m_scr.shape, NEG_BIG, jnp.float32)
    l_scr[...] = jnp.zeros(l_scr.shape, jnp.float32)
    acc_scr[...] = jnp.zeros(acc_scr.shape, jnp.float32)

    locals_[2].wait()
    for offset in range(1, tiles):
        piece_in(2, offset).wait_recv()

    def attend(block, use):
        def head_body(h, carry):
            col = pl.multiple_of(h * HD, HD)
            key_h = block[0, :, pl.ds(col, HD)]
            value_h = block[1, :, pl.ds(col, HD)]
            for c in range(frame_tok // CHUNK):
                rows = pl.ds(c * CHUNK, CHUNK)
                query_h = own_q[rows, pl.ds(col, HD)]
                scores = lax.dot_general(
                    query_h, key_h, (((1,), (1,)), ((), ())),
                    preferred_element_type=jnp.float32,
                ) * scale
                if use is None:
                    code = code_scr[rows, :]
                    shifted = lax.shift_right_logical(jnp.broadcast_to(head_bits(h), code.shape), code)
                    scores = jnp.where((shifted & 1) == 1, scores, NEG_BIG)
                else:
                    scores = scores + jnp.where(use, 0.0, NEG_BIG)
                old_max = m_scr[h, rows, :]
                new_max = jnp.maximum(old_max, jnp.max(scores, axis=1, keepdims=True))
                weights = jnp.exp(scores - new_max)
                factor = jnp.exp(old_max - new_max)
                l_scr[h, rows, :] = l_scr[h, rows, :] * factor + jnp.sum(weights, axis=1, keepdims=True)
                acc_scr[h, rows, :] = acc_scr[h, rows, :] * factor + jnp.dot(
                    weights.astype(jnp.bfloat16), value_h, preferred_element_type=jnp.float32
                )
                m_scr[h, rows, :] = new_max
            return carry

        lax.fori_loop(0, head_share, head_body, 0)

    attend(own_kv, None)
    for step in range(1, WIN + 1):
        @pl.when(me >= step)
        def _():
            if step == 1:
                for p in range(tiles):
                    hop(0, p).wait_recv()
            else:
                for p in range(tiles):
                    hop(step - 1, p).wait_recv()
            if step < WIN:
                @pl.when(me < frames - 1)
                def _():
                    for p in range(tiles):
                        hop(step, p).start()
            attend(slots.at[step - 1], usable(step))

    def finish(h, carry):
        col = pl.multiple_of(h * HD, HD)
        fin[:, pl.ds(col, HD)] = (acc_scr[h] / l_scr[h] * head_gain(h)).astype(fin.dtype)
        return carry

    lax.fori_loop(0, head_share, finish, 0)

    def back_out(offset):
        peer = lax.rem(tile + offset, tiles)
        return pltpu.make_async_remote_copy(
            src_ref=fin.at[tokens_of(peer), :],
            dst_ref=got_out.at[:, channels_of(tile)],
            send_sem=piece_send.at[3, offset],
            recv_sem=piece_recv.at[3, tile],
            device_id=(me, peer),
            device_id_type=MESH_ID,
        )

    def back_in(offset):
        sender = lax.rem(tile + tiles - offset, tiles)
        return pltpu.make_async_remote_copy(
            src_ref=fin.at[tokens_of(tile), :],
            dst_ref=got_out.at[:, channels_of(sender)],
            send_sem=piece_send.at[3, offset],
            recv_sem=piece_recv.at[3, sender],
            device_id=(me, sender),
            device_id_type=MESH_ID,
        )

    home = pltpu.make_async_copy(fin.at[tokens_of(tile), :], got_out.at[:, channels_of(tile)],
                                 local_sem.at[3])
    home.start()
    for offset in range(1, tiles):
        back_out(offset).start()
    home.wait()
    for offset in range(1, tiles):
        back_in(offset).wait_recv()
    out_ref[...] = got_out[...]

    for which in range(3):
        for offset in range(1, tiles):
            piece_out(which, offset).wait_send()
    for offset in range(1, tiles):
        back_out(offset).wait_send()
    for step in range(1, WIN):
        @pl.when((me < frames - 1) & (me >= step))
        def _():
            for p in range(tiles):
                hop(step, p).wait_send()

    @pl.when(me < frames - 1)
    def _():
        for p in range(tiles):
            hop(0, p).wait_send()


def fused_attend(frames, tiles, scalars, q, k, v):
    head_share = HEADS // tiles
    tile_tok, channels = q.shape
    frame_tok = tile_tok * tiles
    share = channels // tiles
    flops = 4 * (WIN + 1) * frame_tok * frame_tok * share
    smem = pl.BlockSpec(memory_space=pltpu.SMEM)
    vmem = pl.BlockSpec(memory_space=pltpu.VMEM)
    hbm = pl.BlockSpec(memory_space=pl.ANY)
    return pl.pallas_call(
        functools.partial(fused_kernel, frames, tiles),
        out_shape=jax.ShapeDtypeStruct(q.shape, jnp.bfloat16),
        in_specs=[smem] * len(scalars) + [hbm] * 3,
        out_specs=vmem,
        scratch_shapes=[
            pltpu.VMEM((2, frame_tok, share), jnp.bfloat16),
            pltpu.VMEM((frame_tok, share), jnp.bfloat16),
            pltpu.VMEM((WIN, 2, frame_tok, share), jnp.bfloat16),
            pltpu.VMEM((frame_tok, share), jnp.bfloat16),
            pltpu.VMEM((tile_tok, channels), jnp.bfloat16),
            pltpu.VMEM((frame_tok, frame_tok), jnp.int32),
            pltpu.VMEM((head_share, frame_tok, 1), jnp.float32),
            pltpu.VMEM((head_share, frame_tok, 1), jnp.float32),
            pltpu.VMEM((head_share, frame_tok, HD), jnp.float32),
            pltpu.SemaphoreType.DMA((4, tiles)),
            pltpu.SemaphoreType.DMA((4, tiles)),
            pltpu.SemaphoreType.DMA((4,)),
            pltpu.SemaphoreType.DMA((WIN,)),
            pltpu.SemaphoreType.DMA((WIN,)),
            pltpu.SemaphoreType.DMA((WIN, tiles)),
            pltpu.SemaphoreType.DMA((WIN, tiles)),
        ],
        compiler_params=pltpu.CompilerParams(
            collective_id=0, has_side_effects=True, vmem_limit_bytes=56 * 1024 * 1024
        ),
        cost_estimate=pl.CostEstimate(
            flops=flops,
            transcendentals=(WIN + 1) * head_share * frame_tok * frame_tok,
            bytes_accessed=(WIN + 6) * 2 * frame_tok * share * 2,
        ),
    )(*scalars, q, k, v)


def hand_over_kernel(src_ref, dst_ref):
    dst_ref[...] = src_ref[...]


def hand_over(block):
    vmem = pl.BlockSpec(memory_space=pltpu.VMEM)
    return pl.pallas_call(
        hand_over_kernel,
        out_shape=jax.ShapeDtypeStruct(block.shape, block.dtype),
        in_specs=[vmem],
        out_specs=vmem,
        cost_estimate=pl.CostEstimate(flops=0, transcendentals=0, bytes_accessed=2 * block.size * 2),
    )(block)


def shards(queries, keys, values, step_index, frame_index, window_mask, history_mask, step_gain):
    tile_count = lax.axis_size("tile")
    frames = lax.axis_size("frame")
    tile_id = lax.axis_index("tile")
    group_id = lax.axis_index("frame")
    channels = queries.shape[-1]
    head_share = HEADS // tile_count
    tile_tok = queries.shape[2]
    frame_tok = tile_tok * tile_count
    finished = fused_attend(
        frames, tile_count, (step_index, frame_index, window_mask.T, history_mask, step_gain),
        queries[0, 0], keys[0, 0], values[0, 0],
    )
    return hand_over(finished).reshape(1, 1, tile_tok, channels)


def solution(mesh):
    return jax.shard_map(
        shards,
        mesh=mesh,
        in_specs=(
            P("frame", "tile", None, None),
            P("frame", "tile", None, None),
            P("frame", "tile", None, None),
            P("frame"),
            P("frame"),
            P(),
            P("frame", None),
            P(),
        ),
        out_specs=P("frame", "tile", None, None),
        check_vma=False,
    )
```
